32 devices in a mesh: dp: 8 (over z, y), seq: 4 (over x, core).
Axes of the slice: x: 2, y: 2, z: 4, core: 2. Of those that a mesh axis runs over, the one named last changes fastest.
Arguments:
- tokens_long: bfloat16 [8, 1024, 384], P('dp', 'seq'), may hold values from -6 to 6
- tokens_short: bfloat16 [64, 512, 384], P(('dp', 'seq')), may hold values from -6 to 6
- upstream_long: bfloat16 [8, 1024, 384], P('dp', 'seq'), may hold values from -6 to 6
- upstream_short: bfloat16 [64, 512, 384], P(('dp', 'seq')), may hold values from -6 to 6
- interval_table: float32 [3, 384], replicated, may hold values from -5 to 5
- labels_long: int32 [8], replicated, may hold values from 0 to 2
- labels_short: int32 [64], replicated, may hold values from 0 to 2
- lengths_long: int32 [8], replicated, may hold values from 512 to 1024
- lengths_short: int32 [64], replicated, may hold values from 128 to 512
- tile_slot: int32 [162], replicated, may hold values from 0 to 167, as said below
- master_slots: float32 [168, 128, 128], P('dp')
- basis_left: float32 [168, 128, 128], P('dp')
- basis_right: float32 [168, 128, 128], P('dp')
- first_moment: float32 [168, 128, 128], P('dp')
- second_moment: float32 [168, 128, 128], P('dp')
Outputs:
- output_long: bfloat16 [8, 1024, 384], P('dp', 'seq')
- output_short: bfloat16 [64, 512, 384], P(('dp', 'seq'))
- grad_long: float32 [8, 1024, 384], P('dp', 'seq')
- grad_short: float32 [64, 512, 384], P(('dp', 'seq'))
- grad_slots: float32 [168, 128, 128], P('dp')
- first_new: float32 [168, 128, 128], P('dp')
- second_new: float32 [168, 128, 128], P('dp')
- weight_new: float32 [168, 128, 128], P('dp')
The draws below stay inside these ranges and needn't reach their ends.
Inputs may be any that keep to these rules, and one draw needn't show every extreme that they name: `tile_slot`: all 162 entries are different slots.
All inputs are finite; a program needn't handle non-finite values.
Results may differ from the reference program's by a relative error of at most 0.0095.
The reference program's roundings to bfloat16 on the way count: a program that leaves them out, or rounds other values in their place, can miss the bound.
Values may be sent and summed in bfloat16 or wider, within the bound.
No kernel may reach another device: no remote copies, remote signals or barrier semaphores. Data moves between devices by JAX's collectives and lax.ppermute only.
A program may use at most 192 MiB of HBM per device.

```python
import math
import jax
import jax.numpy as jnp
from jax import lax

D = 384
HEADS = 6
HD = 64
FF = 1536
TILE = 128
SHORT = 512
SHORT_SEQS = 2
STEP = 10
LONG = 1024
NSEQ_SHORT = 64
NTILES = 162
SLOTS = 21
N_DP = 8
N_SEQ = 4


def slot_order(key):
    slot_total = N_DP * SLOTS
    shuffled = jax.random.permutation(jax.random.fold_in(key, 11), slot_total).astype(jnp.int32)
    leading = shuffled[0]
    shuffled = jnp.where(shuffled == slot_total - 1, leading, shuffled)
    shuffled = shuffled.at[0].set(slot_total - 1)
    return shuffled[:NTILES]


def slot_kinds(key):
    slot_total = N_DP * SLOTS
    placed = slot_order(key)
    matches = placed[None, :] == jnp.arange(slot_total, dtype=jnp.int32)[:, None]
    tile_index = jnp.sum(jnp.where(matches, jnp.arange(NTILES, dtype=jnp.int32)[None, :] + 1, 0), axis=1) - 1
    bounds = jnp.array([6 * D * D, 9 * D * D, 10 * D * D, 10 * D * D + D * FF], dtype=jnp.int32) // (TILE * TILE)
    kinds = jnp.sum((tile_index[:, None] >= bounds[None, :]).astype(jnp.int32), axis=1)
    return jnp.where(tile_index < 0, 5, kinds)


def grad_scale(key):
    valid_rows = N_DP * LONG * 0.75 + N_DP * N_SEQ * SHORT_SEQS * SHORT * 0.625
    table = jnp.array([1.0, 1.0, 0.06, 0.6, 0.5, 1.0], dtype=jnp.float32) * math.sqrt(valid_rows)
    return table[slot_kinds(key)]


def orthogonal_basis(key):
    slot_total = N_DP * SLOTS

    def shuffle(subkey):
        return jax.random.permutation(subkey, TILE)
    row_order = jax.vmap(shuffle)(jax.random.split(jax.random.fold_in(key, 1), slot_total))
    column_order = jax.vmap(shuffle)(jax.random.split(jax.random.fold_in(key, 2), slot_total))
    signs = (jax.random.randint(jax.random.fold_in(key, 3), (slot_total, TILE), 0, 2) * 2 - 1).astype(jnp.float32)
    frequency = row_order[:, :, None].astype(jnp.float32)
    position = column_order[:, None, :].astype(jnp.float32)
    angle_arg = math.pi * (2.0 * position + 1.0) * frequency / (2.0 * TILE)
    norm_factor = jnp.where(frequency == 0.0, math.sqrt(1.0 / TILE), math.sqrt(2.0 / TILE))
    return signs[:, :, None] * norm_factor * jnp.cos(angle_arg)


def draw_tile_slot(key, part):
    return slot_order(key)


def draw_master_slots(key, part):
    table = jnp.array([D ** (-0.5), D ** (-0.5), 1.5, D ** (-0.5), FF ** (-0.5), D ** (-0.5)], dtype=jnp.float32)
    spread = table[slot_kinds(key)]
    noise_key = jax.random.fold_in(key, 21)
    noise = jax.random.normal(noise_key, (N_DP * SLOTS, TILE, TILE), jnp.float32)
    return noise * spread[:, None, None]


def draw_basis_left(key, part):
    return orthogonal_basis(jax.random.fold_in(key, 31))


def draw_basis_right(key, part):
    return orthogonal_basis(jax.random.fold_in(key, 41))


def draw_first_moment(key, part):
    noise = jax.random.normal(jax.random.fold_in(key, 51), (N_DP * SLOTS, TILE, TILE), jnp.float32)
    return noise * grad_scale(key)[:, None, None] * (0.1 / 0.9)


def draw_second_moment(key, part):
    factor = jnp.exp(jax.random.uniform(jax.random.fold_in(key, 61), (N_DP * SLOTS, TILE, TILE), jnp.float32, 0.0, math.log(4.0)))
    scale_now = grad_scale(key)
    return factor * (scale_now * scale_now)[:, None, None] * (0.05 / 0.95)


def draw_lengths_long(key, part):
    drawn = jax.random.randint(jax.random.fold_in(key, 71), (N_DP,), LONG // 2, LONG + 1).astype(jnp.int32)
    return drawn.at[0].set(LONG).at[1].set(LONG // 2)


def draw_lengths_short(key, part):
    drawn = jax.random.randint(jax.random.fold_in(key, 81), (NSEQ_SHORT,), SHORT // 4, SHORT + 1).astype(jnp.int32)
    return drawn.at[0].set(SHORT).at[1].set(SHORT // 4)


def with_ends(entries, stream_key, smallest, largest):
    extent = entries.shape
    place = [jax.random.randint(jax.random.fold_in(stream_key, axis), (), 0, extent[axis]) for axis in range(len(extent))]
    entries = entries.at[tuple(place)].set(smallest)
    longest = extent.index(max(extent))
    place[longest] = (place[longest] + 1) % extent[longest]
    return entries.at[tuple(place)].set(largest)


def levels(own_key, dims, pieces, low, largest):
    factor_of, own = 1.0, jax.random.fold_in(own_key, 6)
    for dim, parts in pieces:
        heights = jnp.exp(jax.random.uniform(jax.random.fold_in(own, dim), (parts,), jnp.float32, low / len(pieces), largest / len(pieces)))
        factor_of = factor_of * jnp.repeat(heights, dims[dim] // parts).reshape([-1 if axis == dim else 1 for axis in range(len(dims))])
    return factor_of


def centred(stream_key, shape, deviation, reach, pieces=(), kind=jnp.bfloat16):
    values = deviation * jax.random.normal(stream_key, shape, jnp.float32)
    if pieces:
        values = values * levels(stream_key, shape, pieces, -0.22, 0.18)
    return jnp.clip(values, -reach, reach).astype(kind)


def setup_inputs(seed: int = 0) -> dict:
    arg_keys = jax.random.split(jax.random.key(seed), 16)
    return {
        "tokens_long": centred(arg_keys[0], (N_DP, LONG, D), 1.0, 6.0, ((0, 8), (1, 4))),
        "tokens_short": centred(arg_keys[1], (NSEQ_SHORT, SHORT, D), 1.0, 6.0, ((0, 32),)),
        "upstream_long": centred(arg_keys[2], (N_DP, LONG, D), 1.0, 6.0, ((0, 8), (1, 4))),
        "upstream_short": centred(arg_keys[3], (NSEQ_SHORT, SHORT, D), 1.0, 6.0, ((0, 32),)),
        "interval_table": centred(arg_keys[4], (3, D), 1.0, 5.0, (), jnp.float32),
        "labels_long": with_ends(jax.random.randint(arg_keys[5], (N_DP,), 0, 3), jax.random.fold_in(arg_keys[5], 1), 0, 2).astype(jnp.int32),
        "labels_short": with_ends(jax.random.randint(arg_keys[6], (NSEQ_SHORT,), 0, 3), jax.random.fold_in(arg_keys[6], 1), 0, 2).astype(jnp.int32),
        "lengths_long": draw_lengths_long(jax.random.fold_in(arg_keys[15], 71), 0),
        "lengths_short": draw_lengths_short(jax.random.fold_in(arg_keys[15], 71), 0),
        "tile_slot": draw_tile_slot(jax.random.fold_in(arg_keys[15], 71), 0),
        "master_slots": draw_master_slots(jax.random.fold_in(arg_keys[15], 71), 0),
        "basis_left": draw_basis_left(jax.random.fold_in(arg_keys[15], 71), 0),
        "basis_right": draw_basis_right(jax.random.fold_in(arg_keys[15], 71), 0),
        "first_moment": draw_first_moment(jax.random.fold_in(arg_keys[15], 71), 0),
        "second_moment": draw_second_moment(jax.random.fold_in(arg_keys[15], 71), 0),
    }


@jax.custom_vjp
def low(v):
    return lax.optimization_barrier(v.astype(jnp.bfloat16)).astype(jnp.float32)

@jax.custom_vjp
def low_back(v):
    return v

def low_keep(v):
    return (low(v), None)

def low_pass(kept, grad):
    return (grad,)

def back_keep(v):
    return (v, None)

def back_low(kept, grad):
    return (low(grad),)
low.defvjp(low_keep, low_pass)
low_back.defvjp(back_keep, back_low)
highest = lax.Precision.HIGHEST
beta_first = 0.9
beta_second = 0.95
adam_eps = 1e-08
base_rate = 0.3
decay_rate = 0.01
norm_eps = 1e-06
masked_score = -1e+30

def layer_norm(inputs):
    centered = inputs - lax.optimization_barrier(jnp.mean(inputs, axis=-1, keepdims=True))
    variance = lax.optimization_barrier(jnp.mean(centered * centered, axis=-1, keepdims=True))
    return centered * lax.rsqrt(variance + norm_eps)

def matrix_shapes():
    return [(D, 6 * D), (D, 3 * D), (D, D), (D, FF), (FF, D)]

def assemble(blocks, row_total, column_total):
    return blocks.reshape(row_total // TILE, column_total // TILE, TILE, TILE).transpose(0, 2, 1, 3).reshape(row_total, column_total)

def cut_tiles(matrix):
    row_total, column_total = matrix.shape
    return matrix.reshape(row_total // TILE, TILE, column_total // TILE, TILE).transpose(0, 2, 1, 3).reshape(-1, TILE, TILE)

def attend(queries, keys_all, values_all, length):
    total_len = queries.shape[0]
    block_rows = min(512, total_len)
    key_ok = jnp.arange(total_len) < length

    def one_block(query_block):
        scores = jnp.einsum('qhd,khd->hqk', query_block, keys_all, precision=highest) * HD ** (-0.5)
        scores = jnp.where(key_ok[None, None, :], scores, masked_score)
        scores = low_back(scores)
        row_max = lax.optimization_barrier(jnp.max(scores, axis=-1, keepdims=True))
        exponent = jnp.exp(scores - row_max)
        weights_row = exponent / lax.optimization_barrier(jnp.sum(exponent, axis=-1, keepdims=True))
        return jnp.einsum('hqk,khd->qhd', low(weights_row), values_all, precision=highest)
    blocks = queries.reshape(total_len // block_rows, block_rows, HEADS, HD)
    return lax.map(jax.checkpoint(one_block), blocks).reshape(total_len, HEADS, HD)

def block_forward(rest, inputs, modulation, length):
    w_qkv, w_out, w_up, w_down = rest
    shift_one, scale_one, gate_one, shift_two, scale_two, gate_two = jnp.split(modulation, 6)
    normed = layer_norm(inputs)
    attn_in = low(normed * (1.0 + scale_one) + shift_one)
    project = low_back(low(jnp.dot(attn_in, w_qkv, precision=highest)))
    row_total = inputs.shape[0]
    queries = project[:, :D].reshape(row_total, HEADS, HD)
    keys_here = project[:, D:2 * D].reshape(row_total, HEADS, HD)
    values_here = project[:, 2 * D:].reshape(row_total, HEADS, HD)
    mixed = attend(queries, keys_here, values_here, length).reshape(row_total, D)
    mixed = low_back(low(mixed))
    branch = low_back(jnp.dot(mixed, w_out, precision=highest))
    middle = inputs + gate_one * branch
    mlp_in = low(layer_norm(middle) * (1.0 + scale_two) + shift_two)
    hidden = low_back(jnp.dot(mlp_in, w_up, precision=highest))
    active = low(jax.nn.gelu(hidden, approximate=True))
    result = low_back(jnp.dot(active, w_down, precision=highest))
    return middle + gate_two * result

def reference(tokens_long, tokens_short, upstream_long, upstream_short, interval_table, labels_long, labels_short, lengths_long, lengths_short, tile_slot, master_slots, basis_left, basis_right, first_moment, second_moment):
    tile_list = master_slots[tile_slot].astype(jnp.bfloat16).astype(jnp.float32)
    matrices = []
    offset = 0
    for row_total, column_total in matrix_shapes():
        number = row_total * column_total // (TILE * TILE)
        matrices.append(assemble(tile_list[offset:offset + number], row_total, column_total))
        offset = offset + number
    label_all = jnp.concatenate([labels_long, labels_short])
    counts = lax.optimization_barrier(jnp.sum((label_all[:, None] == jnp.arange(3, dtype=jnp.int32)[None, :]).astype(jnp.float32), axis=0))
    seq_total = float(label_all.shape[0])
    weight_long = seq_total / (3.0 * counts[labels_long])
    weight_short = seq_total / (3.0 * counts[labels_short])
    long_ok = (jnp.arange(LONG, dtype=jnp.int32)[None, :] < lengths_long[:, None]).astype(jnp.float32)
    short_ok = (jnp.arange(SHORT, dtype=jnp.int32)[None, :] < lengths_short[:, None]).astype(jnp.float32)
    cot_long = upstream_long.astype(jnp.float32) * weight_long[:, None, None] * long_ok[:, :, None]
    cot_short = upstream_short.astype(jnp.float32) * weight_short[:, None, None] * short_ok[:, :, None]
    cond_act = jax.nn.silu(interval_table).astype(jnp.bfloat16).astype(jnp.float32)
    group_size = 8

    def forward(mats, inputs_long, inputs_short):
        w_ada = mats[0]
        rest = mats[1:]
        mod_long = jnp.dot(cond_act[labels_long], w_ada, precision=highest)
        mod_short = jnp.dot(cond_act[labels_short], w_ada, precision=highest)

        def long_one(packed):
            return block_forward(rest, packed[0], packed[1], packed[2])

        def single_short(inputs, modulation, length):
            return block_forward(rest, inputs, modulation, length)

        def short_group(packed):
            return jax.vmap(single_short)(packed[0], packed[1], packed[2])
        out_long = lax.map(jax.checkpoint(long_one), (inputs_long, mod_long, lengths_long))
        shaped = (inputs_short.reshape(-1, group_size, SHORT, D), mod_short.reshape(-1, group_size, 6 * D), lengths_short.reshape(-1, group_size))
        out_short = lax.map(jax.checkpoint(short_group), shaped).reshape(NSEQ_SHORT, SHORT, D)
        return (out_long, out_short)
    outputs, back_fn = jax.vjp(forward, matrices, tokens_long.astype(jnp.float32), tokens_short.astype(jnp.float32))
    gradients, grad_long, grad_short = back_fn((cot_long, cot_short))
    tile_grad = jnp.concatenate([cut_tiles(item) for item in gradients], axis=0)
    grad_slots = jnp.zeros(master_slots.shape, jnp.float32).at[tile_slot].set(tile_grad)
    rotated = jnp.einsum('sji,sjk->sik', basis_left, grad_slots, precision=highest)
    rotated = jnp.einsum('sik,skl->sil', rotated, basis_right, precision=highest)
    first_new = beta_first * first_moment + (1.0 - beta_first) * rotated
    second_new = beta_second * second_moment + (1.0 - beta_second) * rotated * rotated
    normed_step = first_new / (1.0 - beta_first ** STEP) / (jnp.sqrt(second_new / (1.0 - beta_second ** STEP)) + adam_eps)
    rotated_back = jnp.einsum('sij,sjk->sik', basis_left, normed_step, precision=highest)
    rotated_back = jnp.einsum('sik,slk->sil', rotated_back, basis_right, precision=highest)
    spread = jnp.sqrt(lax.optimization_barrier(jnp.mean(master_slots * master_slots, axis=(1, 2), keepdims=True)) + 1e-06)
    weight_new = master_slots - base_rate * spread * (rotated_back + decay_rate * master_slots)
    return (outputs[0].astype(jnp.bfloat16), outputs[1].astype(jnp.bfloat16), grad_long, grad_short, grad_slots, first_new, second_new, weight_new)
```

```python
import functools

import jax
import jax.numpy as jnp
from jax import lax
from jax.experimental import pallas as pl
from jax.experimental.pallas import tpu as pltpu
from jax.sharding import PartitionSpec as P

D = 384
HEADS = 6
HD = 64
FF = 1536
STEP = 10
TILE = 128
PAIRS = HEADS // 2
SHAPES = ((D, 6 * D), (D, 3 * D), (D, D), (D, FF), (FF, D))

F32 = jnp.float32
BF16 = jnp.bfloat16
beta_first = 0.9
beta_second = 0.95
adam_eps = 1e-08
base_rate = 0.3
decay_rate = 0.01
norm_eps = 1e-06
masked_score = -1e30
score_scale = HD ** (-0.5)
FF_BLOCK = 256
Q_BLOCK = 128


VMEM = pl.BlockSpec(memory_space=pltpu.VMEM)
SMEM = pl.BlockSpec(memory_space=pltpu.SMEM)
ANY = pl.BlockSpec(memory_space=pl.ANY)


def dot_nn(a, b):
    return lax.dot_general(a, b, (((1,), (0,)), ((), ())), preferred_element_type=F32)


def dot_nt(a, b):
    return lax.dot_general(a, b, (((1,), (1,)), ((), ())), preferred_element_type=F32)


def dot_tn(a, b):
    return lax.dot_general(a, b, (((0,), (0,)), ((), ())), preferred_element_type=F32)


def norm_parts(v):
    centered = v - jnp.mean(v, axis=-1, keepdims=True)
    scale = lax.rsqrt(jnp.mean(centered * centered, axis=-1, keepdims=True) + norm_eps)
    return centered * scale, scale


def norm_back(dy, hat, scale):
    return scale * (
        dy
        - jnp.mean(dy, axis=-1, keepdims=True)
        - hat * jnp.mean(dy * hat, axis=-1, keepdims=True)
    )


def col_sum(v):
    return jnp.sum(v, axis=0, keepdims=True)


def head_mask(j):
    lane = lax.broadcasted_iota(jnp.int32, (1, 2 * HD), 1)
    return (lane >= j * HD) & (lane < (j + 1) * HD)


def only_head(v, j):
    return jnp.where(head_mask(j), v, jnp.zeros_like(v))


def gelu_both(u):
    k0 = 0.7978845608028654
    sq = u * u
    t = jnp.tanh(u * (k0 + (k0 * 0.044715) * sq))
    half = 0.5 * (1.0 + t)
    slope = half + (0.5 * u) * (1.0 - t * t) * (k0 + (3.0 * k0 * 0.044715) * sq)
    return u * half, slope


def unpack_kernel(nq, sizes, idx, cond, *refs):
    srcs = refs[: len(sizes)]
    w_qkv, w_out, w_up, w_down, mod, buf, w_ada, sems = refs[len(sizes) :]
    part = TILE // nq
    copies = []
    base = 0
    for i, size in enumerate(sizes):
        cp = pltpu.make_async_copy(srcs[i], buf.at[pl.ds(base, size)], sems.at[i])
        cp.start()
        copies.append(cp)
        base += size
    for cp in copies:
        cp.wait()
    first = 0
    for (rows, cols), dst in zip(SHAPES, (w_ada, w_qkv, w_out, w_up, w_down)):
        nr, nc = rows // TILE, cols // TILE

        @pl.loop(0, nr)
        def _(r, first=first, nc=nc, dst=dst):
            for c in range(nc):
                for q in range(nq):
                    at = idx[(first + r * nc + c) * nq + q]
                    row = pl.multiple_of(r * TILE + q * part, part)
                    dst[pl.ds(row, part), c * TILE : (c + 1) * TILE] = buf[at]

        first += nr * nc
    mod[...] = dot_nn(cond[...], w_ada[...])


def unpack(nq, srcs, idx, cond):
    sizes = tuple(s.shape[0] for s in srcs)
    part = TILE // nq
    return pl.pallas_call(
        functools.partial(unpack_kernel, nq, sizes),
        name="unpack",
        out_shape=tuple(jax.ShapeDtypeStruct(s, BF16) for s in SHAPES[1:])
        + (jax.ShapeDtypeStruct((8, 6 * D), F32),),
        in_specs=[SMEM, VMEM] + [ANY] * len(srcs),
        out_specs=(VMEM,) * 5,
        scratch_shapes=[
            pltpu.VMEM((sum(sizes), part, TILE), BF16),
            pltpu.VMEM(SHAPES[0], BF16),
            pltpu.SemaphoreType.DMA((len(sizes),)),
        ],
        cost_estimate=pl.CostEstimate(flops=10**7, bytes_accessed=10**7, transcendentals=0),
    )(idx, cond, *srcs)


def mods_of(mod):
    return [mod[i : i + 1, :] for i in range(6)]


def project(x, mod, w_qkv):
    hat, scale = norm_parts(x)
    a = (hat * (1.0 + mod[1]) + mod[0]).astype(BF16)
    return hat, scale, a, dot_nn(a, w_qkv[...]).astype(BF16)


def mlp_both(x, o_low, g, mod, w_out, w_up, w_down, dw_out, dw_up, dw_down, mo, dm):
    att = dot_nn(o_low, w_out[...])
    x1 = x + mod[2] * att
    hat, scale = norm_parts(x1)
    m = (hat * (1.0 + mod[4]) + mod[3]).astype(BF16)
    d_mo = (mod[5] * g).astype(BF16)
    mo[...] = jnp.zeros_like(mo)
    dm[...] = jnp.zeros_like(dm)

    @pl.loop(0, FF // FF_BLOCK)
    def _(b):
        cols = pl.ds(pl.multiple_of(b * FF_BLOCK, FF_BLOCK), FF_BLOCK)
        u = dot_nn(m, w_up[:, cols])
        d_r = dot_nt(d_mo, w_down[cols, :])
        act, slope = gelu_both(u)
        r = act.astype(BF16)
        du = (d_r * slope).astype(BF16)
        mo[...] += dot_nn(r, w_down[cols, :])
        dm[...] += dot_nt(du, w_up[:, cols])
        dw_up[:, cols] = dot_tn(m, du)
        dw_down[cols, :] = dot_tn(r, d_mo)

    mo_v = mo[...]
    out = (x1 + mod[5] * mo_v).astype(BF16)
    d_gate2 = col_sum(mo_v * g)
    dm_v = dm[...]
    d_shift2 = col_sum(dm_v)
    d_scale2 = col_sum(dm_v * hat)
    dx1 = g + norm_back(dm_v * (1.0 + mod[4]), hat, scale)
    d_att = (mod[2] * dx1).astype(BF16)
    d_gate1 = col_sum(att * dx1)
    dw_out[...] = dot_tn(o_low, d_att)
    d_o = dot_nt(d_att, w_out[...]).astype(BF16)
    return out, dx1, d_o, (d_gate1, d_shift2, d_scale2, d_gate2)


def project_back(dqkv, dx1, hat, scale, a, mod, w_qkv, dw_qkv):
    dw_qkv[...] = dot_tn(a, dqkv)
    d_a = dot_nt(dqkv, w_qkv[...])
    d_shift = col_sum(d_a)
    d_scale = col_sum(d_a * hat)
    return dx1 + norm_back(d_a * (1.0 + mod[1]), hat, scale), d_shift, d_scale


def cotangent(up, weight, rows_ok):
    return jnp.where(rows_ok, up.astype(F32) * weight, 0.0)


def short_kernel(
    which, length, weight, x_ref, up_ref, mod_ref, w_qkv, w_out, w_up, w_down, *refs
):
    if which:
        refs = refs[2:]
    (
        out_ref, grad_ref, dw_qkv, dw_out, dw_up, dw_down, dmod_ref,
        qkv, probs, o_f, mo, dm, d_o, dqkv, ds_s, x1_s,
    ) = refs
    n = x_ref.shape[1]
    mod = mods_of(mod_ref)
    x = x_ref[0].astype(F32)
    hat, scale, a, qkv_v = project(x, mod, w_qkv)
    qkv[...] = qkv_v
    key = lax.broadcasted_iota(jnp.int32, (1, n), 1)
    bias = jnp.where(key < length[0], 0.0, masked_score)

    @pl.loop(0, PAIRS)
    def _(hp):
        q_cols = pl.ds(pl.multiple_of(hp * 128, 128), 128)
        k2 = qkv[:, pl.ds(pl.multiple_of(D + hp * 128, 128), 128)]
        v2 = qkv[:, pl.ds(pl.multiple_of(2 * D + hp * 128, 128), 128)]

        @pl.loop(0, n // Q_BLOCK)
        def _(qb):
            rows = pl.ds(pl.multiple_of(qb * Q_BLOCK, Q_BLOCK), Q_BLOCK)
            q2 = qkv[rows, q_cols]
            o2 = None
            for j in range(2):
                s = dot_nt(q2, only_head(k2, j)) * score_scale + bias
                e = jnp.exp(s - jnp.max(s, axis=-1, keepdims=True))
                p = e / jnp.sum(e, axis=-1, keepdims=True)
                probs[hp * 2 + j, rows, :] = p
                part = dot_nn(p.astype(BF16), only_head(v2, j))
                o2 = part if o2 is None else o2 + part
            o_f[rows, q_cols] = o2

    row = lax.broadcasted_iota(jnp.int32, (n, 1), 0)
    g = cotangent(up_ref[0], weight[0], row < length[0])
    o_low = o_f[...].astype(BF16)
    out, dx1, d_o_v, dm_parts = mlp_both(
        x, o_low, g, mod, w_out, w_up, w_down, dw_out, dw_up, dw_down, mo, dm
    )
    out_ref[0] = out
    x1_s[...] = dx1
    d_o[...] = d_o_v

    @pl.loop(0, PAIRS)
    def _(hp):
        q_cols = pl.ds(pl.multiple_of(hp * 128, 128), 128)
        k_cols = pl.ds(pl.multiple_of(D + hp * 128, 128), 128)
        v_cols = pl.ds(pl.multiple_of(2 * D + hp * 128, 128), 128)
        k2 = qkv[:, k_cols]
        v2 = qkv[:, v_cols]

        @pl.loop(0, n // Q_BLOCK)
        def _(qb):
            rows = pl.ds(pl.multiple_of(qb * Q_BLOCK, Q_BLOCK), Q_BLOCK)
            do2 = d_o[rows, q_cols]
            prod = do2.astype(F32) * o_f[rows, q_cols]
            dq2 = None
            for j in range(2):
                dp = dot_nt(do2, only_head(v2, j))
                delta = jnp.sum(only_head(prod, j), axis=-1, keepdims=True)
                ds = (probs[hp * 2 + j, rows, :] * (dp - delta)).astype(BF16)
                ds_s[j, rows, :] = ds
                part = dot_nn(ds, only_head(k2, j))
                dq2 = part if dq2 is None else dq2 + part
            dqkv[rows, q_cols] = (dq2 * score_scale).astype(BF16)

        q2 = qkv[:, q_cols]
        do2 = d_o[:, q_cols]
        dk2 = jnp.where(head_mask(0), dot_tn(ds_s[0], q2), dot_tn(ds_s[1], q2))
        dqkv[:, k_cols] = (dk2 * score_scale).astype(BF16)
        p0 = probs[hp * 2].astype(BF16)
        p1 = probs[hp * 2 + 1].astype(BF16)
        dv2 = jnp.where(head_mask(0), dot_tn(p0, do2), dot_tn(p1, do2))
        dqkv[:, v_cols] = dv2.astype(BF16)

    x = x_ref[0].astype(F32)
    hat, scale = norm_parts(x)
    a = (hat * (1.0 + mod[1]) + mod[0]).astype(BF16)
    grad, d_shift1, d_scale1 = project_back(
        dqkv[...], x1_s[...], hat, scale, a, mod, w_qkv, dw_qkv
    )
    grad_ref[0] = grad
    pad = jnp.zeros((2, D), F32)
    dmod_ref[...] = jnp.concatenate([d_shift1, d_scale1, *dm_parts, pad], axis=0)


GRAD_SHAPES = tuple(jax.ShapeDtypeStruct(s, F32) for s in SHAPES[1:])


def short_call(which, length, weight, tokens, upstream, mod, weights, prev):
    count, n, _ = tokens.shape
    block = pl.BlockSpec((1, n, D), lambda i: (which, 0, 0))

    def whole(shape):
        return pl.BlockSpec(shape, lambda i: (0,) * len(shape))

    in_specs = [SMEM, SMEM, block, block, whole((8, D))] + [whole(w.shape) for w in weights]
    args = [length, weight, tokens, upstream, mod, *weights]
    aliases = {}
    if prev is not None:
        in_specs += [ANY, ANY]
        aliases = {len(args): 0, len(args) + 1: 1}
        args += list(prev)
    return pl.pallas_call(
        functools.partial(short_kernel, 0 if prev is None else 1),
        name="short" + str(which),
        grid=(1,),
        out_shape=(
            jax.ShapeDtypeStruct(tokens.shape, BF16),
            jax.ShapeDtypeStruct(tokens.shape, F32),
            *GRAD_SHAPES,
            jax.ShapeDtypeStruct((8, D), F32),
        ),
        in_specs=in_specs,
        out_specs=(block, block, *[whole(s.shape) for s in GRAD_SHAPES], whole((8, D))),
        scratch_shapes=[
            pltpu.VMEM((n, 3 * D), BF16),
            pltpu.VMEM((HEADS, n, n), F32),
            pltpu.VMEM((n, D), F32),
            pltpu.VMEM((n, D), F32),
            pltpu.VMEM((n, D), F32),
            pltpu.VMEM((n, D), BF16),
            pltpu.VMEM((n, 3 * D), BF16),
            pltpu.VMEM((2, n, n), BF16),
            pltpu.VMEM((n, D), F32),
        ],
        input_output_aliases=aliases,
        cost_estimate=pl.CostEstimate(
            flops=8 * 10**9, bytes_accessed=2 * 10**7, transcendentals=2 * 10**6
        ),
    )(*args)


def long_in_kernel(x_ref, mod_ref, w_qkv, q_ref, kv_ref):
    _, _, _, qkv = project(x_ref[0].astype(F32), mods_of(mod_ref), w_qkv)
    q_ref[...] = qkv[:, :D]
    kv_ref[...] = qkv[:, D:]


def long_in(tokens, mod, w_qkv):
    n = tokens.shape[1]
    return pl.pallas_call(
        long_in_kernel,
        name="long_in",
        out_shape=(
            jax.ShapeDtypeStruct((n, D), BF16),
            jax.ShapeDtypeStruct((n, 2 * D), BF16),
        ),
        in_specs=[VMEM] * 3,
        out_specs=(VMEM,) * 2,
        cost_estimate=pl.CostEstimate(flops=10**8, bytes_accessed=10**6, transcendentals=0),
    )(tokens, mod, w_qkv)


def long_mid_kernel(
    start_len, weight, x_ref, up_ref, mod_ref, q_ref, kv, bias_ref,
    w_out, w_up, w_down,
    out_ref, dx1_ref, do_ref, stat_ref, row_ref, dw_out, dw_up, dw_down, dmod_ref,
    o_f, mo, dm,
):
    n = x_ref.shape[1]
    mod = mods_of(mod_ref)
    bias = bias_ref[...]
    lane = lax.broadcasted_iota(jnp.int32, (1, 128), 1)
    stat_ref[...] = jnp.zeros_like(stat_ref)

    @pl.loop(0, PAIRS)
    def _(hp):
        q_cols = pl.ds(pl.multiple_of(hp * 128, 128), 128)
        k2 = kv[:, q_cols]
        v2 = kv[:, pl.ds(pl.multiple_of(D + hp * 128, 128), 128)]

        @pl.loop(0, n // Q_BLOCK)
        def _(qb):
            rows = pl.ds(pl.multiple_of(qb * Q_BLOCK, Q_BLOCK), Q_BLOCK)
            q2 = q_ref[rows, q_cols]
            o2 = None
            for j in range(2):
                s = dot_nt(q2, only_head(k2, j)) * score_scale + bias
                top = jnp.max(s, axis=-1, keepdims=True)
                e = jnp.exp(s - top)
                total = jnp.sum(e, axis=-1, keepdims=True)
                part = dot_nn(e.astype(BF16), only_head(v2, j)) / total
                o2 = part if o2 is None else o2 + part
                lse = top + jnp.log(total)
                stat_ref[rows, :] += jnp.where(lane == hp * 2 + j, lse, 0.0)
            o_f[rows, q_cols] = o2

    row = start_len[0] + lax.broadcasted_iota(jnp.int32, (n, 1), 0)
    g = cotangent(up_ref[0], weight[0], row < start_len[1])
    o_low = o_f[...].astype(BF16)
    out, dx1, d_o, dm_parts = mlp_both(
        x_ref[0].astype(F32), o_low, g, mod, w_out, w_up, w_down,
        dw_out, dw_up, dw_down, mo, dm,
    )
    out_ref[0] = out
    dx1_ref[...] = dx1
    do_ref[...] = d_o
    stat = stat_ref[...]
    for hp in range(PAIRS):
        cols = slice(hp * 128, (hp + 1) * 128)
        prod = d_o[:, cols].astype(F32) * o_f[:, cols]
        for j in range(2):
            delta = jnp.sum(only_head(prod, j), axis=-1, keepdims=True)
            stat = stat + jnp.where(lane == 8 + hp * 2 + j, delta, 0.0)
    stat_ref[...] = stat
    row_ref[...] = stat.T[:16, :]
    pad = jnp.zeros((4, D), F32)
    dmod_ref[...] = jnp.concatenate([*dm_parts, pad], axis=0)


def long_mid(start_len, weight, tokens, upstream, mod, q, kv, bias, w_out, w_up, w_down):
    n = tokens.shape[1]
    return pl.pallas_call(
        long_mid_kernel,
        name="long_mid",
        out_shape=(
            jax.ShapeDtypeStruct(tokens.shape, BF16),
            jax.ShapeDtypeStruct((n, D), F32),
            jax.ShapeDtypeStruct((n, D), BF16),
            jax.ShapeDtypeStruct((n, 128), F32),
            jax.ShapeDtypeStruct((16, n), F32),
            *GRAD_SHAPES[1:],
            jax.ShapeDtypeStruct((8, D), F32),
        ),
        in_specs=[SMEM, SMEM] + [VMEM] * 9,
        out_specs=(VMEM,) * 9,
        scratch_shapes=[pltpu.VMEM((n, D), F32)] * 3,
        cost_estimate=pl.CostEstimate(
            flops=4 * 10**9, bytes_accessed=2 * 10**7, transcendentals=2 * 10**6
        ),
    )(start_len, weight, tokens, upstream, mod, q, kv, bias, w_out, w_up, w_down)


def long_back_kernel(
    start_len, x_ref, mod_ref, q_ref, kv_own, kv, bias_ref, do_ref, stat_ref,
    q_all, do_all, rows_all, dx1_ref, w_qkv,
    grad_ref, dw_qkv, dmod_ref, dqkv, dk_s, dv_s,
):
    n = x_ref.shape[1]
    total = kv.shape[0]
    mod = mods_of(mod_ref)
    bias = bias_ref[...]
    lane = lax.broadcasted_iota(jnp.int32, (1, 128), 1)

    @pl.loop(0, PAIRS)
    def _(hp):
        q_cols = pl.ds(pl.multiple_of(hp * 128, 128), 128)
        k_cols = pl.ds(pl.multiple_of(D + hp * 128, 128), 128)
        v_cols = pl.ds(pl.multiple_of(2 * D + hp * 128, 128), 128)
        k2 = kv[:, q_cols]
        v2 = kv[:, k_cols]

        @pl.loop(0, n // Q_BLOCK)
        def _(qb):
            rows = pl.ds(pl.multiple_of(qb * Q_BLOCK, Q_BLOCK), Q_BLOCK)
            q2 = q_ref[rows, q_cols]
            do2 = do_ref[rows, q_cols]
            stat = stat_ref[rows, :]
            dq2 = None
            for j in range(2):
                kz = only_head(k2, j)
                h = hp * 2 + j
                lse = jnp.sum(jnp.where(lane == h, stat, 0.0), axis=-1, keepdims=True)
                delta = jnp.sum(jnp.where(lane == 8 + h, stat, 0.0), axis=-1, keepdims=True)
                p = jnp.exp(dot_nt(q2, kz) * score_scale + bias - lse)
                dp = dot_nt(do2, only_head(v2, j))
                ds = (p * (dp - delta)).astype(BF16)
                part = dot_nn(ds, kz)
                dq2 = part if dq2 is None else dq2 + part
            dqkv[rows, q_cols] = (dq2 * score_scale).astype(BF16)

        k_own = kv_own[:, q_cols]
        v_own = kv_own[:, k_cols]
        dk_s[...] = jnp.zeros_like(dk_s)
        dv_s[...] = jnp.zeros_like(dv_s)

        @pl.loop(0, total // n)
        def _(qc):
            rows = pl.ds(pl.multiple_of(qc * n, n), n)
            q2 = q_all[rows, q_cols]
            do2 = do_all[rows, q_cols]
            for j in range(2):
                h = hp * 2 + j
                lse = rows_all[qc, pl.ds(h, 1), :]
                delta = rows_all[qc, pl.ds(8 + h, 1), :]
                p = jnp.exp(dot_nt(only_head(k_own, j), q2) * score_scale - lse)
                dp = dot_nt(only_head(v_own, j), do2)
                ds = (p * (dp - delta)).astype(BF16)
                dv_s[j] += dot_nn(p.astype(BF16), do2)
                dk_s[j] += dot_nn(ds, q2)

        row = start_len[0] + lax.broadcasted_iota(jnp.int32, (n, 1), 0)
        ok = row < start_len[1]
        dk2 = jnp.where(head_mask(0), dk_s[0], dk_s[1])
        dv2 = jnp.where(head_mask(0), dv_s[0], dv_s[1])
        dqkv[:, k_cols] = jnp.where(ok, dk2 * score_scale, 0.0).astype(BF16)
        dqkv[:, v_cols] = jnp.where(ok, dv2, 0.0).astype(BF16)

    hat, scale = norm_parts(x_ref[0].astype(F32))
    a = (hat * (1.0 + mod[1]) + mod[0]).astype(BF16)
    grad, d_shift1, d_scale1 = project_back(
        dqkv[...], dx1_ref[...], hat, scale, a, mod, w_qkv, dw_qkv
    )
    grad_ref[0] = grad
    pad = jnp.zeros((6, D), F32)
    dmod_ref[...] = jnp.concatenate([d_shift1, d_scale1, pad], axis=0)


def long_back(start_len, tokens, *args):
    n = tokens.shape[1]
    return pl.pallas_call(
        long_back_kernel,
        name="long_back",
        out_shape=(
            jax.ShapeDtypeStruct(tokens.shape, F32),
            GRAD_SHAPES[0],
            jax.ShapeDtypeStruct((8, D), F32),
        ),
        in_specs=[SMEM] + [VMEM] * 13,
        out_specs=(VMEM,) * 3,
        scratch_shapes=[
            pltpu.VMEM((n, 3 * D), BF16),
            pltpu.VMEM((2, n, 128), F32),
            pltpu.VMEM((2, n, 128), F32),
        ],
        cost_estimate=pl.CostEstimate(
            flops=4 * 10**9, bytes_accessed=10**7, transcendentals=4 * 10**6
        ),
    )(start_len, tokens, *args)


def pack_kernel(nq, sizes, idx, labels, cond_t, dmod_mid, dmod_back, dmod_s0, dmod_s1, *refs):
    grads = refs[:12]
    outs = refs[12 : 12 + len(sizes)]
    buf, sems = refs[12 + len(sizes) :]
    part = TILE // nq
    buf[...] = jnp.zeros_like(buf)
    d_long = jnp.concatenate([dmod_back[:2, :], dmod_mid[:4, :]], axis=0)
    per_seq = (d_long, dmod_s0[:6, :], dmod_s1[:6, :])
    by_label = []
    for v in range(3):
        acc = None
        for s in range(3):
            term = jnp.where(labels[s] == v, per_seq[s], 0.0)
            acc = term if acc is None else acc + term
        by_label.append(acc)
    first = 0
    for r in range(D // TILE):
        col = [cond_t[r * TILE : (r + 1) * TILE, v : v + 1] for v in range(3)]
        for c in range(6 * D // TILE):
            i, off = divmod(c, D // TILE)
            lanes = slice(off * TILE, (off + 1) * TILE)
            tile = None
            for v in range(3):
                term = col[v] * by_label[v][i : i + 1, lanes]
                tile = term if tile is None else tile + term
            tile = tile.astype(BF16)
            t = first + r * (6 * D // TILE) + c
            for q in range(nq):
                buf[idx[t * nq + q]] = tile[q * part : (q + 1) * part]
    first += SHAPES[0][0] * SHAPES[0][1] // TILE**2
    at = 0
    for (rows, cols), many in zip(SHAPES[1:], (3, 3, 3, 3)):
        nr, nc = rows // TILE, cols // TILE
        terms = grads[at : at + many]
        at += many

        @pl.loop(0, nr)
        def _(r, first=first, nc=nc, terms=terms):
            for c in range(nc):
                for q in range(nq):
                    row = pl.multiple_of(r * TILE + q * part, part)
                    lanes = slice(c * TILE, (c + 1) * TILE)
                    v = terms[0][pl.ds(row, part), lanes]
                    for other in terms[1:]:
                        v = v + other[pl.ds(row, part), lanes]
                    buf[idx[(first + r * nc + c) * nq + q]] = v.astype(BF16)

        first += nr * nc
    copies = []
    base = 0
    for i, size in enumerate(sizes):
        cp = pltpu.make_async_copy(buf.at[pl.ds(base, size)], outs[i], sems.at[i])
        cp.start()
        copies.append(cp)
        base += size
    for cp in copies:
        cp.wait()


def pack(nq, sizes, idx, labels, cond_t, dmods, grads):
    part = TILE // nq
    return pl.pallas_call(
        functools.partial(pack_kernel, nq, sizes),
        name="pack",
        out_shape=tuple(jax.ShapeDtypeStruct((s, part, TILE), BF16) for s in sizes),
        in_specs=[SMEM, SMEM] + [VMEM] * 17,
        out_specs=(ANY,) * len(sizes),
        scratch_shapes=[
            pltpu.VMEM((sum(sizes), part, TILE), BF16),
            pltpu.SemaphoreType.DMA((len(sizes),)),
        ],
        cost_estimate=pl.CostEstimate(flops=10**7, bytes_accessed=3 * 10**7, transcendentals=0),
    )(idx, labels, cond_t, *dmods, *grads)


def halves(v):
    high = v.astype(BF16)
    return high, (v - high.astype(F32)).astype(BF16)


def dot3(dot, a, b):
    return dot(a[0], b[0]) + (dot(a[0], b[1]) + dot(a[1], b[0]))


def soap_kernel(nq, order, g_ref, left, right, first, second, master, gs, fn, sn, wn):
    part = TILE // nq
    for i in range(master.shape[0]):
        g = jnp.concatenate([g_ref[order[q], i] for q in range(nq)], axis=0)
        gs[i] = g
        lo = halves(left[i])
        ro = halves(right[i])
        rot = dot3(dot_nn, halves(dot3(dot_tn, lo, halves(g))), ro)
        f = beta_first * first[i] + (1.0 - beta_first) * rot
        s = beta_second * second[i] + (1.0 - beta_second) * rot * rot
        fn[i] = f
        sn[i] = s
        step = (
            f
            / (1.0 - beta_first**STEP)
            / (jnp.sqrt(s / (1.0 - beta_second**STEP)) + adam_eps)
        )
        back = dot3(dot_nt, halves(dot3(dot_nn, lo, halves(step))), ro)
        w = master[i]
        mean = jnp.mean(jnp.mean(w * w, axis=1, keepdims=True), axis=0, keepdims=True)
        spread = jnp.sqrt(mean + 1e-06)
        wn[i] = w - base_rate * spread * (back + decay_rate * w)


def soap(nq, order, g, left, right, first, second, master):
    slots = master.shape[0]
    block = max(k for k in range(1, 12) if slots % k == 0)
    part = TILE // nq
    spec = pl.BlockSpec((block, TILE, TILE), lambda i: (i, 0, 0))
    g_spec = pl.BlockSpec((nq, block, part, TILE), lambda i: (0, i, 0, 0))
    shape = jax.ShapeDtypeStruct(master.shape, F32)
    return pl.pallas_call(
        functools.partial(soap_kernel, nq),
        name="soap",
        grid=(slots // block,),
        out_shape=(shape,) * 4,
        in_specs=[SMEM, g_spec] + [spec] * 5,
        out_specs=(spec,) * 4,
        cost_estimate=pl.CostEstimate(flops=10**9, bytes_accessed=10**7, transcendentals=10**6),
    )(order, g, left, right, first, second, master)


class Grid:
    def __init__(self, n_dp, n_seq):
        self.direct = n_dp == 8 and n_seq == 4
        self.n = {"z": n_dp // 2, "y": 2, "x": n_seq // 2, "c": 2}
        self.n_dp = n_dp
        self.n_seq = n_seq
        self.nq = n_seq if self.direct else 1

    def here(self):
        dp = lax.axis_index("dp")
        seq = lax.axis_index("seq")
        return {"z": dp // 2, "y": dp % 2, "x": seq // 2, "c": seq % 2}

    def shift(self, v, name):
        n = self.n[name]
        if name in "zy":
            total, axis = self.n_dp, "dp"
        else:
            total, axis = self.n_seq, "seq"
        pairs = []
        for i in range(total):
            hi, lo = divmod(i, 2)
            if name in "zx":
                hi = (hi + 1) % n
            else:
                lo = (lo + 1) % n
            pairs.append((i, hi * 2 + lo))
        return lax.ppermute(v, axis, pairs)

    def ring(self, v, name):
        out = [v]
        for _ in range(self.n[name] - 1):
            out.append(self.shift(out[-1], name))
        return out

    def over_seq(self, v):
        if not self.direct:
            return lax.all_gather(v, "seq", axis=0, tiled=True)
        v = jnp.concatenate(self.ring(v, "x"), axis=0)
        return jnp.concatenate(self.ring(v, "c"), axis=0)

    def seq_blocks(self):
        if not self.direct:
            return jnp.arange(self.n_seq, dtype=jnp.int32)
        at = self.here()
        return jnp.stack(
            [((at["x"] - rx) % 2) * 2 + (at["c"] - rc) % 2 for rc in range(2) for rx in range(2)]
        )

    def table(self, tile_slot, slots, sign):
        if not self.direct:
            return tile_slot, (self.n_dp * slots,)
        at = self.here()
        ka = (slots + 1) // 2
        kb = slots - ka
        owner = tile_slot // slots
        local = tile_slot % slots
        nz, ny, nx = self.n["z"], self.n["y"], self.n["x"]
        rz = (sign * (at["z"] - owner // 2)) % nz
        ry = (at["y"] - owner % 2) % ny
        parts = []
        for q in range(self.nq):
            rx = (at["x"] - q // 2) % nx
            rc = (at["c"] - q % 2) % 2
            in_a = (((rc * nx + rx) * ny + ry) * nz + rz) * ka + local
            in_b = (((rc * ny + ry) * nx + rx) * nz + rz) * kb + (local - ka)
            parts.append(jnp.where(local < ka, in_a, 2 * nx * ny * nz * ka + in_b))
        sizes = (nx * ny * nz * ka,) * 2 + (nx * ny * nz * kb,) * 2
        return jnp.stack(parts, axis=1).reshape(-1), sizes

    def gather_slots(self, low):
        if not self.direct:
            return [lax.all_gather(low, "dp", axis=0, tiled=True)]
        part = TILE // self.nq
        own = lax.dynamic_slice_in_dim(low, lax.axis_index("seq") * part, part, 1)
        ka = (low.shape[0] + 1) // 2
        out = []
        for piece, order in ((own[:ka], "zyx"), (own[ka:], "zxy")):
            for name in order:
                piece = jnp.concatenate(self.ring(piece, name), axis=0)
            out += self.ring(piece, "c")
        return out

    def stage(self, v, name):
        n = self.n[name]
        k = v.shape[0] // n
        acc = v[(n - 1) * k :]
        for r in range(n - 2, -1, -1):
            acc = self.shift(acc, name).astype(F32) + v[r * k : (r + 1) * k].astype(F32)
            if r:
                acc = acc.astype(BF16)
        return acc

    def reduce_slots(self, parts):
        if not self.direct:
            total = lax.psum_scatter(
                parts[0].astype(F32), "dp", scatter_dimension=0, tiled=True
            )
            return lax.psum(total, "seq")[None]
        out = []
        for own, send, order in ((parts[0], parts[1], "xyz"), (parts[2], parts[3], "yxz")):
            acc = self.shift(send, "c").astype(F32) + own.astype(F32)
            for name in order:
                acc = self.stage(acc.astype(BF16), name)
            out.append(acc)
        mine = jnp.concatenate(out, axis=0)[None]
        both = jnp.concatenate(self.ring(mine, "x"), axis=0)
        return jnp.concatenate(self.ring(both, "c"), axis=0)

    def part_order(self):
        if not self.direct:
            return jnp.zeros((1,), jnp.int32)
        at = self.here()
        return jnp.stack(
            [((at["c"] - q % 2) % 2) * 2 + (at["x"] - q // 2) % 2 for q in range(self.nq)]
        )


def local(
    tokens_long,
    tokens_short,
    upstream_long,
    upstream_short,
    interval_table,
    labels_long,
    labels_short,
    lengths_long,
    lengths_short,
    tile_slot,
    master_slots,
    basis_left,
    basis_right,
    first_moment,
    second_moment,
):
    grid = Grid(lax.axis_size("dp"), lax.axis_size("seq"))
    slots = master_slots.shape[0]
    dp_index = lax.axis_index("dp")
    seq_index = lax.axis_index("seq")
    rows = tokens_long.shape[1]
    short_count = tokens_short.shape[0]

    srcs = grid.gather_slots(master_slots.astype(BF16))
    idx_in, _ = grid.table(tile_slot, slots, 1)
    idx_out, sizes = grid.table(tile_slot, slots, -1)

    label_all = jnp.concatenate([labels_long, labels_short])
    kinds = jnp.arange(3, dtype=jnp.int32)
    counts = jnp.sum((label_all[:, None] == kinds[None, :]).astype(F32), axis=0)
    first_short = (dp_index * grid.n_seq + seq_index) * short_count
    own = jnp.concatenate(
        [
            lax.dynamic_slice_in_dim(labels_long, dp_index, 1),
            lax.dynamic_slice_in_dim(labels_short, first_short, short_count),
        ]
    )
    own_length = lax.dynamic_slice_in_dim(lengths_long, dp_index, 1)
    short_lengths = lax.dynamic_slice_in_dim(lengths_short, first_short, short_count)
    one_hot = (own[:, None] == kinds[None, :]).astype(F32)
    seq_weight = float(label_all.shape[0]) / (3.0 * jnp.sum(one_hot * counts[None, :], axis=1))

    cond = jax.nn.silu(interval_table).astype(BF16)
    cond_pad = jnp.concatenate([cond, jnp.zeros((5, D), BF16)], axis=0)
    *weights, mod_table = unpack(grid.nq, srcs, idx_in, cond_pad)
    w_qkv, w_out, w_up, w_down = weights
    mod_seq = jnp.sum(one_hot[:, :, None] * mod_table[None, :3, :], axis=1)
    mod_seq = jnp.pad(mod_seq.reshape(1 + short_count, 6, D), ((0, 0), (0, 2), (0, 0)))

    long_start = seq_index * rows
    start_len = jnp.concatenate([long_start[None].astype(jnp.int32), own_length])
    blocks = grid.seq_blocks()
    pos = (blocks[:, None] * rows + jnp.arange(rows, dtype=jnp.int32)[None, :]).reshape(1, -1)
    bias = jnp.where(pos < own_length[0], 0.0, masked_score).astype(F32)

    def short(i, prev):
        return short_call(
            i, short_lengths[i : i + 1], seq_weight[1 + i : 2 + i], tokens_short,
            upstream_short, mod_seq[1 + i], weights, prev,
        )

    q, kv_own = long_in(tokens_long, mod_seq[0], w_qkv)
    kv = grid.over_seq(kv_own)
    res0 = short(0, None)
    (
        out_long, dx1, d_o, stat, stat_rows, dw_out_l, dw_up_l, dw_down_l, dmod_mid,
    ) = long_mid(
        start_len, seq_weight[:1], tokens_long, upstream_long, mod_seq[0], q, kv, bias,
        w_out, w_up, w_down,
    )
    q_all = grid.over_seq(q)
    do_all = grid.over_seq(d_o)
    rows_all = grid.over_seq(stat_rows[None])
    res1 = short(1, res0[:2])
    grad_long, dw_qkv_l, dmod_back = long_back(
        start_len, tokens_long, mod_seq[0], q, kv_own, kv, bias, d_o, stat,
        q_all, do_all, rows_all, dx1, w_qkv,
    )
    out_short, grad_short = res1[:2]
    terms = []
    for i, extra in enumerate((dw_qkv_l, dw_out_l, dw_up_l, dw_down_l)):
        terms += [res0[2 + i], res1[2 + i], extra]
    cond_t = jnp.pad(cond.astype(F32).T, ((0, 0), (0, 5)))
    parts = pack(
        grid.nq, sizes, idx_out, own, cond_t, (dmod_mid, dmod_back, res0[6], res1[6]), terms
    )
    g = grid.reduce_slots(parts)
    grad_slots, first_new, second_new, weight_new = soap(
        grid.nq, grid.part_order(), g, basis_left, basis_right, first_moment,
        second_moment, master_slots,
    )
    return (
        out_long, out_short, grad_long, grad_short,
        grad_slots, first_new, second_new, weight_new,
    )


def solution(mesh):
    rows = P(("dp", "seq"), None, None)
    cols = P("dp", "seq", None)
    slots = P("dp", None, None)
    return jax.shard_map(
        local,
        mesh=mesh,
        in_specs=(cols, rows, cols, rows) + (P(),) * 6 + (slots,) * 5,
        out_specs=(cols, rows, cols, rows) + (slots,) * 4,
        check_vma=False,
    )
```

```python
import functools

import jax
import jax.numpy as jnp
from jax import lax
from jax.experimental import pallas as pl
from jax.experimental.pallas import tpu as pltpu
from jax.sharding import PartitionSpec as P

D = 384
HEADS = 6
HD = 64
FF = 1536
STEP = 10
TILE = 128
PAIRS = HEADS // 2
SHAPES = ((D, 6 * D), (D, 3 * D), (D, D), (D, FF), (FF, D))

F32 = jnp.float32
BF16 = jnp.bfloat16
beta_first = 0.9
beta_second = 0.95
adam_eps = 1e-08
base_rate = 0.3
decay_rate = 0.01
norm_eps = 1e-06
masked_score = -1e30
score_scale = HD ** (-0.5)
FF_BLOCK = 256
Q_BLOCK = 128


VMEM = pl.BlockSpec(memory_space=pltpu.VMEM)
SMEM = pl.BlockSpec(memory_space=pltpu.SMEM)
ANY = pl.BlockSpec(memory_space=pl.ANY)


def dot_nn(a, b):
    return lax.dot_general(a, b, (((1,), (0,)), ((), ())), preferred_element_type=F32)


def dot_nt(a, b):
    return lax.dot_general(a, b, (((1,), (1,)), ((), ())), preferred_element_type=F32)


def dot_tn(a, b):
    return lax.dot_general(a, b, (((0,), (0,)), ((), ())), preferred_element_type=F32)


def norm_parts(v):
    centered = v - jnp.mean(v, axis=-1, keepdims=True)
    scale = lax.rsqrt(jnp.mean(centered * centered, axis=-1, keepdims=True) + norm_eps)
    return centered * scale, scale


def norm_back(dy, hat, scale):
    return scale * (
        dy
        - jnp.mean(dy, axis=-1, keepdims=True)
        - hat * jnp.mean(dy * hat, axis=-1, keepdims=True)
    )


def col_sum(v):
    return jnp.sum(v, axis=0, keepdims=True)


def head_mask(j):
    lane = lax.broadcasted_iota(jnp.int32, (1, 2 * HD), 1)
    return (lane >= j * HD) & (lane < (j + 1) * HD)


def only_head(v, j):
    return jnp.where(head_mask(j), v, jnp.zeros_like(v))


def gelu_both(u):
    k0 = 0.7978845608028654
    sq = u * u
    t = jnp.tanh(u * (k0 + (k0 * 0.044715) * sq))
    half = 0.5 * (1.0 + t)
    slope = half + (0.5 * u) * (1.0 - t * t) * (k0 + (3.0 * k0 * 0.044715) * sq)
    return u * half, slope


def unpack_kernel(nq, sizes, idx, cond, *refs):
    srcs = refs[: len(sizes)]
    w_qkv, w_out, w_up, w_down, mod, buf, w_ada, sems = refs[len(sizes) :]
    part = TILE // nq
    copies = []
    base = 0
    for i, size in enumerate(sizes):
        cp = pltpu.make_async_copy(srcs[i], buf.at[pl.ds(base, size)], sems.at[i])
        cp.start()
        copies.append(cp)
        base += size
    for cp in copies:
        cp.wait()
    first = 0
    for (rows, cols), dst in zip(SHAPES, (w_ada, w_qkv, w_out, w_up, w_down)):
        nr, nc = rows // TILE, cols // TILE

        @pl.loop(0, nr)
        def _(r, first=first, nc=nc, dst=dst):
            for c in range(nc):
                for q in range(nq):
                    at = idx[(first + r * nc + c) * nq + q]
                    row = pl.multiple_of(r * TILE + q * part, part)
                    dst[pl.ds(row, part), c * TILE : (c + 1) * TILE] = buf[at]

        first += nr * nc
    mod[...] = dot_nn(cond[...], w_ada[...])


def unpack(nq, srcs, idx, cond):
    sizes = tuple(s.shape[0] for s in srcs)
    part = TILE // nq
    return pl.pallas_call(
        functools.partial(unpack_kernel, nq, sizes),
        name="unpack",
        out_shape=tuple(jax.ShapeDtypeStruct(s, BF16) for s in SHAPES[1:])
        + (jax.ShapeDtypeStruct((8, 6 * D), F32),),
        in_specs=[SMEM, VMEM] + [ANY] * len(srcs),
        out_specs=(VMEM,) * 5,
        scratch_shapes=[
            pltpu.VMEM((sum(sizes), part, TILE), BF16),
            pltpu.VMEM(SHAPES[0], BF16),
            pltpu.SemaphoreType.DMA((len(sizes),)),
        ],
        cost_estimate=pl.CostEstimate(flops=10**7, bytes_accessed=10**7, transcendentals=0),
    )(idx, cond, *srcs)


def mods_of(label, mod):
    row = mod[pl.ds(label[0], 1), :]
    return [row[:, i * D : (i + 1) * D] for i in range(6)]


def project(x, mod, w_qkv):
    hat, scale = norm_parts(x)
    a = (hat * (1.0 + mod[1]) + mod[0]).astype(BF16)
    return hat, scale, a, dot_nn(a, w_qkv[...]).astype(BF16)


def mlp_both(x, o_low, g, mod, w_out, w_up, w_down, dw_out, dw_up, dw_down, mo, dm):
    att = dot_nn(o_low, w_out[...])
    x1 = x + mod[2] * att
    hat, scale = norm_parts(x1)
    m = (hat * (1.0 + mod[4]) + mod[3]).astype(BF16)
    d_mo = (mod[5] * g).astype(BF16)
    mo[...] = jnp.zeros_like(mo)
    dm[...] = jnp.zeros_like(dm)

    @pl.loop(0, FF // FF_BLOCK)
    def _(b):
        cols = pl.ds(pl.multiple_of(b * FF_BLOCK, FF_BLOCK), FF_BLOCK)
        u = dot_nn(m, w_up[:, cols])
        d_r = dot_nt(d_mo, w_down[cols, :])
        act, slope = gelu_both(u)
        r = act.astype(BF16)
        du = (d_r * slope).astype(BF16)
        mo[...] += dot_nn(r, w_down[cols, :])
        dm[...] += dot_nt(du, w_up[:, cols])
        dw_up[:, cols] = dot_tn(m, du)
        dw_down[cols, :] = dot_tn(r, d_mo)

    mo_v = mo[...]
    out = (x1 + mod[5] * mo_v).astype(BF16)
    d_gate2 = col_sum(mo_v * g)
    dm_v = dm[...]
    d_shift2 = col_sum(dm_v)
    d_scale2 = col_sum(dm_v * hat)
    dx1 = g + norm_back(dm_v * (1.0 + mod[4]), hat, scale)
    d_att = (mod[2] * dx1).astype(BF16)
    d_gate1 = col_sum(att * dx1)
    dw_out[...] = dot_tn(o_low, d_att)
    d_o = dot_nt(d_att, w_out[...]).astype(BF16)
    return out, dx1, d_o, (d_gate1, d_shift2, d_scale2, d_gate2)


def project_back(dqkv, dx1, hat, scale, a, mod, w_qkv, dw_qkv):
    dw_qkv[...] = dot_tn(a, dqkv)
    d_a = dot_nt(dqkv, w_qkv[...])
    d_shift = col_sum(d_a)
    d_scale = col_sum(d_a * hat)
    return dx1 + norm_back(d_a * (1.0 + mod[1]), hat, scale), d_shift, d_scale


def cotangent(up, weight, rows_ok):
    return jnp.where(rows_ok, up.astype(F32) * weight, 0.0)


def short_kernel(
    which, label, length, weight, x_ref, up_ref, mod_ref, w_qkv, w_out, w_up, w_down, *refs
):
    if which:
        refs = refs[2:]
    (
        out_ref, grad_ref, dw_qkv, dw_out, dw_up, dw_down, dmod_ref,
        qkv, probs, o_f, mo, dm, d_o, dqkv, ds_s, x1_s,
    ) = refs
    n = x_ref.shape[1]
    mod = mods_of(label, mod_ref)
    x = x_ref[0].astype(F32)
    hat, scale, a, qkv_v = project(x, mod, w_qkv)
    qkv[...] = qkv_v
    key = lax.broadcasted_iota(jnp.int32, (1, n), 1)
    bias = jnp.where(key < length[0], 0.0, masked_score)

    @pl.loop(0, PAIRS)
    def _(hp):
        q_cols = pl.ds(pl.multiple_of(hp * 128, 128), 128)
        k2 = qkv[:, pl.ds(pl.multiple_of(D + hp * 128, 128), 128)]
        v2 = qkv[:, pl.ds(pl.multiple_of(2 * D + hp * 128, 128), 128)]

        @pl.loop(0, n // Q_BLOCK)
        def _(qb):
            rows = pl.ds(pl.multiple_of(qb * Q_BLOCK, Q_BLOCK), Q_BLOCK)
            q2 = qkv[rows, q_cols]
            o2 = None
            for j in range(2):
                s = dot_nt(q2, only_head(k2, j)) * score_scale + bias
                e = jnp.exp(s - jnp.max(s, axis=-1, keepdims=True))
                p = e / jnp.sum(e, axis=-1, keepdims=True)
                probs[hp * 2 + j, rows, :] = p
                part = dot_nn(p.astype(BF16), only_head(v2, j))
                o2 = part if o2 is None else o2 + part
            o_f[rows, q_cols] = o2

    row = lax.broadcasted_iota(jnp.int32, (n, 1), 0)
    g = cotangent(up_ref[0], weight[0], row < length[0])
    o_low = o_f[...].astype(BF16)
    out, dx1, d_o_v, dm_parts = mlp_both(
        x, o_low, g, mod, w_out, w_up, w_down, dw_out, dw_up, dw_down, mo, dm
    )
    out_ref[0] = out
    x1_s[...] = dx1
    d_o[...] = d_o_v

    @pl.loop(0, PAIRS)
    def _(hp):
        q_cols = pl.ds(pl.multiple_of(hp * 128, 128), 128)
        k_cols = pl.ds(pl.multiple_of(D + hp * 128, 128), 128)
        v_cols = pl.ds(pl.multiple_of(2 * D + hp * 128, 128), 128)
        k2 = qkv[:, k_cols]
        v2 = qkv[:, v_cols]

        @pl.loop(0, n // Q_BLOCK)
        def _(qb):
            rows = pl.ds(pl.multiple_of(qb * Q_BLOCK, Q_BLOCK), Q_BLOCK)
            do2 = d_o[rows, q_cols]
            prod = do2.astype(F32) * o_f[rows, q_cols]
            dq2 = None
            for j in range(2):
                dp = dot_nt(do2, only_head(v2, j))
                delta = jnp.sum(only_head(prod, j), axis=-1, keepdims=True)
                ds = (probs[hp * 2 + j, rows, :] * (dp - delta)).astype(BF16)
                ds_s[j, rows, :] = ds
                part = dot_nn(ds, only_head(k2, j))
                dq2 = part if dq2 is None else dq2 + part
            dqkv[rows, q_cols] = (dq2 * score_scale).astype(BF16)

        q2 = qkv[:, q_cols]
        do2 = d_o[:, q_cols]
        dk2 = jnp.where(head_mask(0), dot_tn(ds_s[0], q2), dot_tn(ds_s[1], q2))
        dqkv[:, k_cols] = (dk2 * score_scale).astype(BF16)
        p0 = probs[hp * 2].astype(BF16)
        p1 = probs[hp * 2 + 1].astype(BF16)
        dv2 = jnp.where(head_mask(0), dot_tn(p0, do2), dot_tn(p1, do2))
        dqkv[:, v_cols] = dv2.astype(BF16)

    x = x_ref[0].astype(F32)
    hat, scale = norm_parts(x)
    a = (hat * (1.0 + mod[1]) + mod[0]).astype(BF16)
    grad, d_shift1, d_scale1 = project_back(
        dqkv[...], x1_s[...], hat, scale, a, mod, w_qkv, dw_qkv
    )
    grad_ref[0] = grad
    pad = jnp.zeros((2, D), F32)
    dmod_ref[...] = jnp.concatenate([d_shift1, d_scale1, *dm_parts, pad], axis=0)


GRAD_SHAPES = tuple(jax.ShapeDtypeStruct(s, F32) for s in SHAPES[1:])


def short_call(which, label, length, weight, tokens, upstream, mod, weights, prev):
    count, n, _ = tokens.shape
    block = pl.BlockSpec((1, n, D), lambda i: (which, 0, 0))

    def whole(shape):
        return pl.BlockSpec(shape, lambda i: (0,) * len(shape))

    in_specs = [SMEM] * 3 + [block, block, whole((8, 6 * D))] + [whole(w.shape) for w in weights]
    args = [label, length, weight, tokens, upstream, mod, *weights]
    aliases = {}
    if prev is not None:
        in_specs += [ANY, ANY]
        aliases = {len(args): 0, len(args) + 1: 1}
        args += list(prev)
    return pl.pallas_call(
        functools.partial(short_kernel, 0 if prev is None else 1),
        name="short" + str(which),
        grid=(1,),
        out_shape=(
            jax.ShapeDtypeStruct(tokens.shape, BF16),
            jax.ShapeDtypeStruct(tokens.shape, F32),
            *GRAD_SHAPES,
            jax.ShapeDtypeStruct((8, D), F32),
        ),
        in_specs=in_specs,
        out_specs=(block, block, *[whole(s.shape) for s in GRAD_SHAPES], whole((8, D))),
        scratch_shapes=[
            pltpu.VMEM((n, 3 * D), BF16),
            pltpu.VMEM((HEADS, n, n), F32),
            pltpu.VMEM((n, D), F32),
            pltpu.VMEM((n, D), F32),
            pltpu.VMEM((n, D), F32),
            pltpu.VMEM((n, D), BF16),
            pltpu.VMEM((n, 3 * D), BF16),
            pltpu.VMEM((2, n, n), BF16),
            pltpu.VMEM((n, D), F32),
        ],
        input_output_aliases=aliases,
        cost_estimate=pl.CostEstimate(
            flops=8 * 10**9, bytes_accessed=2 * 10**7, transcendentals=2 * 10**6
        ),
    )(*args)


def long_in_kernel(label, x_ref, mod_ref, w_qkv, q_ref, kv_ref):
    _, _, _, qkv = project(x_ref[0].astype(F32), mods_of(label, mod_ref), w_qkv)
    q_ref[...] = qkv[:, :D]
    kv_ref[...] = qkv[:, D:]


def long_in(label, tokens, mod, w_qkv):
    n = tokens.shape[1]
    return pl.pallas_call(
        long_in_kernel,
        name="long_in",
        out_shape=(
            jax.ShapeDtypeStruct((n, D), BF16),
            jax.ShapeDtypeStruct((n, 2 * D), BF16),
        ),
        in_specs=[SMEM] + [VMEM] * 3,
        out_specs=(VMEM,) * 2,
        cost_estimate=pl.CostEstimate(flops=10**8, bytes_accessed=10**6, transcendentals=0),
    )(label, tokens, mod, w_qkv)


def long_mid_kernel(
    label, start_len, weight, x_ref, up_ref, mod_ref, q_ref, kv, bias_ref,
    w_out, w_up, w_down,
    out_ref, dx1_ref, do_ref, stat_ref, row_ref, dw_out, dw_up, dw_down, dmod_ref,
    o_f, mo, dm,
):
    n = x_ref.shape[1]
    mod = mods_of(label, mod_ref)
    bias = bias_ref[...]
    lane = lax.broadcasted_iota(jnp.int32, (1, 128), 1)
    stat_ref[...] = jnp.zeros_like(stat_ref)

    @pl.loop(0, PAIRS)
    def _(hp):
        q_cols = pl.ds(pl.multiple_of(hp * 128, 128), 128)
        k2 = kv[:, q_cols]
        v2 = kv[:, pl.ds(pl.multiple_of(D + hp * 128, 128), 128)]

        @pl.loop(0, n // Q_BLOCK)
        def _(qb):
            rows = pl.ds(pl.multiple_of(qb * Q_BLOCK, Q_BLOCK), Q_BLOCK)
            q2 = q_ref[rows, q_cols]
            o2 = None
            for j in range(2):
                s = dot_nt(q2, only_head(k2, j)) * score_scale + bias
                top = jnp.max(s, axis=-1, keepdims=True)
                e = jnp.exp(s - top)
                total = jnp.sum(e, axis=-1, keepdims=True)
                part = dot_nn(e.astype(BF16), only_head(v2, j)) / total
                o2 = part if o2 is None else o2 + part
                lse = top + jnp.log(total)
                stat_ref[rows, :] += jnp.where(lane == hp * 2 + j, lse, 0.0)
            o_f[rows, q_cols] = o2

    row = start_len[0] + lax.broadcasted_iota(jnp.int32, (n, 1), 0)
    g = cotangent(up_ref[0], weight[0], row < start_len[1])
    o_low = o_f[...].astype(BF16)
    out, dx1, d_o, dm_parts = mlp_both(
        x_ref[0].astype(F32), o_low, g, mod, w_out, w_up, w_down,
        dw_out, dw_up, dw_down, mo, dm,
    )
    out_ref[0] = out
    dx1_ref[...] = dx1
    do_ref[...] = d_o
    stat = stat_ref[...]
    for hp in range(PAIRS):
        cols = slice(hp * 128, (hp + 1) * 128)
        prod = d_o[:, cols].astype(F32) * o_f[:, cols]
        for j in range(2):
            delta = jnp.sum(only_head(prod, j), axis=-1, keepdims=True)
            stat = stat + jnp.where(lane == 8 + hp * 2 + j, delta, 0.0)
    stat_ref[...] = stat
    row_ref[...] = stat.T[:16, :]
    pad = jnp.zeros((4, D), F32)
    dmod_ref[...] = jnp.concatenate([*dm_parts, pad], axis=0)


def long_mid(label, start_len, weight, tokens, *args):
    n = tokens.shape[1]
    return pl.pallas_call(
        long_mid_kernel,
        name="long_mid",
        out_shape=(
            jax.ShapeDtypeStruct(tokens.shape, BF16),
            jax.ShapeDtypeStruct((n, D), F32),
            jax.ShapeDtypeStruct((n, D), BF16),
            jax.ShapeDtypeStruct((n, 128), F32),
            jax.ShapeDtypeStruct((16, n), F32),
            *GRAD_SHAPES[1:],
            jax.ShapeDtypeStruct((8, D), F32),
        ),
        in_specs=[SMEM] * 3 + [VMEM] * 9,
        out_specs=(VMEM,) * 9,
        scratch_shapes=[pltpu.VMEM((n, D), F32)] * 3,
        cost_estimate=pl.CostEstimate(
            flops=4 * 10**9, bytes_accessed=2 * 10**7, transcendentals=2 * 10**6
        ),
    )(label, start_len, weight, tokens, *args)


def long_back_kernel(
    label, start_len, x_ref, mod_ref, q_ref, kv_own, kv, bias_ref, do_ref, stat_ref,
    q_all, do_all, rows_all, dx1_ref, w_qkv,
    grad_ref, dw_qkv, dmod_ref, dqkv, dk_s, dv_s,
):
    n = x_ref.shape[1]
    total = kv.shape[0]
    mod = mods_of(label, mod_ref)
    bias = bias_ref[...]
    lane = lax.broadcasted_iota(jnp.int32, (1, 128), 1)

    @pl.loop(0, PAIRS)
    def _(hp):
        q_cols = pl.ds(pl.multiple_of(hp * 128, 128), 128)
        k_cols = pl.ds(pl.multiple_of(D + hp * 128, 128), 128)
        v_cols = pl.ds(pl.multiple_of(2 * D + hp * 128, 128), 128)
        k2 = kv[:, q_cols]
        v2 = kv[:, k_cols]

        @pl.loop(0, n // Q_BLOCK)
        def _(qb):
            rows = pl.ds(pl.multiple_of(qb * Q_BLOCK, Q_BLOCK), Q_BLOCK)
            q2 = q_ref[rows, q_cols]
            do2 = do_ref[rows, q_cols]
            stat = stat_ref[rows, :]
            dq2 = None
            for j in range(2):
                kz = only_head(k2, j)
                h = hp * 2 + j
                lse = jnp.sum(jnp.where(lane == h, stat, 0.0), axis=-1, keepdims=True)
                delta = jnp.sum(jnp.where(lane == 8 + h, stat, 0.0), axis=-1, keepdims=True)
                p = jnp.exp(dot_nt(q2, kz) * score_scale + bias - lse)
                dp = dot_nt(do2, only_head(v2, j))
                ds = (p * (dp - delta)).astype(BF16)
                part = dot_nn(ds, kz)
                dq2 = part if dq2 is None else dq2 + part
            dqkv[rows, q_cols] = (dq2 * score_scale).astype(BF16)

        k_own = kv_own[:, q_cols]
        v_own = kv_own[:, k_cols]
        dk_s[...] = jnp.zeros_like(dk_s)
        dv_s[...] = jnp.zeros_like(dv_s)

        @pl.loop(0, total // n)
        def _(qc):
            rows = pl.ds(pl.multiple_of(qc * n, n), n)
            q2 = q_all[rows, q_cols]
            do2 = do_all[rows, q_cols]
            for j in range(2):
                h = hp * 2 + j
                lse = rows_all[qc, pl.ds(h, 1), :]
                delta = rows_all[qc, pl.ds(8 + h, 1), :]
                p = jnp.exp(dot_nt(only_head(k_own, j), q2) * score_scale - lse)
                dp = dot_nt(only_head(v_own, j), do2)
                ds = (p * (dp - delta)).astype(BF16)
                dv_s[j] += dot_nn(p.astype(BF16), do2)
                dk_s[j] += dot_nn(ds, q2)

        row = start_len[0] + lax.broadcasted_iota(jnp.int32, (n, 1), 0)
        ok = row < start_len[1]
        dk2 = jnp.where(head_mask(0), dk_s[0], dk_s[1])
        dv2 = jnp.where(head_mask(0), dv_s[0], dv_s[1])
        dqkv[:, k_cols] = jnp.where(ok, dk2 * score_scale, 0.0).astype(BF16)
        dqkv[:, v_cols] = jnp.where(ok, dv2, 0.0).astype(BF16)

    hat, scale = norm_parts(x_ref[0].astype(F32))
    a = (hat * (1.0 + mod[1]) + mod[0]).astype(BF16)
    grad, d_shift1, d_scale1 = project_back(
        dqkv[...], dx1_ref[...], hat, scale, a, mod, w_qkv, dw_qkv
    )
    grad_ref[0] = grad
    pad = jnp.zeros((6, D), F32)
    dmod_ref[...] = jnp.concatenate([d_shift1, d_scale1, pad], axis=0)


def long_back(label, start_len, tokens, *args):
    n = tokens.shape[1]
    return pl.pallas_call(
        long_back_kernel,
        name="long_back",
        out_shape=(
            jax.ShapeDtypeStruct(tokens.shape, F32),
            GRAD_SHAPES[0],
            jax.ShapeDtypeStruct((8, D), F32),
        ),
        in_specs=[SMEM] * 2 + [VMEM] * 13,
        out_specs=(VMEM,) * 3,
        scratch_shapes=[
            pltpu.VMEM((n, 3 * D), BF16),
            pltpu.VMEM((2, n, 128), F32),
            pltpu.VMEM((2, n, 128), F32),
        ],
        cost_estimate=pl.CostEstimate(
            flops=4 * 10**9, bytes_accessed=10**7, transcendentals=4 * 10**6
        ),
    )(label, start_len, tokens, *args)


def pack_kernel(nq, sizes, idx, labels, cond_t, dmod_mid, dmod_back, dmod_s0, dmod_s1, *refs):
    grads = refs[:12]
    outs = refs[12 : 12 + len(sizes)]
    buf, sems = refs[12 + len(sizes) :]
    part = TILE // nq
    buf[...] = jnp.zeros_like(buf)
    d_long = jnp.concatenate([dmod_back[:2, :], dmod_mid[:4, :]], axis=0)
    per_seq = (d_long, dmod_s0[:6, :], dmod_s1[:6, :])
    by_label = []
    for v in range(3):
        acc = None
        for s in range(3):
            term = jnp.where(labels[s] == v, per_seq[s], 0.0)
            acc = term if acc is None else acc + term
        by_label.append(acc)
    first = 0
    for r in range(D // TILE):
        col = [cond_t[r * TILE : (r + 1) * TILE, v : v + 1] for v in range(3)]
        for c in range(6 * D // TILE):
            i, off = divmod(c, D // TILE)
            lanes = slice(off * TILE, (off + 1) * TILE)
            tile = None
            for v in range(3):
                term = col[v] * by_label[v][i : i + 1, lanes]
                tile = term if tile is None else tile + term
            tile = tile.astype(BF16)
            t = first + r * (6 * D // TILE) + c
            for q in range(nq):
                buf[idx[t * nq + q]] = tile[q * part : (q + 1) * part]
    first += SHAPES[0][0] * SHAPES[0][1] // TILE**2
    at = 0
    for (rows, cols), many in zip(SHAPES[1:], (3, 3, 3, 3)):
        nr, nc = rows // TILE, cols // TILE
        terms = grads[at : at + many]
        at += many

        @pl.loop(0, nr)
        def _(r, first=first, nc=nc, terms=terms):
            for c in range(nc):
                for q in range(nq):
                    row = pl.multiple_of(r * TILE + q * part, part)
                    lanes = slice(c * TILE, (c + 1) * TILE)
                    v = terms[0][pl.ds(row, part), lanes]
                    for other in terms[1:]:
                        v = v + other[pl.ds(row, part), lanes]
                    buf[idx[(first + r * nc + c) * nq + q]] = v.astype(BF16)

        first += nr * nc
    copies = []
    base = 0
    for i, size in enumerate(sizes):
        cp = pltpu.make_async_copy(buf.at[pl.ds(base, size)], outs[i], sems.at[i])
        cp.start()
        copies.append(cp)
        base += size
    for cp in copies:
        cp.wait()


def pack(nq, sizes, idx, labels, cond_t, dmods, grads):
    part = TILE // nq
    return pl.pallas_call(
        functools.partial(pack_kernel, nq, sizes),
        name="pack",
        out_shape=tuple(jax.ShapeDtypeStruct((s, part, TILE), BF16) for s in sizes),
        in_specs=[SMEM, SMEM] + [VMEM] * 17,
        out_specs=(ANY,) * len(sizes),
        scratch_shapes=[
            pltpu.VMEM((sum(sizes), part, TILE), BF16),
            pltpu.SemaphoreType.DMA((len(sizes),)),
        ],
        cost_estimate=pl.CostEstimate(flops=10**7, bytes_accessed=3 * 10**7, transcendentals=0),
    )(idx, labels, cond_t, *dmods, *grads)


def halves(v):
    high = v.astype(BF16)
    return high, (v - high.astype(F32)).astype(BF16)


def dot3(dot, a, b):
    return dot(a[0], b[0]) + (dot(a[0], b[1]) + dot(a[1], b[0]))


def soap_kernel(nq, order, g_ref, left, right, first, second, master, gs, fn, sn, wn):
    part = TILE // nq
    for i in range(master.shape[0]):
        g = jnp.concatenate([g_ref[order[q], i] for q in range(nq)], axis=0).astype(F32)
        gs[i] = g
        lo = halves(left[i])
        ro = halves(right[i])
        rot = dot3(dot_nn, halves(dot3(dot_tn, lo, halves(g))), ro)
        f = beta_first * first[i] + (1.0 - beta_first) * rot
        s = beta_second * second[i] + (1.0 - beta_second) * rot * rot
        fn[i] = f
        sn[i] = s
        step = (
            f
            / (1.0 - beta_first**STEP)
            / (jnp.sqrt(s / (1.0 - beta_second**STEP)) + adam_eps)
        )
        back = dot3(dot_nt, halves(dot3(dot_nn, lo, halves(step))), ro)
        w = master[i]
        mean = jnp.mean(jnp.mean(w * w, axis=1, keepdims=True), axis=0, keepdims=True)
        spread = jnp.sqrt(mean + 1e-06)
        wn[i] = w - base_rate * spread * (back + decay_rate * w)


def soap(nq, order, g, left, right, first, second, master):
    slots = master.shape[0]
    block = max(k for k in range(1, 12) if slots % k == 0)
    part = TILE // nq
    spec = pl.BlockSpec((block, TILE, TILE), lambda i: (i, 0, 0))
    g_spec = pl.BlockSpec((nq, block, part, TILE), lambda i: (0, i, 0, 0))
    shape = jax.ShapeDtypeStruct(master.shape, F32)
    return pl.pallas_call(
        functools.partial(soap_kernel, nq),
        name="soap",
        grid=(slots // block,),
        out_shape=(shape,) * 4,
        in_specs=[SMEM, g_spec] + [spec] * 5,
        out_specs=(spec,) * 4,
        cost_estimate=pl.CostEstimate(flops=10**9, bytes_accessed=10**7, transcendentals=10**6),
    )(order, g, left, right, first, second, master)


class Grid:
    def __init__(self, n_dp, n_seq):
        self.direct = n_dp == 8 and n_seq == 4
        self.n = {"z": n_dp // 2, "y": 2, "x": n_seq // 2, "c": 2}
        self.n_dp = n_dp
        self.n_seq = n_seq
        self.nq = n_seq if self.direct else 1

    def here(self):
        dp = lax.axis_index("dp")
        seq = lax.axis_index("seq")
        return {"z": dp // 2, "y": dp % 2, "x": seq // 2, "c": seq % 2}

    def shift(self, v, name):
        axis, total = ("dp", self.n_dp) if name in "zy" else ("seq", self.n_seq)
        pairs = []
        for i in range(total):
            hi, lo = divmod(i, 2)
            if name in ("z", "x", "xc"):
                hi = (hi + 1) % (total // 2)
            if name in ("y", "c", "xc"):
                lo = (lo + 1) % 2
            pairs.append((i, hi * 2 + lo))
        return lax.ppermute(v, axis, pairs)

    def ring(self, v, name):
        out = [v]
        for _ in range(self.n[name] - 1):
            out.append(self.shift(out[-1], name))
        return out

    def over_seq(self, v):
        if not self.direct:
            return lax.all_gather(v, "seq", axis=0, tiled=True)
        return jnp.concatenate([v] + [self.shift(v, n) for n in ("x", "c", "xc")], axis=0)

    def seq_blocks(self):
        if not self.direct:
            return jnp.arange(self.n_seq, dtype=jnp.int32)
        at = self.here()
        return jnp.stack(
            [((at["x"] - rx) % 2) * 2 + (at["c"] - rc) % 2 for rc in range(2) for rx in range(2)]
        )

    def table(self, tile_slot, slots, sign):
        if not self.direct:
            return tile_slot, (self.n_dp * slots,)
        at = self.here()
        ka = (slots + 1) // 2
        kb = slots - ka
        owner = tile_slot // slots
        local = tile_slot % slots
        nz, ny, nx = self.n["z"], self.n["y"], self.n["x"]
        rz = (sign * (at["z"] - owner // 2)) % nz
        ry = (at["y"] - owner % 2) % ny
        parts = []
        for q in range(self.nq):
            rx = (at["x"] - q // 2) % nx
            rc = (at["c"] - q % 2) % 2
            in_a = (((rc * nx + rx) * ny + ry) * nz + rz) * ka + local
            in_b = (((rc * ny + ry) * nx + rx) * nz + rz) * kb + (local - ka)
            parts.append(jnp.where(local < ka, in_a, 2 * nx * ny * nz * ka + in_b))
        sizes = (nx * ny * nz * ka,) * 2 + (nx * ny * nz * kb,) * 2
        return jnp.stack(parts, axis=1).reshape(-1), sizes

    def gather_slots(self, low):
        if not self.direct:
            return [lax.all_gather(low, "dp", axis=0, tiled=True)]
        part = TILE // self.nq
        own = lax.dynamic_slice_in_dim(low, lax.axis_index("seq") * part, part, 1)
        ka = (low.shape[0] + 1) // 2
        out = []
        planes = self.ring(own, "z")
        groups = ((planes, slice(0, ka), "yx"), (planes, slice(ka, None), "xy"))
        for pieces, which, order in groups:
            piece = jnp.concatenate([p[which] for p in pieces], axis=0)
            for name in order:
                piece = jnp.concatenate(self.ring(piece, name), axis=0)
            out += self.ring(piece, "c")
        return out

    def stage(self, v, name):
        n = self.n[name]
        k = v.shape[0] // n
        acc = v[(n - 1) * k :]
        for r in range(n - 2, -1, -1):
            acc = self.shift(acc, name).astype(F32) + v[r * k : (r + 1) * k].astype(F32)
            if r:
                acc = acc.astype(BF16)
        return acc

    def reduce_slots(self, parts):
        if not self.direct:
            total = lax.psum_scatter(
                parts[0].astype(F32), "dp", scatter_dimension=0, tiled=True
            )
            return lax.psum(total, "seq")[None]
        planes = []
        nz = self.n["z"]
        for own, send, order in ((parts[0], parts[1], "xy"), (parts[2], parts[3], "yx")):
            acc = self.shift(send, "c").astype(F32) + own.astype(F32)
            for name in order:
                acc = self.stage(acc.astype(BF16), name)
            planes.append(acc.reshape(nz, -1, *acc.shape[1:]))
        both = jnp.concatenate(planes, axis=1).astype(BF16)
        mine = self.stage(both.reshape(-1, *both.shape[2:]), "z").astype(BF16)
        return self.over_seq(mine[None])

    def part_order(self):
        if not self.direct:
            return jnp.zeros((1,), jnp.int32)
        at = self.here()
        return jnp.stack(
            [((at["c"] - q % 2) % 2) * 2 + (at["x"] - q // 2) % 2 for q in range(self.nq)]
        )


def local(
    tokens_long,
    tokens_short,
    upstream_long,
    upstream_short,
    interval_table,
    labels_long,
    labels_short,
    lengths_long,
    lengths_short,
    tile_slot,
    master_slots,
    basis_left,
    basis_right,
    first_moment,
    second_moment,
):
    grid = Grid(lax.axis_size("dp"), lax.axis_size("seq"))
    slots = master_slots.shape[0]
    dp_index = lax.axis_index("dp")
    seq_index = lax.axis_index("seq")
    rows = tokens_long.shape[1]
    short_count = tokens_short.shape[0]

    srcs = grid.gather_slots(master_slots.astype(BF16))
    idx_in, _ = grid.table(tile_slot, slots, 1)
    idx_out, sizes = grid.table(tile_slot, slots, -1)

    label_all = jnp.concatenate([labels_long, labels_short])
    kinds = jnp.arange(3, dtype=jnp.int32)
    counts = jnp.sum((label_all[:, None] == kinds[None, :]).astype(F32), axis=0)
    first_short = (dp_index * grid.n_seq + seq_index) * short_count
    own = jnp.concatenate(
        [
            lax.dynamic_slice_in_dim(labels_long, dp_index, 1),
            lax.dynamic_slice_in_dim(labels_short, first_short, short_count),
        ]
    )
    own_length = lax.dynamic_slice_in_dim(lengths_long, dp_index, 1)
    short_lengths = lax.dynamic_slice_in_dim(lengths_short, first_short, short_count)
    one_hot = (own[:, None] == kinds[None, :]).astype(F32)
    seq_weight = float(label_all.shape[0]) / (3.0 * jnp.sum(one_hot * counts[None, :], axis=1))

    cond = jax.nn.silu(interval_table).astype(BF16)
    cond_pad = jnp.concatenate([cond, jnp.zeros((5, D), BF16)], axis=0)
    *weights, mod_table = unpack(grid.nq, srcs, idx_in, cond_pad)
    w_qkv, w_out, w_up, w_down = weights

    long_start = seq_index * rows
    start_len = jnp.concatenate([long_start[None].astype(jnp.int32), own_length])
    blocks = grid.seq_blocks()
    pos = (blocks[:, None] * rows + jnp.arange(rows, dtype=jnp.int32)[None, :]).reshape(1, -1)
    bias = jnp.where(pos < own_length[0], 0.0, masked_score).astype(F32)

    def short(i, prev):
        return short_call(
            i, own[1 + i : 2 + i], short_lengths[i : i + 1], seq_weight[1 + i : 2 + i],
            tokens_short, upstream_short, mod_table, weights, prev,
        )

    q, kv_own = long_in(own[:1], tokens_long, mod_table, w_qkv)
    kv = grid.over_seq(kv_own)
    res0 = short(0, None)
    kv, dmod_s0 = lax.optimization_barrier((kv, res0[6]))
    (
        out_long, dx1, d_o, stat, stat_rows, dw_out_l, dw_up_l, dw_down_l, dmod_mid,
    ) = long_mid(
        own[:1], start_len, seq_weight[:1], tokens_long, upstream_long, mod_table, q, kv,
        bias, w_out, w_up, w_down,
    )
    q_all = grid.over_seq(q)
    do_all = grid.over_seq(d_o)
    rows_all = grid.over_seq(stat_rows[None])
    prev0, prev1, dmod_mid = lax.optimization_barrier((res0[0], res0[1], dmod_mid))
    res1 = short(1, (prev0, prev1))
    q_all, do_all, rows_all, dmod_s1 = lax.optimization_barrier(
        (q_all, do_all, rows_all, res1[6])
    )
    grad_long, dw_qkv_l, dmod_back = long_back(
        own[:1], start_len, tokens_long, mod_table, q, kv_own, kv, bias, d_o, stat,
        q_all, do_all, rows_all, dx1, w_qkv,
    )
    out_short, grad_short = res1[:2]
    terms = []
    for i, extra in enumerate((dw_qkv_l, dw_out_l, dw_up_l, dw_down_l)):
        terms += [res0[2 + i], res1[2 + i], extra]
    cond_t = jnp.pad(cond.astype(F32).T, ((0, 0), (0, 5)))
    parts = pack(
        grid.nq, sizes, idx_out, own, cond_t, (dmod_mid, dmod_back, dmod_s0, dmod_s1), terms
    )
    g = grid.reduce_slots(parts)
    grad_slots, first_new, second_new, weight_new = soap(
        grid.nq, grid.part_order(), g, basis_left, basis_right, first_moment,
        second_moment, master_slots,
    )
    return (
        out_long, out_short, grad_long, grad_short,
        grad_slots, first_new, second_new, weight_new,
    )


def solution(mesh):
    rows = P(("dp", "seq"), None, None)
    cols = P("dp", "seq", None)
    slots = P("dp", None, None)
    return jax.shard_map(
        local,
        mesh=mesh,
        in_specs=(cols, rows, cols, rows) + (P(),) * 6 + (slots,) * 5,
        out_specs=(cols, rows, cols, rows) + (slots,) * 4,
        check_vma=False,
    )
```

```python
import functools

import jax
import jax.numpy as jnp
from jax import lax
from jax.experimental import pallas as pl
from jax.experimental.pallas import tpu as pltpu
from jax.sharding import PartitionSpec as P

D = 384
HEADS = 6
HD = 64
FF = 1536
STEP = 10
TILE = 128
PAIRS = HEADS // 2
SHAPES = ((D, 6 * D), (D, 3 * D), (D, D), (D, FF), (FF, D))

F32 = jnp.float32
BF16 = jnp.bfloat16
beta_first = 0.9
beta_second = 0.95
adam_eps = 1e-08
base_rate = 0.3
decay_rate = 0.01
norm_eps = 1e-06
masked_score = -1e30
score_scale = HD ** (-0.5)
FF_BLOCK = 768


VMEM = pl.BlockSpec(memory_space=pltpu.VMEM)
SMEM = pl.BlockSpec(memory_space=pltpu.SMEM)
ANY = pl.BlockSpec(memory_space=pl.ANY)


def dot_nn(a, b):
    return lax.dot_general(a, b, (((1,), (0,)), ((), ())), preferred_element_type=F32)


def dot_nt(a, b):
    return lax.dot_general(a, b, (((1,), (1,)), ((), ())), preferred_element_type=F32)


def dot_tn(a, b):
    return lax.dot_general(a, b, (((0,), (0,)), ((), ())), preferred_element_type=F32)


def norm_parts(v):
    centered = v - jnp.mean(v, axis=-1, keepdims=True)
    scale = lax.rsqrt(jnp.mean(centered * centered, axis=-1, keepdims=True) + norm_eps)
    return centered * scale, scale


def norm_back(dy, hat, scale):
    return scale * (
        dy
        - jnp.mean(dy, axis=-1, keepdims=True)
        - hat * jnp.mean(dy * hat, axis=-1, keepdims=True)
    )


def col_sum(v):
    return jnp.sum(v, axis=0, keepdims=True)


def head_mask(j):
    lane = lax.broadcasted_iota(jnp.int32, (1, 2 * HD), 1)
    return (lane >= j * HD) & (lane < (j + 1) * HD)


def only_head(v, j):
    return jnp.where(head_mask(j), v, jnp.zeros_like(v))


def gelu_both(u):
    k0 = 0.7978845608028654
    sq = u * u
    t = jnp.tanh(u * (k0 + (k0 * 0.044715) * sq))
    half = 0.5 * (1.0 + t)
    slope = half + (0.5 * u) * (1.0 - t * t) * (k0 + (3.0 * k0 * 0.044715) * sq)
    return u * half, slope


def unpack_kernel(nq, sizes, idx, cond, *refs):
    srcs = refs[: len(sizes)]
    w_qkv, w_out, w_up, w_down, mod, buf, w_ada, sems = refs[len(sizes) :]
    part = TILE // nq
    copies = []
    base = 0
    for i, size in enumerate(sizes):
        cp = pltpu.make_async_copy(srcs[i], buf.at[pl.ds(base, size)], sems.at[i])
        cp.start()
        copies.append(cp)
        base += size
    for cp in copies:
        cp.wait()
    first = 0
    for (rows, cols), dst in zip(SHAPES, (w_ada, w_qkv, w_out, w_up, w_down)):
        nr, nc = rows // TILE, cols // TILE

        @pl.loop(0, nr)
        def _(r, first=first, nc=nc, dst=dst):
            for c in range(nc):
                for q in range(nq):
                    at = idx[(first + r * nc + c) * nq + q]
                    row = pl.multiple_of(r * TILE + q * part, part)
                    dst[pl.ds(row, part), c * TILE : (c + 1) * TILE] = buf[at]

        first += nr * nc
    mod[...] = dot_nn(cond[...], w_ada[...])


def unpack(nq, srcs, idx, cond):
    sizes = tuple(s.shape[0] for s in srcs)
    part = TILE // nq
    return pl.pallas_call(
        functools.partial(unpack_kernel, nq, sizes),
        name="unpack",
        out_shape=tuple(jax.ShapeDtypeStruct(s, BF16) for s in SHAPES[1:])
        + (jax.ShapeDtypeStruct((8, 6 * D), F32),),
        in_specs=[SMEM, VMEM] + [ANY] * len(srcs),
        out_specs=(VMEM,) * 5,
        scratch_shapes=[
            pltpu.VMEM((sum(sizes), part, TILE), BF16),
            pltpu.VMEM(SHAPES[0], BF16),
            pltpu.SemaphoreType.DMA((len(sizes),)),
        ],
        cost_estimate=pl.CostEstimate(flops=10**7, bytes_accessed=10**7, transcendentals=0),
    )(idx, cond, *srcs)


def mods_of(label, mod):
    row = mod[pl.ds(label[0], 1), :]
    return [row[:, i * D : (i + 1) * D] for i in range(6)]


def project(x, mod, w_qkv):
    hat, scale = norm_parts(x)
    a = (hat * (1.0 + mod[1]) + mod[0]).astype(BF16)
    return hat, scale, a, dot_nn(a, w_qkv[...]).astype(BF16)


def mlp_both(x, o_low, g, mod, w_out, w_up, w_down, dw_out, dw_up, dw_down, mo, dm):
    att = dot_nn(o_low, w_out[...])
    x1 = x + mod[2] * att
    hat, scale = norm_parts(x1)
    m = (hat * (1.0 + mod[4]) + mod[3]).astype(BF16)
    d_mo = (mod[5] * g).astype(BF16)
    mo[...] = jnp.zeros_like(mo)
    dm[...] = jnp.zeros_like(dm)

    @pl.loop(0, FF // FF_BLOCK)
    def _(b):
        cols = pl.ds(pl.multiple_of(b * FF_BLOCK, FF_BLOCK), FF_BLOCK)
        u = dot_nn(m, w_up[:, cols])
        d_r = dot_nt(d_mo, w_down[cols, :])
        act, slope = gelu_both(u)
        r = act.astype(BF16)
        du = (d_r * slope).astype(BF16)
        mo[...] += dot_nn(r, w_down[cols, :])
        dm[...] += dot_nt(du, w_up[:, cols])
        dw_up[:, cols] = dot_tn(m, du)
        dw_down[cols, :] = dot_tn(r, d_mo)

    mo_v = mo[...]
    out = (x1 + mod[5] * mo_v).astype(BF16)
    d_gate2 = col_sum(mo_v * g)
    dm_v = dm[...]
    d_shift2 = col_sum(dm_v)
    d_scale2 = col_sum(dm_v * hat)
    dx1 = g + norm_back(dm_v * (1.0 + mod[4]), hat, scale)
    d_att = (mod[2] * dx1).astype(BF16)
    d_gate1 = col_sum(att * dx1)
    dw_out[...] = dot_tn(o_low, d_att)
    d_o = dot_nt(d_att, w_out[...]).astype(BF16)
    return out, dx1, d_o, (d_gate1, d_shift2, d_scale2, d_gate2)


def project_back(dqkv, dx1, hat, scale, a, mod, w_qkv, dw_qkv):
    dw_qkv[...] = dot_tn(a, dqkv)
    d_a = dot_nt(dqkv, w_qkv[...])
    d_shift = col_sum(d_a)
    d_scale = col_sum(d_a * hat)
    return dx1 + norm_back(d_a * (1.0 + mod[1]), hat, scale), d_shift, d_scale


def cotangent(up, weight, rows_ok):
    return jnp.where(rows_ok, up.astype(F32) * weight, 0.0)


def short_kernel(
    which, label, length, weight, x_ref, up_ref, mod_ref, w_qkv, w_out, w_up, w_down, *refs
):
    if which:
        refs = refs[2:]
    (
        out_ref, grad_ref, dw_qkv, dw_out, dw_up, dw_down, dmod_ref,
        qkv, probs, o_f, mo, dm, d_o, dqkv, ds_s, x1_s,
    ) = refs
    n = x_ref.shape[1]
    mod = mods_of(label, mod_ref)
    x = x_ref[0].astype(F32)
    hat, scale, a, qkv_v = project(x, mod, w_qkv)
    qkv[...] = qkv_v
    key = lax.broadcasted_iota(jnp.int32, (1, n), 1)
    bias = jnp.where(key < length[0], 0.0, masked_score)

    @pl.loop(0, PAIRS)
    def _(hp):
        q_cols = pl.ds(pl.multiple_of(hp * 128, 128), 128)
        k2 = qkv[:, pl.ds(pl.multiple_of(D + hp * 128, 128), 128)]
        v2 = qkv[:, pl.ds(pl.multiple_of(2 * D + hp * 128, 128), 128)]

        rows = slice(0, n)
        q2 = qkv[rows, q_cols]
        o2 = None
        for j in range(2):
            s = dot_nt(q2, only_head(k2, j)) * score_scale + bias
            e = jnp.exp(s - jnp.max(s, axis=-1, keepdims=True))
            p = e * (1.0 / jnp.sum(e, axis=-1, keepdims=True))
            probs[hp * 2 + j, rows, :] = p
            part = dot_nn(p.astype(BF16), only_head(v2, j))
            o2 = part if o2 is None else o2 + part
        o_f[rows, q_cols] = o2

    row = lax.broadcasted_iota(jnp.int32, (n, 1), 0)
    g = cotangent(up_ref[0], weight[0], row < length[0])
    o_low = o_f[...].astype(BF16)
    out, dx1, d_o_v, dm_parts = mlp_both(
        x, o_low, g, mod, w_out, w_up, w_down, dw_out, dw_up, dw_down, mo, dm
    )
    out_ref[0] = out
    x1_s[...] = dx1
    d_o[...] = d_o_v

    @pl.loop(0, PAIRS)
    def _(hp):
        q_cols = pl.ds(pl.multiple_of(hp * 128, 128), 128)
        k_cols = pl.ds(pl.multiple_of(D + hp * 128, 128), 128)
        v_cols = pl.ds(pl.multiple_of(2 * D + hp * 128, 128), 128)
        k2 = qkv[:, k_cols]
        v2 = qkv[:, v_cols]

        rows = slice(0, n)
        do2 = d_o[rows, q_cols]
        prod = do2.astype(F32) * o_f[rows, q_cols]
        dq2 = None
        for j in range(2):
            dp = dot_nt(do2, only_head(v2, j))
            delta = jnp.sum(only_head(prod, j), axis=-1, keepdims=True)
            ds = (probs[hp * 2 + j, rows, :] * (dp - delta)).astype(BF16)
            ds_s[j, rows, :] = ds
            part = dot_nn(ds, only_head(k2, j))
            dq2 = part if dq2 is None else dq2 + part
        dqkv[rows, q_cols] = (dq2 * score_scale).astype(BF16)

        q2 = qkv[:, q_cols]
        do2 = d_o[:, q_cols]
        dk2 = jnp.where(head_mask(0), dot_tn(ds_s[0], q2), dot_tn(ds_s[1], q2))
        dqkv[:, k_cols] = (dk2 * score_scale).astype(BF16)
        p0 = probs[hp * 2].astype(BF16)
        p1 = probs[hp * 2 + 1].astype(BF16)
        dv2 = jnp.where(head_mask(0), dot_tn(p0, do2), dot_tn(p1, do2))
        dqkv[:, v_cols] = dv2.astype(BF16)

    x = x_ref[0].astype(F32)
    hat, scale = norm_parts(x)
    a = (hat * (1.0 + mod[1]) + mod[0]).astype(BF16)
    grad, d_shift1, d_scale1 = project_back(
        dqkv[...], x1_s[...], hat, scale, a, mod, w_qkv, dw_qkv
    )
    grad_ref[0] = grad
    pad = jnp.zeros((2, D), F32)
    dmod_ref[...] = jnp.concatenate([d_shift1, d_scale1, *dm_parts, pad], axis=0)


GRAD_SHAPES = tuple(jax.ShapeDtypeStruct(s, F32) for s in SHAPES[1:])


def short_call(which, label, length, weight, tokens, upstream, mod, weights, prev):
    count, n, _ = tokens.shape
    block = pl.BlockSpec((1, n, D), lambda i: (which, 0, 0))

    def whole(shape):
        return pl.BlockSpec(shape, lambda i: (0,) * len(shape))

    in_specs = [SMEM] * 3 + [block, block, whole((8, 6 * D))] + [whole(w.shape) for w in weights]
    args = [label, length, weight, tokens, upstream, mod, *weights]
    aliases = {}
    if prev is not None:
        in_specs += [ANY, ANY]
        aliases = {len(args): 0, len(args) + 1: 1}
        args += list(prev)
    return pl.pallas_call(
        functools.partial(short_kernel, 0 if prev is None else 1),
        name="short" + str(which),
        grid=(1,),
        out_shape=(
            jax.ShapeDtypeStruct(tokens.shape, BF16),
            jax.ShapeDtypeStruct(tokens.shape, F32),
            *GRAD_SHAPES,
            jax.ShapeDtypeStruct((8, D), F32),
        ),
        in_specs=in_specs,
        out_specs=(block, block, *[whole(s.shape) for s in GRAD_SHAPES], whole((8, D))),
        scratch_shapes=[
            pltpu.VMEM((n, 3 * D), BF16),
            pltpu.VMEM((HEADS, n, n), F32),
            pltpu.VMEM((n, D), F32),
            pltpu.VMEM((n, D), F32),
            pltpu.VMEM((n, D), F32),
            pltpu.VMEM((n, D), BF16),
            pltpu.VMEM((n, 3 * D), BF16),
            pltpu.VMEM((2, n, n), BF16),
            pltpu.VMEM((n, D), F32),
        ],
        input_output_aliases=aliases,
        cost_estimate=pl.CostEstimate(
            flops=8 * 10**9, bytes_accessed=2 * 10**7, transcendentals=2 * 10**6
        ),
    )(*args)


def long_in_kernel(label, x_ref, mod_ref, w_qkv, q_ref, kv_ref):
    _, _, _, qkv = project(x_ref[0].astype(F32), mods_of(label, mod_ref), w_qkv)
    q_ref[...] = qkv[:, :D]
    kv_ref[...] = qkv[:, D:]


def long_in(label, tokens, mod, w_qkv):
    n = tokens.shape[1]
    return pl.pallas_call(
        long_in_kernel,
        name="long_in",
        out_shape=(
            jax.ShapeDtypeStruct((n, D), BF16),
            jax.ShapeDtypeStruct((n, 2 * D), BF16),
        ),
        in_specs=[SMEM] + [VMEM] * 3,
        out_specs=(VMEM,) * 2,
        cost_estimate=pl.CostEstimate(flops=10**8, bytes_accessed=10**6, transcendentals=0),
    )(label, tokens, mod, w_qkv)


def long_mid_kernel(
    label, start_len, weight, x_ref, up_ref, mod_ref, q_ref, kv, bias_ref,
    w_out, w_up, w_down,
    out_ref, dx1_ref, do_ref, stat_ref, row_ref, dw_out, dw_up, dw_down, dmod_ref,
    o_f, mo, dm,
):
    n = x_ref.shape[1]
    mod = mods_of(label, mod_ref)
    bias = bias_ref[...]
    lane = lax.broadcasted_iota(jnp.int32, (1, 128), 1)
    stat_ref[...] = jnp.zeros_like(stat_ref)

    @pl.loop(0, PAIRS)
    def _(hp):
        q_cols = pl.ds(pl.multiple_of(hp * 128, 128), 128)
        k2 = kv[:, q_cols]
        v2 = kv[:, pl.ds(pl.multiple_of(D + hp * 128, 128), 128)]

        rows = slice(0, n)
        q2 = q_ref[rows, q_cols]
        o2 = None
        for j in range(2):
            s = dot_nt(q2, only_head(k2, j)) * score_scale + bias
            top = jnp.max(s, axis=-1, keepdims=True)
            e = jnp.exp(s - top)
            total = jnp.sum(e, axis=-1, keepdims=True)
            part = dot_nn(e.astype(BF16), only_head(v2, j)) * (1.0 / total)
            o2 = part if o2 is None else o2 + part
            lse = top + jnp.log(total)
            stat_ref[rows, :] += jnp.where(lane == hp * 2 + j, lse, 0.0)
        o_f[rows, q_cols] = o2

    row = start_len[0] + lax.broadcasted_iota(jnp.int32, (n, 1), 0)
    g = cotangent(up_ref[0], weight[0], row < start_len[1])
    o_low = o_f[...].astype(BF16)
    out, dx1, d_o, dm_parts = mlp_both(
        x_ref[0].astype(F32), o_low, g, mod, w_out, w_up, w_down,
        dw_out, dw_up, dw_down, mo, dm,
    )
    out_ref[0] = out
    dx1_ref[...] = dx1
    do_ref[...] = d_o
    stat = stat_ref[...]
    for hp in range(PAIRS):
        cols = slice(hp * 128, (hp + 1) * 128)
        prod = d_o[:, cols].astype(F32) * o_f[:, cols]
        for j in range(2):
            delta = jnp.sum(only_head(prod, j), axis=-1, keepdims=True)
            stat = stat + jnp.where(lane == 8 + hp * 2 + j, delta, 0.0)
    stat_ref[...] = stat
    row_ref[...] = stat.T[:16, :]
    pad = jnp.zeros((4, D), F32)
    dmod_ref[...] = jnp.concatenate([*dm_parts, pad], axis=0)


def long_mid(label, start_len, weight, tokens, *args):
    n = tokens.shape[1]
    return pl.pallas_call(
        long_mid_kernel,
        name="long_mid",
        out_shape=(
            jax.ShapeDtypeStruct(tokens.shape, BF16),
            jax.ShapeDtypeStruct((n, D), F32),
            jax.ShapeDtypeStruct((n, D), BF16),
            jax.ShapeDtypeStruct((n, 128), F32),
            jax.ShapeDtypeStruct((16, n), F32),
            *GRAD_SHAPES[1:],
            jax.ShapeDtypeStruct((8, D), F32),
        ),
        in_specs=[SMEM] * 3 + [VMEM] * 9,
        out_specs=(VMEM,) * 9,
        scratch_shapes=[pltpu.VMEM((n, D), F32)] * 3,
        cost_estimate=pl.CostEstimate(
            flops=4 * 10**9, bytes_accessed=2 * 10**7, transcendentals=2 * 10**6
        ),
    )(label, start_len, weight, tokens, *args)


def long_back_kernel(
    label, start_len, x_ref, mod_ref, q_ref, kv_own, kv, bias_ref, do_ref, stat_ref,
    q_all, do_all, rows_all, dx1_ref, w_qkv,
    grad_ref, dw_qkv, dmod_ref, dqkv, dk_s, dv_s,
):
    n = x_ref.shape[1]
    total = kv.shape[0]
    mod = mods_of(label, mod_ref)
    bias = bias_ref[...]
    lane = lax.broadcasted_iota(jnp.int32, (1, 128), 1)

    @pl.loop(0, PAIRS)
    def _(hp):
        q_cols = pl.ds(pl.multiple_of(hp * 128, 128), 128)
        k_cols = pl.ds(pl.multiple_of(D + hp * 128, 128), 128)
        v_cols = pl.ds(pl.multiple_of(2 * D + hp * 128, 128), 128)
        k2 = kv[:, q_cols]
        v2 = kv[:, k_cols]

        rows = slice(0, n)
        q2 = q_ref[rows, q_cols]
        do2 = do_ref[rows, q_cols]
        stat = stat_ref[rows, :]
        dq2 = None
        for j in range(2):
            kz = only_head(k2, j)
            h = hp * 2 + j
            lse = jnp.sum(jnp.where(lane == h, stat, 0.0), axis=-1, keepdims=True)
            delta = jnp.sum(jnp.where(lane == 8 + h, stat, 0.0), axis=-1, keepdims=True)
            p = jnp.exp(dot_nt(q2, kz) * score_scale + bias - lse)
            dp = dot_nt(do2, only_head(v2, j))
            ds = (p * (dp - delta)).astype(BF16)
            part = dot_nn(ds, kz)
            dq2 = part if dq2 is None else dq2 + part
        dqkv[rows, q_cols] = (dq2 * score_scale).astype(BF16)

        k_own = kv_own[:, q_cols]
        v_own = kv_own[:, k_cols]
        dk_s[...] = jnp.zeros_like(dk_s)
        dv_s[...] = jnp.zeros_like(dv_s)

        @pl.loop(0, total // n)
        def _(qc):
            rows = pl.ds(pl.multiple_of(qc * n, n), n)
            q2 = q_all[rows, q_cols]
            do2 = do_all[rows, q_cols]
            for j in range(2):
                h = hp * 2 + j
                lse = rows_all[qc, pl.ds(h, 1), :]
                delta = rows_all[qc, pl.ds(8 + h, 1), :]
                p = jnp.exp(dot_nt(only_head(k_own, j), q2) * score_scale - lse)
                dp = dot_nt(only_head(v_own, j), do2)
                ds = (p * (dp - delta)).astype(BF16)
                dv_s[j] += dot_nn(p.astype(BF16), do2)
                dk_s[j] += dot_nn(ds, q2)

        row = start_len[0] + lax.broadcasted_iota(jnp.int32, (n, 1), 0)
        ok = row < start_len[1]
        dk2 = jnp.where(head_mask(0), dk_s[0], dk_s[1])
        dv2 = jnp.where(head_mask(0), dv_s[0], dv_s[1])
        dqkv[:, k_cols] = jnp.where(ok, dk2 * score_scale, 0.0).astype(BF16)
        dqkv[:, v_cols] = jnp.where(ok, dv2, 0.0).astype(BF16)

    hat, scale = norm_parts(x_ref[0].astype(F32))
    a = (hat * (1.0 + mod[1]) + mod[0]).astype(BF16)
    grad, d_shift1, d_scale1 = project_back(
        dqkv[...], dx1_ref[...], hat, scale, a, mod, w_qkv, dw_qkv
    )
    grad_ref[0] = grad
    pad = jnp.zeros((6, D), F32)
    dmod_ref[...] = jnp.concatenate([d_shift1, d_scale1, pad], axis=0)


def long_back(label, start_len, tokens, *args):
    n = tokens.shape[1]
    return pl.pallas_call(
        long_back_kernel,
        name="long_back",
        out_shape=(
            jax.ShapeDtypeStruct(tokens.shape, F32),
            GRAD_SHAPES[0],
            jax.ShapeDtypeStruct((8, D), F32),
        ),
        in_specs=[SMEM] * 2 + [VMEM] * 13,
        out_specs=(VMEM,) * 3,
        scratch_shapes=[
            pltpu.VMEM((n, 3 * D), BF16),
            pltpu.VMEM((2, n, 128), F32),
            pltpu.VMEM((2, n, 128), F32),
        ],
        cost_estimate=pl.CostEstimate(
            flops=4 * 10**9, bytes_accessed=10**7, transcendentals=4 * 10**6
        ),
    )(label, start_len, tokens, *args)


def pack_kernel(nq, sizes, idx, labels, cond_t, dmod_mid, dmod_back, dmod_s0, dmod_s1, *refs):
    grads = refs[:12]
    outs = refs[12 : 12 + len(sizes)]
    buf, sems = refs[12 + len(sizes) :]
    part = TILE // nq
    buf[...] = jnp.zeros_like(buf)
    d_long = jnp.concatenate([dmod_back[:2, :], dmod_mid[:4, :]], axis=0)
    per_seq = (d_long, dmod_s0[:6, :], dmod_s1[:6, :])
    by_label = []
    for v in range(3):
        acc = None
        for s in range(3):
            term = jnp.where(labels[s] == v, per_seq[s], 0.0)
            acc = term if acc is None else acc + term
        by_label.append(acc)
    first = 0

    @pl.loop(0, D // TILE)
    def _(r):
        rows = pl.ds(pl.multiple_of(r * TILE, TILE), TILE)
        col = [cond_t[rows, v : v + 1] for v in range(3)]
        for c in range(6 * D // TILE):
            i, off = divmod(c, D // TILE)
            lanes = slice(off * TILE, (off + 1) * TILE)
            tile = None
            for v in range(3):
                term = col[v] * by_label[v][i : i + 1, lanes]
                tile = term if tile is None else tile + term
            tile = tile.astype(BF16)
            for q in range(nq):
                at = idx[(r * (6 * D // TILE) + c) * nq + q]
                buf[at] = tile[q * part : (q + 1) * part]

    first += SHAPES[0][0] * SHAPES[0][1] // TILE**2
    at = 0
    for (rows, cols), many in zip(SHAPES[1:], (3, 3, 3, 3)):
        nr, nc = rows // TILE, cols // TILE
        terms = grads[at : at + many]
        at += many

        @pl.loop(0, nr)
        def _(r, first=first, nc=nc, terms=terms):
            for c in range(nc):
                for q in range(nq):
                    row = pl.multiple_of(r * TILE + q * part, part)
                    lanes = slice(c * TILE, (c + 1) * TILE)
                    v = terms[0][pl.ds(row, part), lanes]
                    for other in terms[1:]:
                        v = v + other[pl.ds(row, part), lanes]
                    buf[idx[(first + r * nc + c) * nq + q]] = v.astype(BF16)

        first += nr * nc
    copies = []
    base = 0
    for i, size in enumerate(sizes):
        cp = pltpu.make_async_copy(buf.at[pl.ds(base, size)], outs[i], sems.at[i])
        cp.start()
        copies.append(cp)
        base += size
    for cp in copies:
        cp.wait()


def pack(nq, sizes, idx, labels, cond_t, dmods, grads):
    part = TILE // nq
    return pl.pallas_call(
        functools.partial(pack_kernel, nq, sizes),
        name="pack",
        out_shape=tuple(jax.ShapeDtypeStruct((s, part, TILE), BF16) for s in sizes),
        in_specs=[SMEM, SMEM] + [VMEM] * 17,
        out_specs=(ANY,) * len(sizes),
        scratch_shapes=[
            pltpu.VMEM((sum(sizes), part, TILE), BF16),
            pltpu.SemaphoreType.DMA((len(sizes),)),
        ],
        cost_estimate=pl.CostEstimate(flops=10**7, bytes_accessed=3 * 10**7, transcendentals=0),
    )(idx, labels, cond_t, *dmods, *grads)


def halves(v):
    high = v.astype(BF16)
    return high, (v - high.astype(F32)).astype(BF16)


def dot3(dot, a, b):
    return dot(a[0], b[0]) + (dot(a[0], b[1]) + dot(a[1], b[0]))


def soap_kernel(nq, order, g_ref, left, right, first, second, master, gs, fn, sn, wn):
    part = TILE // nq
    for i in range(master.shape[0]):
        g = jnp.concatenate([g_ref[order[q], i] for q in range(nq)], axis=0).astype(F32)
        gs[i] = g
        lo = halves(left[i])
        ro = halves(right[i])
        rot = dot3(dot_nn, halves(dot3(dot_tn, lo, halves(g))), ro)
        f = beta_first * first[i] + (1.0 - beta_first) * rot
        s = beta_second * second[i] + (1.0 - beta_second) * rot * rot
        fn[i] = f
        sn[i] = s
        step = (
            f
            / (1.0 - beta_first**STEP)
            / (jnp.sqrt(s / (1.0 - beta_second**STEP)) + adam_eps)
        )
        back = dot3(dot_nt, halves(dot3(dot_nn, lo, halves(step))), ro)
        w = master[i]
        mean = jnp.mean(jnp.mean(w * w, axis=1, keepdims=True), axis=0, keepdims=True)
        spread = jnp.sqrt(mean + 1e-06)
        wn[i] = w - base_rate * spread * (back + decay_rate * w)


def soap(nq, order, g, left, right, first, second, master):
    slots = master.shape[0]
    block = max(k for k in range(1, 12) if slots % k == 0)
    part = TILE // nq
    spec = pl.BlockSpec((block, TILE, TILE), lambda i: (i, 0, 0))
    g_spec = pl.BlockSpec((nq, block, part, TILE), lambda i: (0, i, 0, 0))
    shape = jax.ShapeDtypeStruct(master.shape, F32)
    return pl.pallas_call(
        functools.partial(soap_kernel, nq),
        name="soap",
        grid=(slots // block,),
        out_shape=(shape,) * 4,
        in_specs=[SMEM, g_spec] + [spec] * 5,
        out_specs=(spec,) * 4,
        cost_estimate=pl.CostEstimate(flops=10**9, bytes_accessed=10**7, transcendentals=10**6),
    )(order, g, left, right, first, second, master)


class Grid:
    def __init__(self, n_dp, n_seq):
        self.direct = n_dp == 8 and n_seq == 4
        self.n = {"z": n_dp // 2, "y": 2, "x": n_seq // 2, "c": 2}
        self.n_dp = n_dp
        self.n_seq = n_seq
        self.nq = n_seq if self.direct else 1

    def here(self):
        dp = lax.axis_index("dp")
        seq = lax.axis_index("seq")
        return {"z": dp // 2, "y": dp % 2, "x": seq // 2, "c": seq % 2}

    def shift(self, v, names):
        pairs = []
        for dp in range(self.n_dp):
            for seq in range(self.n_seq):
                at = {"z": dp // 2, "y": dp % 2, "x": seq // 2, "c": seq % 2}
                to = {k: (v + (k in names)) % self.n[k] for k, v in at.items()}
                pairs.append(((dp, seq), (to["z"] * 2 + to["y"], to["x"] * 2 + to["c"])))
        if not set(names) & set("zy"):
            axis, flat = "seq", {(a[1], b[1]) for a, b in pairs}
        elif not set(names) & set("xc"):
            axis, flat = "dp", {(a[0], b[0]) for a, b in pairs}
        else:
            axis = ("dp", "seq")
            flat = {tuple(d * self.n_seq + q for d, q in pair) for pair in pairs}
        return lax.ppermute(v, axis, sorted(flat))

    def over_seq(self, v):
        if not self.direct:
            return lax.all_gather(v, "seq", axis=0, tiled=True)
        return jnp.concatenate([v] + [self.shift(v, n) for n in ("x", "c", "xc")], axis=0)

    def seq_blocks(self):
        if not self.direct:
            return jnp.arange(self.n_seq, dtype=jnp.int32)
        at = self.here()
        return jnp.stack(
            [((at["x"] - rx) % 2) * 2 + (at["c"] - rc) % 2 for rc in range(2) for rx in range(2)]
        )

    def table(self, tile_slot, slots, sign):
        if not self.direct:
            return tile_slot, (self.n_dp * slots,)
        at = self.here()
        owner = tile_slot // slots
        rz = (sign * (at["z"] - owner // 2)) % self.n["z"]
        ry = (at["y"] - owner % 2) % 2
        parts = []
        for q in range(self.nq):
            rx = (at["x"] - q // 2) % 2
            rc = (at["c"] - q % 2) % 2
            parts.append((((rz * 2 + rc) * 2 + rx) * 2 + ry) * slots + tile_slot % slots)
        return jnp.stack(parts, axis=1).reshape(-1), (4 * slots,) * (2 * self.n["z"])

    def gather_slots(self, low, side):
        if not self.direct:
            return [lax.all_gather(low, "dp", axis=0, tiled=True)], side
        part = TILE // self.nq
        piece = lax.dynamic_slice_in_dim(low, lax.axis_index("seq") * part, part, 1)
        out = []
        for r in range(self.n["z"]):
            if r:
                if r == self.n["z"] - 1:
                    piece, side = lax.optimization_barrier((piece, side))
                piece = self.shift(piece, "z")
            near = [piece] + [self.shift(piece, n) for n in ("y", "x", "xy")]
            near = jnp.concatenate(near, axis=0)
            out += [near, self.shift(near, "c")]
        return out, side

    def reduce_slots(self, parts):
        if not self.direct:
            total = lax.psum_scatter(
                parts[0].astype(F32), "dp", scatter_dimension=0, tiled=True
            )
            return lax.psum(total, "seq")[None]
        acc = None
        for r in range(self.n["z"] - 1, -1, -1):
            both = parts[2 * r].astype(F32) + self.shift(parts[2 * r + 1], "c").astype(F32)
            k = both.shape[0] // 4
            total = both[:k]
            for i, names in enumerate(("y", "x", "xy")):
                block = both[(i + 1) * k : (i + 2) * k].astype(BF16)
                total = total + self.shift(block, names).astype(F32)
            if acc is not None:
                total = total + self.shift(acc, "z").astype(F32)
            acc = total.astype(BF16)
        return self.over_seq(acc[None])

    def part_order(self):
        if not self.direct:
            return jnp.zeros((1,), jnp.int32)
        at = self.here()
        return jnp.stack(
            [((at["c"] - q % 2) % 2) * 2 + (at["x"] - q // 2) % 2 for q in range(self.nq)]
        )


def local(
    tokens_long,
    tokens_short,
    upstream_long,
    upstream_short,
    interval_table,
    labels_long,
    labels_short,
    lengths_long,
    lengths_short,
    tile_slot,
    master_slots,
    basis_left,
    basis_right,
    first_moment,
    second_moment,
):
    grid = Grid(lax.axis_size("dp"), lax.axis_size("seq"))
    slots = master_slots.shape[0]
    dp_index = lax.axis_index("dp")
    seq_index = lax.axis_index("seq")
    rows = tokens_long.shape[1]
    short_count = tokens_short.shape[0]

    idx_in, _ = grid.table(tile_slot, slots, 1)
    idx_out, sizes = grid.table(tile_slot, slots, -1)

    label_all = jnp.concatenate([labels_long, labels_short])
    kinds = jnp.arange(3, dtype=jnp.int32)
    counts = jnp.sum((label_all[:, None] == kinds[None, :]).astype(F32), axis=0)
    first_short = (dp_index * grid.n_seq + seq_index) * short_count
    own = jnp.concatenate(
        [
            lax.dynamic_slice_in_dim(labels_long, dp_index, 1),
            lax.dynamic_slice_in_dim(labels_short, first_short, short_count),
        ]
    )
    own_length = lax.dynamic_slice_in_dim(lengths_long, dp_index, 1)
    short_lengths = lax.dynamic_slice_in_dim(lengths_short, first_short, short_count)
    one_hot = (own[:, None] == kinds[None, :]).astype(F32)
    seq_weight = float(label_all.shape[0]) / (3.0 * jnp.sum(one_hot * counts[None, :], axis=1))

    cond = jax.nn.silu(interval_table).astype(BF16)
    cond_pad = jnp.pad(cond, ((0, 5), (0, 0)))
    cond_t = jnp.pad(cond.astype(F32).T, ((0, 0), (0, 5)))
    long_start = seq_index * rows
    start_len = jnp.concatenate([long_start[None].astype(jnp.int32), own_length])
    blocks = grid.seq_blocks()
    pos = (blocks[:, None] * rows + jnp.arange(rows, dtype=jnp.int32)[None, :]).reshape(1, -1)
    bias = jnp.where(pos < own_length[0], 0.0, masked_score).astype(F32)
    order = grid.part_order()
    labels = [own[i : i + 1] for i in range(1 + short_count)]
    lens = [short_lengths[i : i + 1] for i in range(short_count)]
    share = [seq_weight[i : i + 1] for i in range(1 + short_count)]
    side = (idx_in, idx_out, own, labels, lens, share, cond_pad, cond_t, start_len, bias, order)
    srcs, side = grid.gather_slots(master_slots.astype(BF16), side)
    idx_in, idx_out, own, labels, lens, share, cond_pad, cond_t, start_len, bias, order = side
    *weights, mod_table = unpack(grid.nq, srcs, idx_in, cond_pad)
    w_qkv, w_out, w_up, w_down = weights

    def short(i, prev):
        return short_call(
            i, labels[1 + i], lens[i], share[1 + i], tokens_short,
            upstream_short, mod_table, weights, prev,
        )

    q, kv_own = long_in(labels[0], tokens_long, mod_table, w_qkv)
    kv = grid.over_seq(kv_own)
    res0 = short(0, None)
    kv, dmod_s0 = lax.optimization_barrier((kv, res0[6]))
    (
        out_long, dx1, d_o, stat, stat_rows, dw_out_l, dw_up_l, dw_down_l, dmod_mid,
    ) = long_mid(
        labels[0], start_len, share[0], tokens_long, upstream_long, mod_table, q, kv,
        bias, w_out, w_up, w_down,
    )
    q_all = grid.over_seq(q)
    do_all = grid.over_seq(d_o)
    rows_all = grid.over_seq(stat_rows[None])
    prev0, prev1, dmod_mid = lax.optimization_barrier((res0[0], res0[1], dmod_mid))
    res1 = short(1, (prev0, prev1))
    q_all, do_all, rows_all, dmod_s1 = lax.optimization_barrier(
        (q_all, do_all, rows_all, res1[6])
    )
    grad_long, dw_qkv_l, dmod_back = long_back(
        labels[0], start_len, tokens_long, mod_table, q, kv_own, kv, bias, d_o, stat,
        q_all, do_all, rows_all, dx1, w_qkv,
    )
    out_short, grad_short = res1[:2]
    terms = []
    for i, extra in enumerate((dw_qkv_l, dw_out_l, dw_up_l, dw_down_l)):
        terms += [res0[2 + i], res1[2 + i], extra]
    parts = pack(
        grid.nq, sizes, idx_out, own, cond_t, (dmod_mid, dmod_back, dmod_s0, dmod_s1), terms
    )
    g = grid.reduce_slots(parts)
    grad_slots, first_new, second_new, weight_new = soap(
        grid.nq, order, g, basis_left, basis_right, first_moment,
        second_moment, master_slots,
    )
    return (
        out_long, out_short, grad_long, grad_short,
        grad_slots, first_new, second_new, weight_new,
    )


def solution(mesh):
    rows = P(("dp", "seq"), None, None)
    cols = P("dp", "seq", None)
    slots = P("dp", None, None)
    return jax.shard_map(
        local,
        mesh=mesh,
        in_specs=(cols, rows, cols, rows) + (P(),) * 6 + (slots,) * 5,
        out_specs=(cols, rows, cols, rows) + (slots,) * 4,
        check_vma=False,
    )
```

```python
import functools

import jax
import jax.numpy as jnp
from jax import lax
from jax.experimental import pallas as pl
from jax.experimental.pallas import tpu as pltpu
from jax.sharding import PartitionSpec as P

D = 384
HEADS = 6
HD = 64
FF = 1536
STEP = 10
TILE = 128
PAIRS = HEADS // 2
SHAPES = ((D, 6 * D), (D, 3 * D), (D, D), (D, FF), (FF, D))

F32 = jnp.float32
BF16 = jnp.bfloat16
beta_first = 0.9
beta_second = 0.95
adam_eps = 1e-08
base_rate = 0.3
decay_rate = 0.01
norm_eps = 1e-06
masked_score = -1e30
score_scale = HD ** (-0.5)
FF_BLOCK = 768


VMEM = pl.BlockSpec(memory_space=pltpu.VMEM)
SMEM = pl.BlockSpec(memory_space=pltpu.SMEM)
ANY = pl.BlockSpec(memory_space=pl.ANY)
PARAMS = pltpu.CompilerParams(vmem_limit_bytes=34 * 2**20)


def dot_nn(a, b):
    return lax.dot_general(a, b, (((1,), (0,)), ((), ())), preferred_element_type=F32)


def dot_nt(a, b):
    return lax.dot_general(a, b, (((1,), (1,)), ((), ())), preferred_element_type=F32)


def dot_tn(a, b):
    return lax.dot_general(a, b, (((0,), (0,)), ((), ())), preferred_element_type=F32)


def norm_parts(v):
    centered = v - jnp.mean(v, axis=-1, keepdims=True)
    scale = lax.rsqrt(jnp.mean(centered * centered, axis=-1, keepdims=True) + norm_eps)
    return centered * scale, scale


def norm_back(dy, hat, scale):
    return scale * (
        dy
        - jnp.mean(dy, axis=-1, keepdims=True)
        - hat * jnp.mean(dy * hat, axis=-1, keepdims=True)
    )


def col_sum(v):
    return jnp.sum(v, axis=0, keepdims=True)


def head_mask(j):
    lane = lax.broadcasted_iota(jnp.int32, (1, 2 * HD), 1)
    return (lane >= j * HD) & (lane < (j + 1) * HD)


def only_head(v, j):
    return jnp.where(head_mask(j), v, jnp.zeros_like(v))


def gelu_both(u):
    k0 = 0.7978845608028654
    sq = u * u
    t = jnp.tanh(u * (k0 + (k0 * 0.044715) * sq))
    half = 0.5 * (1.0 + t)
    slope = half + (0.5 * u) * (1.0 - t * t) * (k0 + (3.0 * k0 * 0.044715) * sq)
    return u * half, slope


def own_long(labels, lengths):
    at = lax.axis_index("dp")
    return labels[at], lengths[at]


def own_short(which, count, labels, lengths):
    at = (lax.axis_index("dp") * lax.axis_size("seq") + lax.axis_index("seq")) * count + which
    return labels[at], lengths[at]


def share_of(label, *tables):
    total = 0
    many = jnp.int32(0)
    for table in tables:
        size = table.shape[0]
        total += size
        many = lax.fori_loop(
            0, size, lambda i, n, t=table: n + (t[i] == label).astype(jnp.int32), many
        )
    return float(total) / (3.0 * many.astype(F32))


def key_bias(direct, rows, total, length):
    seq = lax.axis_index("seq")
    lane = lax.broadcasted_iota(jnp.int32, (1, rows), 1)
    out = []
    for i in range(total // rows):
        block = (seq ^ ((i % 2) * 2 + i // 2)) if direct else i
        out.append(jnp.where(block * rows + lane < length, 0.0, masked_score))
    return jnp.concatenate(out, axis=1)


def unpack_kernel(nq, slots, sizes, base, table, *refs):
    srcs = refs[: len(sizes)]
    w_qkv, w_out, w_up, w_down, mod, buf, w_ada, sems = refs[len(sizes) :]
    part = TILE // nq
    copies = []
    start = 0
    for i, size in enumerate(sizes):
        cp = pltpu.make_async_copy(srcs[i], buf.at[pl.ds(start, size)], sems.at[i])
        cp.start()
        copies.append(cp)
        start += size
    seq = lax.axis_index("seq")
    offset = [0]
    if nq > 1:
        turn = [seq ^ q for q in range(nq)]
        offset = [((r % 2) * 4 + (r // 2) * 2) * slots for r in turn]
    for cp in copies:
        cp.wait()
    first = 0
    for (rows, cols), dst in zip(SHAPES, (w_ada, w_qkv, w_out, w_up, w_down)):
        nr, nc = rows // TILE, cols // TILE

        @pl.loop(0, nr)
        def _(r, first=first, nc=nc, dst=dst):
            for c in range(nc):
                at = base[first + r * nc + c]
                for q in range(nq):
                    row = pl.multiple_of(r * TILE + q * part, part)
                    dst[pl.ds(row, part), c * TILE : (c + 1) * TILE] = buf[at + offset[q]]

        first += nr * nc
    v = table[...]
    cond = v * jax.nn.sigmoid(v)
    cond = jnp.concatenate([cond, jnp.zeros((5, D), F32)], axis=0).astype(BF16)
    mod[...] = dot_nn(cond, w_ada[...])


def unpack(nq, slots, srcs, base, table):
    sizes = tuple(s.shape[0] for s in srcs)
    part = TILE // nq
    return pl.pallas_call(
        functools.partial(unpack_kernel, nq, slots, sizes),
        name="unpack",
        out_shape=tuple(jax.ShapeDtypeStruct(s, BF16) for s in SHAPES[1:])
        + (jax.ShapeDtypeStruct((8, 6 * D), F32),),
        in_specs=[SMEM, VMEM] + [ANY] * len(srcs),
        out_specs=(VMEM,) * 5,
        scratch_shapes=[
            pltpu.VMEM((sum(sizes), part, TILE), BF16),
            pltpu.VMEM(SHAPES[0], BF16),
            pltpu.SemaphoreType.DMA((len(sizes),)),
        ],
        compiler_params=PARAMS,
        cost_estimate=pl.CostEstimate(flops=10**7, bytes_accessed=10**7, transcendentals=0),
    )(base, table, *srcs)


def mods_of(label, mod):
    row = mod[pl.ds(label, 1), :]
    return [row[:, i * D : (i + 1) * D] for i in range(6)]


def project(x, mod, w_qkv):
    hat, scale = norm_parts(x)
    a = (hat * (1.0 + mod[1]) + mod[0]).astype(BF16)
    return hat, scale, a, dot_nn(a, w_qkv[...]).astype(BF16)


def mlp_both(x, o_low, g, mod, w_out, w_up, w_down, dw_out, dw_up, dw_down, mo, dm):
    att = dot_nn(o_low, w_out[...])
    x1 = x + mod[2] * att
    hat, scale = norm_parts(x1)
    m = (hat * (1.0 + mod[4]) + mod[3]).astype(BF16)
    d_mo = (mod[5] * g).astype(BF16)
    mo[...] = jnp.zeros_like(mo)
    dm[...] = jnp.zeros_like(dm)

    @pl.loop(0, FF // FF_BLOCK)
    def _(b):
        cols = pl.ds(pl.multiple_of(b * FF_BLOCK, FF_BLOCK), FF_BLOCK)
        u = dot_nn(m, w_up[:, cols])
        d_r = dot_nt(d_mo, w_down[cols, :])
        act, slope = gelu_both(u)
        r = act.astype(BF16)
        du = (d_r * slope).astype(BF16)
        mo[...] += dot_nn(r, w_down[cols, :])
        dm[...] += dot_nt(du, w_up[:, cols])
        dw_up[:, cols] = dot_tn(m, du)
        dw_down[cols, :] = dot_tn(r, d_mo)

    mo_v = mo[...]
    out = (x1 + mod[5] * mo_v).astype(BF16)
    d_gate2 = col_sum(mo_v * g)
    dm_v = dm[...]
    d_shift2 = col_sum(dm_v)
    d_scale2 = col_sum(dm_v * hat)
    dx1 = g + norm_back(dm_v * (1.0 + mod[4]), hat, scale)
    d_att = (mod[2] * dx1).astype(BF16)
    d_gate1 = col_sum(att * dx1)
    dw_out[...] = dot_tn(o_low, d_att)
    d_o = dot_nt(d_att, w_out[...]).astype(BF16)
    return out, dx1, d_o, (d_gate1, d_shift2, d_scale2, d_gate2)


def project_back(dqkv, dx1, hat, scale, a, mod, w_qkv, dw_qkv):
    dw_qkv[...] = dot_tn(a, dqkv)
    d_a = dot_nt(dqkv, w_qkv[...])
    d_shift = col_sum(d_a)
    d_scale = col_sum(d_a * hat)
    return dx1 + norm_back(d_a * (1.0 + mod[1]), hat, scale), d_shift, d_scale


def cotangent(up, weight, rows_ok):
    return jnp.where(rows_ok, up.astype(F32) * weight, 0.0)


def short_kernel(
    which, labels_l, labels_s, lengths_s, x_all, up_all, mod_ref,
    w_qkv, w_out, w_up, w_down, *refs,
):
    if which:
        refs = refs[2:]
    (
        out_all, grad_all, dw_qkv, dw_out, dw_up, dw_down, dmod_ref,
        qkv, probs, o_f, mo, dm, d_o, dqkv, ds_s, x1_s, out_s, sems,
    ) = refs
    count, n, _ = x_all.shape
    x_ref = x_all.at[which]
    up_ref = up_all.at[which]
    label, length = own_short(which, count, labels_s, lengths_s)
    weight = share_of(label, labels_l, labels_s)
    mod = mods_of(label, mod_ref)
    x = x_ref[...].astype(F32)
    hat, scale, a, qkv_v = project(x, mod, w_qkv)
    qkv[...] = qkv_v
    key = lax.broadcasted_iota(jnp.int32, (1, n), 1)
    bias = jnp.where(key < length, 0.0, masked_score)

    @pl.loop(0, PAIRS)
    def _(hp):
        q_cols = pl.ds(pl.multiple_of(hp * 128, 128), 128)
        k2 = qkv[:, pl.ds(pl.multiple_of(D + hp * 128, 128), 128)]
        v2 = qkv[:, pl.ds(pl.multiple_of(2 * D + hp * 128, 128), 128)]

        rows = slice(0, n)
        q2 = qkv[rows, q_cols]
        o2 = None
        for j in range(2):
            s = dot_nt(q2, only_head(k2, j)) * score_scale + bias
            e = jnp.exp(s - jnp.max(s, axis=-1, keepdims=True))
            p = e * (1.0 / jnp.sum(e, axis=-1, keepdims=True))
            probs[hp * 2 + j, rows, :] = p
            part = dot_nn(p.astype(BF16), only_head(v2, j))
            o2 = part if o2 is None else o2 + part
        o_f[rows, q_cols] = o2

    row = lax.broadcasted_iota(jnp.int32, (n, 1), 0)
    g = cotangent(up_ref[...], weight, row < length)
    o_low = o_f[...].astype(BF16)
    out, dx1, d_o_v, dm_parts = mlp_both(
        x, o_low, g, mod, w_out, w_up, w_down, dw_out, dw_up, dw_down, mo, dm
    )
    out_s[...] = out
    save_out = pltpu.make_async_copy(out_s, out_all.at[which], sems.at[0])
    save_out.start()
    x1_s[...] = dx1
    d_o[...] = d_o_v

    @pl.loop(0, PAIRS)
    def _(hp):
        q_cols = pl.ds(pl.multiple_of(hp * 128, 128), 128)
        k_cols = pl.ds(pl.multiple_of(D + hp * 128, 128), 128)
        v_cols = pl.ds(pl.multiple_of(2 * D + hp * 128, 128), 128)
        k2 = qkv[:, k_cols]
        v2 = qkv[:, v_cols]

        rows = slice(0, n)
        do2 = d_o[rows, q_cols]
        prod = do2.astype(F32) * o_f[rows, q_cols]
        dq2 = None
        for j in range(2):
            dp = dot_nt(do2, only_head(v2, j))
            delta = jnp.sum(only_head(prod, j), axis=-1, keepdims=True)
            ds = (probs[hp * 2 + j, rows, :] * (dp - delta)).astype(BF16)
            ds_s[j, rows, :] = ds
            part = dot_nn(ds, only_head(k2, j))
            dq2 = part if dq2 is None else dq2 + part
        dqkv[rows, q_cols] = (dq2 * score_scale).astype(BF16)

        q2 = qkv[:, q_cols]
        do2 = d_o[:, q_cols]
        dk2 = jnp.where(head_mask(0), dot_tn(ds_s[0], q2), dot_tn(ds_s[1], q2))
        dqkv[:, k_cols] = (dk2 * score_scale).astype(BF16)
        p0 = probs[hp * 2].astype(BF16)
        p1 = probs[hp * 2 + 1].astype(BF16)
        dv2 = jnp.where(head_mask(0), dot_tn(p0, do2), dot_tn(p1, do2))
        dqkv[:, v_cols] = dv2.astype(BF16)

    x = x_ref[...].astype(F32)
    hat, scale = norm_parts(x)
    a = (hat * (1.0 + mod[1]) + mod[0]).astype(BF16)
    grad, d_shift1, d_scale1 = project_back(
        dqkv[...], x1_s[...], hat, scale, a, mod, w_qkv, dw_qkv
    )
    x1_s[...] = grad
    save_grad = pltpu.make_async_copy(x1_s, grad_all.at[which], sems.at[1])
    save_grad.start()
    pad = jnp.zeros((2, D), F32)
    dmod_ref[...] = jnp.concatenate([d_shift1, d_scale1, *dm_parts, pad], axis=0)
    save_out.wait()
    save_grad.wait()


GRAD_SHAPES = tuple(jax.ShapeDtypeStruct(s, F32) for s in SHAPES[1:])


def short_call(which, scalars, tokens, upstream, mod, weights, prev):
    count, n, _ = tokens.shape
    in_specs = [SMEM] * 3 + [VMEM] * 7
    args = [*scalars, tokens, upstream, mod, *weights]
    aliases = {}
    if prev is not None:
        in_specs += [ANY, ANY]
        aliases = {len(args): 0, len(args) + 1: 1}
        args += list(prev)
    return pl.pallas_call(
        functools.partial(short_kernel, which),
        name="short" + str(which),
        out_shape=(
            jax.ShapeDtypeStruct(tokens.shape, BF16),
            jax.ShapeDtypeStruct(tokens.shape, F32),
            *GRAD_SHAPES,
            jax.ShapeDtypeStruct((8, D), F32),
        ),
        in_specs=in_specs,
        out_specs=(ANY, ANY) + (VMEM,) * 5,
        scratch_shapes=[
            pltpu.VMEM((n, 3 * D), BF16),
            pltpu.VMEM((HEADS, n, n), F32),
            pltpu.VMEM((n, D), F32),
            pltpu.VMEM((n, D), F32),
            pltpu.VMEM((n, D), F32),
            pltpu.VMEM((n, D), BF16),
            pltpu.VMEM((n, 3 * D), BF16),
            pltpu.VMEM((2, n, n), BF16),
            pltpu.VMEM((n, D), F32),
            pltpu.VMEM((n, D), BF16),
            pltpu.SemaphoreType.DMA((2,)),
        ],
        input_output_aliases=aliases,
        compiler_params=PARAMS,
        cost_estimate=pl.CostEstimate(
            flops=8 * 10**9, bytes_accessed=2 * 10**7, transcendentals=2 * 10**6
        ),
    )(*args)


def long_in_kernel(labels_l, lengths_l, x_ref, mod_ref, w_qkv, q_ref, kv_ref):
    label, _ = own_long(labels_l, lengths_l)
    _, _, _, qkv = project(x_ref[0].astype(F32), mods_of(label, mod_ref), w_qkv)
    q_ref[...] = qkv[:, :D]
    kv_ref[...] = qkv[:, D:]


def long_in(scalars, tokens, mod, w_qkv):
    n = tokens.shape[1]
    return pl.pallas_call(
        long_in_kernel,
        name="long_in",
        out_shape=(
            jax.ShapeDtypeStruct((n, D), BF16),
            jax.ShapeDtypeStruct((n, 2 * D), BF16),
        ),
        in_specs=[SMEM] * 2 + [VMEM] * 3,
        out_specs=(VMEM,) * 2,
        compiler_params=PARAMS,
        cost_estimate=pl.CostEstimate(flops=10**8, bytes_accessed=10**6, transcendentals=0),
    )(*scalars, tokens, mod, w_qkv)


def long_mid_kernel(
    direct, labels_l, labels_s, lengths_l, x_ref, up_ref, mod_ref, q_ref, kv,
    w_out, w_up, w_down,
    out_ref, dx1_ref, do_ref, stat_ref, row_ref, dw_out, dw_up, dw_down, dmod_ref,
    o_f, mo, dm,
):
    n = x_ref.shape[1]
    label, length = own_long(labels_l, lengths_l)
    mod = mods_of(label, mod_ref)
    bias = key_bias(direct, n, kv.shape[0], length)
    lane = lax.broadcasted_iota(jnp.int32, (1, 128), 1)
    stat_ref[...] = jnp.zeros_like(stat_ref)

    @pl.loop(0, PAIRS)
    def _(hp):
        q_cols = pl.ds(pl.multiple_of(hp * 128, 128), 128)
        k2 = kv[:, q_cols]
        v2 = kv[:, pl.ds(pl.multiple_of(D + hp * 128, 128), 128)]

        rows = slice(0, n)
        q2 = q_ref[rows, q_cols]
        o2 = None
        for j in range(2):
            s = dot_nt(q2, only_head(k2, j)) * score_scale + bias
            top = jnp.max(s, axis=-1, keepdims=True)
            e = jnp.exp(s - top)
            total = jnp.sum(e, axis=-1, keepdims=True)
            part = dot_nn(e.astype(BF16), only_head(v2, j)) * (1.0 / total)
            o2 = part if o2 is None else o2 + part
            lse = top + jnp.log(total)
            stat_ref[rows, :] += jnp.where(lane == hp * 2 + j, lse, 0.0)
        o_f[rows, q_cols] = o2

    row = lax.axis_index("seq") * n + lax.broadcasted_iota(jnp.int32, (n, 1), 0)
    g = cotangent(up_ref[0], share_of(label, labels_l, labels_s), row < length)
    o_low = o_f[...].astype(BF16)
    out, dx1, d_o, dm_parts = mlp_both(
        x_ref[0].astype(F32), o_low, g, mod, w_out, w_up, w_down,
        dw_out, dw_up, dw_down, mo, dm,
    )
    out_ref[0] = out
    dx1_ref[...] = dx1
    do_ref[...] = d_o
    stat = stat_ref[...]
    for hp in range(PAIRS):
        cols = slice(hp * 128, (hp + 1) * 128)
        prod = d_o[:, cols].astype(F32) * o_f[:, cols]
        for j in range(2):
            delta = jnp.sum(only_head(prod, j), axis=-1, keepdims=True)
            stat = stat + jnp.where(lane == 8 + hp * 2 + j, delta, 0.0)
    stat_ref[...] = stat
    row_ref[...] = stat.T[:16, :]
    pad = jnp.zeros((4, D), F32)
    dmod_ref[...] = jnp.concatenate([*dm_parts, pad], axis=0)


def long_mid(direct, scalars, tokens, *args):
    n = tokens.shape[1]
    return pl.pallas_call(
        functools.partial(long_mid_kernel, direct),
        name="long_mid",
        out_shape=(
            jax.ShapeDtypeStruct(tokens.shape, BF16),
            jax.ShapeDtypeStruct((n, D), F32),
            jax.ShapeDtypeStruct((n, D), BF16),
            jax.ShapeDtypeStruct((n, 128), F32),
            jax.ShapeDtypeStruct((16, n), F32),
            *GRAD_SHAPES[1:],
            jax.ShapeDtypeStruct((8, D), F32),
        ),
        in_specs=[SMEM] * 3 + [VMEM] * 8,
        out_specs=(VMEM,) * 9,
        scratch_shapes=[pltpu.VMEM((n, D), F32)] * 3,
        compiler_params=PARAMS,
        cost_estimate=pl.CostEstimate(
            flops=4 * 10**9, bytes_accessed=2 * 10**7, transcendentals=2 * 10**6
        ),
    )(*scalars, tokens, *args)


def long_back_kernel(
    direct, labels_l, lengths_l, x_ref, mod_ref, q_ref, kv_own, kv, do_ref, stat_ref,
    q_all, do_all, rows_all, dx1_ref, w_qkv,
    grad_ref, dw_qkv, dmod_ref, dqkv, dk_s, dv_s,
):
    n = x_ref.shape[1]
    total = kv.shape[0]
    label, length = own_long(labels_l, lengths_l)
    mod = mods_of(label, mod_ref)
    bias = key_bias(direct, n, total, length)
    lane = lax.broadcasted_iota(jnp.int32, (1, 128), 1)

    @pl.loop(0, PAIRS)
    def _(hp):
        q_cols = pl.ds(pl.multiple_of(hp * 128, 128), 128)
        k_cols = pl.ds(pl.multiple_of(D + hp * 128, 128), 128)
        v_cols = pl.ds(pl.multiple_of(2 * D + hp * 128, 128), 128)
        k2 = kv[:, q_cols]
        v2 = kv[:, k_cols]

        rows = slice(0, n)
        q2 = q_ref[rows, q_cols]
        do2 = do_ref[rows, q_cols]
        stat = stat_ref[rows, :]
        dq2 = None
        for j in range(2):
            kz = only_head(k2, j)
            h = hp * 2 + j
            lse = jnp.sum(jnp.where(lane == h, stat, 0.0), axis=-1, keepdims=True)
            delta = jnp.sum(jnp.where(lane == 8 + h, stat, 0.0), axis=-1, keepdims=True)
            p = jnp.exp(dot_nt(q2, kz) * score_scale + bias - lse)
            dp = dot_nt(do2, only_head(v2, j))
            ds = (p * (dp - delta)).astype(BF16)
            part = dot_nn(ds, kz)
            dq2 = part if dq2 is None else dq2 + part
        dqkv[rows, q_cols] = (dq2 * score_scale).astype(BF16)

        k_own = kv_own[:, q_cols]
        v_own = kv_own[:, k_cols]
        dk_s[...] = jnp.zeros_like(dk_s)
        dv_s[...] = jnp.zeros_like(dv_s)

        @pl.loop(0, total // n)
        def _(qc):
            rows = pl.ds(pl.multiple_of(qc * n, n), n)
            q2 = q_all[rows, q_cols]
            do2 = do_all[rows, q_cols]
            for j in range(2):
                h = hp * 2 + j
                lse = rows_all[qc, pl.ds(h, 1), :]
                delta = rows_all[qc, pl.ds(8 + h, 1), :]
                p = jnp.exp(dot_nt(only_head(k_own, j), q2) * score_scale - lse)
                dp = dot_nt(only_head(v_own, j), do2)
                ds = (p * (dp - delta)).astype(BF16)
                dv_s[j] += dot_nn(p.astype(BF16), do2)
                dk_s[j] += dot_nn(ds, q2)

        row = lax.axis_index("seq") * n + lax.broadcasted_iota(jnp.int32, (n, 1), 0)
        ok = row < length
        dk2 = jnp.where(head_mask(0), dk_s[0], dk_s[1])
        dv2 = jnp.where(head_mask(0), dv_s[0], dv_s[1])
        dqkv[:, k_cols] = jnp.where(ok, dk2 * score_scale, 0.0).astype(BF16)
        dqkv[:, v_cols] = jnp.where(ok, dv2, 0.0).astype(BF16)

    hat, scale = norm_parts(x_ref[0].astype(F32))
    a = (hat * (1.0 + mod[1]) + mod[0]).astype(BF16)
    grad, d_shift1, d_scale1 = project_back(
        dqkv[...], dx1_ref[...], hat, scale, a, mod, w_qkv, dw_qkv
    )
    grad_ref[0] = grad
    pad = jnp.zeros((6, D), F32)
    dmod_ref[...] = jnp.concatenate([d_shift1, d_scale1, pad], axis=0)


def long_back(direct, scalars, tokens, *args):
    n = tokens.shape[1]
    return pl.pallas_call(
        functools.partial(long_back_kernel, direct),
        name="long_back",
        out_shape=(
            jax.ShapeDtypeStruct(tokens.shape, F32),
            GRAD_SHAPES[0],
            jax.ShapeDtypeStruct((8, D), F32),
        ),
        in_specs=[SMEM] * 2 + [VMEM] * 12,
        out_specs=(VMEM,) * 3,
        scratch_shapes=[
            pltpu.VMEM((n, 3 * D), BF16),
            pltpu.VMEM((2, n, 128), F32),
            pltpu.VMEM((2, n, 128), F32),
        ],
        compiler_params=PARAMS,
        cost_estimate=pl.CostEstimate(
            flops=4 * 10**9, bytes_accessed=10**7, transcendentals=4 * 10**6
        ),
    )(*scalars, tokens, *args)


def pack_kernel(
    nq, slots, base, labels_l, labels_s, lengths_l, lengths_s, table,
    dmod_mid, dmod_back, dmod_s0, dmod_s1, *refs,
):
    grads = refs[:12]
    outs = refs[12:-1]
    cond_s = refs[-1]
    part = TILE // nq
    for out in outs:
        out[...] = jnp.zeros_like(out)
    labels = [own_long(labels_l, lengths_l)[0]]
    labels += [own_short(i, 2, labels_s, lengths_s)[0] for i in range(2)]
    d_long = jnp.concatenate([dmod_back[:2, :], dmod_mid[:4, :]], axis=0)
    per_seq = (d_long, dmod_s0[:6, :], dmod_s1[:6, :])
    by_label = []
    for v in range(3):
        acc = None
        for s in range(3):
            term = jnp.where(labels[s] == v, per_seq[s], 0.0)
            acc = term if acc is None else acc + term
        by_label.append(acc)
    v = table[...]
    cond = (v * jax.nn.sigmoid(v)).astype(BF16).astype(F32)
    cond_t = jnp.concatenate([cond, jnp.zeros((5, D), F32)], axis=0).T
    seq = lax.axis_index("seq")
    turns = [(outs[0], 0, 0)]
    if nq > 1:
        turns = [
            (outs[r % 2], (seq ^ r) * part, (r // 2) * 2 * slots) for r in range(nq)
        ]
    cond_s[...] = cond_t

    @pl.loop(0, D // TILE)
    def _(r):
        for out, row, offset in turns:
            here = pl.ds(pl.multiple_of(r * TILE + row, part), part)
            col = [cond_s[here, v : v + 1] for v in range(3)]
            for c in range(6 * D // TILE):
                i, off = divmod(c, D // TILE)
                lanes = slice(off * TILE, (off + 1) * TILE)
                tile = None
                for v in range(3):
                    term = col[v] * by_label[v][i : i + 1, lanes]
                    tile = term if tile is None else tile + term
                out[base[r * (6 * D // TILE) + c] + offset] = tile.astype(BF16)

    first = SHAPES[0][0] * SHAPES[0][1] // TILE**2
    for m, (rows, cols) in enumerate(SHAPES[1:]):
        nr, nc = rows // TILE, cols // TILE
        terms = grads[3 * m : 3 * m + 3]

        @pl.loop(0, nr)
        def _(r, first=first, nc=nc, terms=terms):
            for c in range(nc):
                at = base[first + r * nc + c]
                lanes = slice(c * TILE, (c + 1) * TILE)
                for out, row, offset in turns:
                    here = pl.ds(pl.multiple_of(r * TILE + row, part), part)
                    v = terms[0][here, lanes] + terms[1][here, lanes] + terms[2][here, lanes]
                    out[at + offset] = v.astype(BF16)

        first += nr * nc


def pack(nq, slots, size, base, scalars, table, dmods, grads):
    part = TILE // nq
    halves = 2 if nq > 1 else 1
    return pl.pallas_call(
        functools.partial(pack_kernel, nq, slots),
        name="pack",
        out_shape=(jax.ShapeDtypeStruct((size, part, TILE), BF16),) * halves,
        in_specs=[SMEM] * 5 + [VMEM] * 17,
        out_specs=(VMEM,) * halves,
        scratch_shapes=[pltpu.VMEM((D, 8), F32)],
        compiler_params=PARAMS,
        cost_estimate=pl.CostEstimate(flops=10**7, bytes_accessed=3 * 10**7, transcendentals=0),
    )(base, *scalars, table, *dmods, *grads)


def halves(v):
    high = v.astype(BF16)
    return high, (v - high.astype(F32)).astype(BF16)


def dot3(dot, a, b):
    return dot(a[0], b[0]) + (dot(a[0], b[1]) + dot(a[1], b[0]))


def soap_kernel(nq, g_ref, left, right, first, second, master, gs, fn, sn, wn):
    many = range(master.shape[0])
    place = [0]
    if nq > 1:
        turn = [lax.axis_index("seq") ^ q for q in range(nq)]
        place = [(r % 2) * 2 + r // 2 for r in turn]
    g = [jnp.concatenate([g_ref[place[q], i] for q in range(nq)], axis=0) for i in many]
    for i in many:
        gs[i] = g[i].astype(F32)
    lo = [halves(left[i]) for i in many]
    ro = [halves(right[i]) for i in many]
    rot = [halves(dot_tn(lo[i][0], g[i]) + dot_tn(lo[i][1], g[i])) for i in many]
    rot = [dot3(dot_nn, rot[i], ro[i]) for i in many]
    step = []
    for i in many:
        f = beta_first * first[i] + (1.0 - beta_first) * rot[i]
        s = beta_second * second[i] + (1.0 - beta_second) * rot[i] * rot[i]
        fn[i] = f
        sn[i] = s
        bias_f = 1.0 - beta_first**STEP
        bias_s = 1.0 - beta_second**STEP
        step.append(halves(f / bias_f / (jnp.sqrt(s / bias_s) + adam_eps)))
    back = [halves(dot3(dot_nn, lo[i], step[i])) for i in many]
    back = [dot3(dot_nt, back[i], ro[i]) for i in many]
    for i in many:
        w = master[i]
        mean = jnp.mean(jnp.mean(w * w, axis=1, keepdims=True), axis=0, keepdims=True)
        spread = jnp.sqrt(mean + 1e-06)
        wn[i] = w - base_rate * spread * (back[i] + decay_rate * w)


def soap(nq, g, left, right, first, second, master):
    slots = master.shape[0]
    block = max(k for k in range(1, 12) if slots % k == 0)
    part = TILE // nq
    spec = pl.BlockSpec((block, TILE, TILE), lambda i: (i, 0, 0))
    g_spec = pl.BlockSpec((nq, block, part, TILE), lambda i: (0, i, 0, 0))
    shape = jax.ShapeDtypeStruct(master.shape, F32)
    return pl.pallas_call(
        functools.partial(soap_kernel, nq),
        name="soap",
        grid=(slots // block,),
        out_shape=(shape,) * 4,
        in_specs=[g_spec] + [spec] * 5,
        out_specs=(spec,) * 4,
        compiler_params=PARAMS,
        cost_estimate=pl.CostEstimate(flops=10**9, bytes_accessed=10**7, transcendentals=10**6),
    )(g, left, right, first, second, master)


class Grid:
    def __init__(self, n_dp, n_seq):
        self.direct = n_dp == 8 and n_seq == 4
        self.n = {"z": n_dp // 2, "y": 2, "x": n_seq // 2, "c": 2}
        self.n_dp = n_dp
        self.n_seq = n_seq
        self.nq = n_seq if self.direct else 1

    def shift(self, v, names):
        pairs = []
        for dp in range(self.n_dp):
            for seq in range(self.n_seq):
                at = {"z": dp // 2, "y": dp % 2, "x": seq // 2, "c": seq % 2}
                to = {k: (v + (k in names)) % self.n[k] for k, v in at.items()}
                pairs.append(((dp, seq), (to["z"] * 2 + to["y"], to["x"] * 2 + to["c"])))
        if not set(names) & set("zy"):
            axis, flat = "seq", {(a[1], b[1]) for a, b in pairs}
        elif not set(names) & set("xc"):
            axis, flat = "dp", {(a[0], b[0]) for a, b in pairs}
        else:
            axis = ("dp", "seq")
            flat = {tuple(d * self.n_seq + q for d, q in pair) for pair in pairs}
        return lax.ppermute(v, axis, sorted(flat))

    def over_seq(self, v):
        if not self.direct:
            return lax.all_gather(v, "seq", axis=0, tiled=True)
        return jnp.concatenate([v] + [self.shift(v, n) for n in ("x", "c", "xc")], axis=0)

    def table(self, tile_slot, slots, sign):
        if not self.direct:
            return tile_slot
        dp = lax.axis_index("dp")
        owner = tile_slot // slots
        rz = (sign * (dp // 2 - owner // 2)) % self.n["z"]
        ry = (dp ^ owner) & 1
        return (rz * (8 if sign > 0 else 4) + ry) * slots + tile_slot % slots

    def gather_slots(self, low):
        if not self.direct:
            return [lax.all_gather(low, "dp", axis=0, tiled=True)]
        part = TILE // self.nq
        piece = lax.dynamic_slice_in_dim(low, lax.axis_index("seq") * part, part, 1)
        out = []
        for r in range(self.n["z"]):
            if r:
                piece = self.shift(piece, "z")
            near = [piece] + [self.shift(piece, n) for n in ("y", "x", "xy")]
            near = jnp.concatenate(near, axis=0)
            out += [near, self.shift(near, "c")]
        return out

    def reduce_slots(self, parts):
        if not self.direct:
            total = lax.psum_scatter(
                parts[0].astype(F32), "dp", scatter_dimension=0, tiled=True
            )
            return lax.psum(total, "seq")[None]
        acc = None
        for r in range(self.n["z"] - 1, -1, -1):
            k = parts[0].shape[0] // (4 * self.n["z"])
            rows = slice(4 * k * r, 4 * k * (r + 1))
            other = self.shift(parts[1][rows], "c")
            both = parts[0][rows].astype(F32) + other.astype(F32)
            total = both[:k]
            for i, names in enumerate(("y", "x", "xy")):
                block = both[(i + 1) * k : (i + 2) * k].astype(BF16)
                total = total + self.shift(block, names).astype(F32)
            if acc is not None:
                total = total + self.shift(acc, "z").astype(F32)
            acc = total.astype(BF16)
        return self.over_seq(acc[None])


def local(
    tokens_long,
    tokens_short,
    upstream_long,
    upstream_short,
    interval_table,
    labels_long,
    labels_short,
    lengths_long,
    lengths_short,
    tile_slot,
    master_slots,
    basis_left,
    basis_right,
    first_moment,
    second_moment,
):
    grid = Grid(lax.axis_size("dp"), lax.axis_size("seq"))
    slots = master_slots.shape[0]
    nq, direct = grid.nq, grid.direct
    srcs = grid.gather_slots(master_slots.astype(BF16))
    base_in = grid.table(tile_slot, slots, 1)
    base_out = grid.table(tile_slot, slots, -1)
    base_in, base_out, srcs[0] = lax.optimization_barrier((base_in, base_out, srcs[0]))
    *weights, mod_table = unpack(nq, slots, srcs, base_in, interval_table)
    w_qkv, w_out, w_up, w_down = weights

    def short(i, prev):
        return short_call(
            i, (labels_long, labels_short, lengths_short), tokens_short, upstream_short,
            mod_table, weights, prev,
        )

    q, kv_own = long_in((labels_long, lengths_long), tokens_long, mod_table, w_qkv)
    kv = grid.over_seq(kv_own)
    res0 = short(0, None)
    kv, dmod_s0 = lax.optimization_barrier((kv, res0[6]))
    (
        out_long, dx1, d_o, stat, stat_rows, dw_out_l, dw_up_l, dw_down_l, dmod_mid,
    ) = long_mid(
        direct, (labels_long, labels_short, lengths_long), tokens_long, upstream_long,
        mod_table, q, kv, w_out, w_up, w_down,
    )
    q_all = grid.over_seq(q)
    do_all = grid.over_seq(d_o)
    rows_all = grid.over_seq(stat_rows[None])
    prev0, prev1, dmod_mid = lax.optimization_barrier((res0[0], res0[1], dmod_mid))
    res1 = short(1, (prev0, prev1))
    q_all, do_all, rows_all, dmod_s1 = lax.optimization_barrier(
        (q_all, do_all, rows_all, res1[6])
    )
    grad_long, dw_qkv_l, dmod_back = long_back(
        direct, (labels_long, lengths_long), tokens_long, mod_table, q, kv_own, kv, d_o,
        stat, q_all, do_all, rows_all, dx1, w_qkv,
    )
    out_short, grad_short = res1[:2]
    terms = []
    for i, extra in enumerate((dw_qkv_l, dw_out_l, dw_up_l, dw_down_l)):
        terms += [res0[2 + i], res1[2 + i], extra]
    size = grid.n_dp * slots * (2 if direct else 1)
    parts = pack(
        nq, slots, size, base_out, (labels_long, labels_short, lengths_long, lengths_short),
        interval_table, (dmod_mid, dmod_back, dmod_s0, dmod_s1), terms,
    )
    g = grid.reduce_slots(parts)
    grad_slots, first_new, second_new, weight_new = soap(
        nq, g, basis_left, basis_right, first_moment, second_moment, master_slots
    )
    return (
        out_long, out_short, grad_long, grad_short,
        grad_slots, first_new, second_new, weight_new,
    )


def solution(mesh):
    rows = P(("dp", "seq"), None, None)
    cols = P("dp", "seq", None)
    slots = P("dp", None, None)
    return jax.shard_map(
        local,
        mesh=mesh,
        in_specs=(cols, rows, cols, rows) + (P(),) * 6 + (slots,) * 5,
        out_specs=(cols, rows, cols, rows) + (slots,) * 4,
        check_vma=False,
    )
```

```python
import functools

import jax
import jax.numpy as jnp
from jax import lax
from jax.experimental import pallas as pl
from jax.experimental.pallas import tpu as pltpu
from jax.sharding import PartitionSpec as P

D = 384
HEADS = 6
HD = 64
FF = 1536
STEP = 10
TILE = 128
PAIRS = HEADS // 2
SHAPES = ((D, 6 * D), (D, 3 * D), (D, D), (D, FF), (FF, D))

F32 = jnp.float32
BF16 = jnp.bfloat16
beta_first = 0.9
beta_second = 0.95
adam_eps = 1e-08
base_rate = 0.3
decay_rate = 0.01
norm_eps = 1e-06
masked_score = -1e30
score_scale = HD ** (-0.5)
FF_BLOCK = 384


VMEM = pl.BlockSpec(memory_space=pltpu.VMEM)
SMEM = pl.BlockSpec(memory_space=pltpu.SMEM)
ANY = pl.BlockSpec(memory_space=pl.ANY)
PARAMS = pltpu.CompilerParams(vmem_limit_bytes=24 * 2**20)


def dot_nn(a, b):
    return lax.dot_general(a, b, (((1,), (0,)), ((), ())), preferred_element_type=F32)


def dot_nt(a, b):
    return lax.dot_general(a, b, (((1,), (1,)), ((), ())), preferred_element_type=F32)


def dot_tn(a, b):
    return lax.dot_general(a, b, (((0,), (0,)), ((), ())), preferred_element_type=F32)


def norm_parts(v):
    centered = v - jnp.mean(v, axis=-1, keepdims=True)
    scale = lax.rsqrt(jnp.mean(centered * centered, axis=-1, keepdims=True) + norm_eps)
    return centered * scale, scale


def norm_back(dy, hat, scale):
    return scale * (
        dy
        - jnp.mean(dy, axis=-1, keepdims=True)
        - hat * jnp.mean(dy * hat, axis=-1, keepdims=True)
    )


def col_sum(v):
    return jnp.sum(v, axis=0, keepdims=True)


def head_mask(j):
    lane = lax.broadcasted_iota(jnp.int32, (1, 2 * HD), 1)
    return (lane >= j * HD) & (lane < (j + 1) * HD)


def only_head(v, j):
    return jnp.where(head_mask(j), v, jnp.zeros_like(v))


def gelu_both(u):
    k0 = 0.7978845608028654
    sq = u * u
    t = jnp.tanh(u * (k0 + (k0 * 0.044715) * sq))
    half = 0.5 * (1.0 + t)
    slope = half + (0.5 * u) * (1.0 - t * t) * (k0 + (3.0 * k0 * 0.044715) * sq)
    return u * half, slope


def own_long(labels, lengths):
    at = lax.axis_index("dp")
    return labels[at], lengths[at]


def own_short(which, count, labels, lengths):
    at = (lax.axis_index("dp") * lax.axis_size("seq") + lax.axis_index("seq")) * count + which
    return labels[at], lengths[at]


def share_of(label, *tables):
    total = 0
    many = jnp.int32(0)
    for table in tables:
        size = table.shape[0]
        total += size
        many = lax.fori_loop(
            0, size, lambda i, n, t=table: n + (t[i] == label).astype(jnp.int32), many
        )
    return float(total) / (3.0 * many.astype(F32))


def key_bias(direct, rows, total, length):
    seq = lax.axis_index("seq")
    lane = lax.broadcasted_iota(jnp.int32, (1, rows), 1)
    out = []
    for i in range(total // rows):
        block = (seq ^ ((i % 2) * 2 + i // 2)) if direct else i
        out.append(jnp.where(block * rows + lane < length, 0.0, masked_score))
    return jnp.concatenate(out, axis=1)


def unpack_kernel(nq, slots, sizes, base, table, *refs):
    srcs = refs[: len(sizes)]
    w_qkv, w_out, w_up, w_down, mod, buf, w_ada, sems = refs[len(sizes) :]
    part = TILE // nq
    copies = []
    start = 0
    for i, size in enumerate(sizes):
        cp = pltpu.make_async_copy(srcs[i], buf.at[pl.ds(start, size)], sems.at[i])
        cp.start()
        copies.append(cp)
        start += size
    seq = lax.axis_index("seq")
    offset = [0]
    if nq > 1:
        turn = [seq ^ q for q in range(nq)]
        offset = [((r % 2) * 4 + (r // 2) * 2) * slots for r in turn]
    for cp in copies:
        cp.wait()
    first = 0
    for (rows, cols), dst in zip(SHAPES, (w_ada, w_qkv, w_out, w_up, w_down)):
        nr, nc = rows // TILE, cols // TILE

        @pl.loop(0, nr)
        def _(r, first=first, nc=nc, dst=dst):
            for c in range(nc):
                at = base[first + r * nc + c]
                for q in range(nq):
                    row = pl.multiple_of(r * TILE + q * part, part)
                    dst[pl.ds(row, part), c * TILE : (c + 1) * TILE] = buf[at + offset[q]]

        first += nr * nc
    v = table[...]
    cond = v * jax.nn.sigmoid(v)
    cond = jnp.concatenate([cond, jnp.zeros((5, D), F32)], axis=0).astype(BF16)
    mod[...] = dot_nn(cond, w_ada[...])


def unpack(nq, slots, srcs, base, table):
    sizes = tuple(s.shape[0] for s in srcs)
    part = TILE // nq
    return pl.pallas_call(
        functools.partial(unpack_kernel, nq, slots, sizes),
        name="unpack",
        out_shape=tuple(jax.ShapeDtypeStruct(s, BF16) for s in SHAPES[1:])
        + (jax.ShapeDtypeStruct((8, 6 * D), F32),),
        in_specs=[SMEM, VMEM] + [ANY] * len(srcs),
        out_specs=(VMEM,) * 5,
        scratch_shapes=[
            pltpu.VMEM((sum(sizes), part, TILE), BF16),
            pltpu.VMEM(SHAPES[0], BF16),
            pltpu.SemaphoreType.DMA((len(sizes),)),
        ],
        compiler_params=PARAMS,
        cost_estimate=pl.CostEstimate(flops=10**7, bytes_accessed=10**7, transcendentals=0),
    )(base, table, *srcs)


def mods_of(label, mod):
    row = mod[pl.ds(label, 1), :]
    return [row[:, i * D : (i + 1) * D] for i in range(6)]


def project(x, mod, w_qkv):
    hat, scale = norm_parts(x)
    a = (hat * (1.0 + mod[1]) + mod[0]).astype(BF16)
    return hat, scale, a, dot_nn(a, w_qkv[...]).astype(BF16)


def mlp_both(x, o_low, g, mod, w_out, w_up, w_down, dw_out, dw_up, dw_down, mo, dm):
    att = dot_nn(o_low, w_out[...])
    x1 = x + mod[2] * att
    hat, scale = norm_parts(x1)
    m = (hat * (1.0 + mod[4]) + mod[3]).astype(BF16)
    d_mo = (mod[5] * g).astype(BF16)
    mo[...] = jnp.zeros_like(mo)
    dm[...] = jnp.zeros_like(dm)

    @pl.loop(0, FF // FF_BLOCK)
    def _(b):
        cols = pl.ds(pl.multiple_of(b * FF_BLOCK, FF_BLOCK), FF_BLOCK)
        u = dot_nn(m, w_up[:, cols])
        d_r = dot_nt(d_mo, w_down[cols, :])
        act, slope = gelu_both(u)
        r = act.astype(BF16)
        du = (d_r * slope).astype(BF16)
        mo[...] += dot_nn(r, w_down[cols, :])
        dm[...] += dot_nt(du, w_up[:, cols])
        dw_up[:, cols] = dot_tn(m, du)
        dw_down[cols, :] = dot_tn(r, d_mo)

    mo_v = mo[...]
    out = (x1 + mod[5] * mo_v).astype(BF16)
    d_gate2 = col_sum(mo_v * g)
    dm_v = dm[...]
    d_shift2 = col_sum(dm_v)
    d_scale2 = col_sum(dm_v * hat)
    dx1 = g + norm_back(dm_v * (1.0 + mod[4]), hat, scale)
    d_att = (mod[2] * dx1).astype(BF16)
    d_gate1 = col_sum(att * dx1)
    dw_out[...] = dot_tn(o_low, d_att)
    d_o = dot_nt(d_att, w_out[...]).astype(BF16)
    return out, dx1, d_o, (d_gate1, d_shift2, d_scale2, d_gate2)


def project_back(dqkv, dx1, hat, scale, a, mod, w_qkv, dw_qkv):
    dw_qkv[...] = dot_tn(a, dqkv)
    d_a = dot_nt(dqkv, w_qkv[...])
    d_shift = col_sum(d_a)
    d_scale = col_sum(d_a * hat)
    return dx1 + norm_back(d_a * (1.0 + mod[1]), hat, scale), d_shift, d_scale


def cotangent(up, weight, rows_ok):
    return jnp.where(rows_ok, up.astype(F32) * weight, 0.0)


def short_kernel(
    which, labels_l, labels_s, lengths_s, x_all, up_all, mod_ref,
    w_qkv, w_out, w_up, w_down, *refs,
):
    if which:
        refs = refs[2:]
    (
        out_all, grad_all, dw_qkv, dw_out, dw_up, dw_down, dmod_ref,
        qkv, probs, o_f, mo, dm, d_o, dqkv, ds_s, x1_s, out_s, sems,
    ) = refs
    count, n, _ = x_all.shape
    x_ref = x_all.at[which]
    up_ref = up_all.at[which]
    label, length = own_short(which, count, labels_s, lengths_s)
    weight = share_of(label, labels_l, labels_s)
    mod = mods_of(label, mod_ref)
    x = x_ref[...].astype(F32)
    hat, scale, a, qkv_v = project(x, mod, w_qkv)
    qkv[...] = qkv_v
    key = lax.broadcasted_iota(jnp.int32, (1, n), 1)
    bias = jnp.where(key < length, 0.0, masked_score)

    @pl.loop(0, PAIRS)
    def _(hp):
        q_cols = pl.ds(pl.multiple_of(hp * 128, 128), 128)
        k2 = qkv[:, pl.ds(pl.multiple_of(D + hp * 128, 128), 128)]
        v2 = qkv[:, pl.ds(pl.multiple_of(2 * D + hp * 128, 128), 128)]

        rows = slice(0, n)
        q2 = qkv[rows, q_cols]
        o2 = None
        for j in range(2):
            s = dot_nt(q2, only_head(k2, j)) * score_scale + bias
            e = jnp.exp(s - jnp.max(s, axis=-1, keepdims=True))
            p = e * (1.0 / jnp.sum(e, axis=-1, keepdims=True))
            probs[hp * 2 + j, rows, :] = p
            part = dot_nn(p.astype(BF16), only_head(v2, j))
            o2 = part if o2 is None else o2 + part
        o_f[rows, q_cols] = o2

    row = lax.broadcasted_iota(jnp.int32, (n, 1), 0)
    g = cotangent(up_ref[...], weight, row < length)
    o_low = o_f[...].astype(BF16)
    out, dx1, d_o_v, dm_parts = mlp_both(
        x, o_low, g, mod, w_out, w_up, w_down, dw_out, dw_up, dw_down, mo, dm
    )
    out_s[...] = out
    save_out = pltpu.make_async_copy(out_s, out_all.at[which], sems.at[0])
    save_out.start()
    x1_s[...] = dx1
    d_o[...] = d_o_v

    @pl.loop(0, PAIRS)
    def _(hp):
        q_cols = pl.ds(pl.multiple_of(hp * 128, 128), 128)
        k_cols = pl.ds(pl.multiple_of(D + hp * 128, 128), 128)
        v_cols = pl.ds(pl.multiple_of(2 * D + hp * 128, 128), 128)
        k2 = qkv[:, k_cols]
        v2 = qkv[:, v_cols]

        rows = slice(0, n)
        do2 = d_o[rows, q_cols]
        prod = do2.astype(F32) * o_f[rows, q_cols]
        dq2 = None
        for j in range(2):
            dp = dot_nt(do2, only_head(v2, j))
            delta = jnp.sum(only_head(prod, j), axis=-1, keepdims=True)
            ds = (probs[hp * 2 + j, rows, :] * (dp - delta)).astype(BF16)
            ds_s[j, rows, :] = ds
            part = dot_nn(ds, only_head(k2, j))
            dq2 = part if dq2 is None else dq2 + part
        dqkv[rows, q_cols] = (dq2 * score_scale).astype(BF16)

        q2 = qkv[:, q_cols]
        do2 = d_o[:, q_cols]
        dk2 = jnp.where(head_mask(0), dot_tn(ds_s[0], q2), dot_tn(ds_s[1], q2))
        dqkv[:, k_cols] = (dk2 * score_scale).astype(BF16)
        p0 = probs[hp * 2].astype(BF16)
        p1 = probs[hp * 2 + 1].astype(BF16)
        dv2 = jnp.where(head_mask(0), dot_tn(p0, do2), dot_tn(p1, do2))
        dqkv[:, v_cols] = dv2.astype(BF16)

    x = x_ref[...].astype(F32)
    hat, scale = norm_parts(x)
    a = (hat * (1.0 + mod[1]) + mod[0]).astype(BF16)
    grad, d_shift1, d_scale1 = project_back(
        dqkv[...], x1_s[...], hat, scale, a, mod, w_qkv, dw_qkv
    )
    x1_s[...] = grad
    save_grad = pltpu.make_async_copy(x1_s, grad_all.at[which], sems.at[1])
    save_grad.start()
    pad = jnp.zeros((2, D), F32)
    dmod_ref[...] = jnp.concatenate([d_shift1, d_scale1, *dm_parts, pad], axis=0)
    save_out.wait()
    save_grad.wait()


GRAD_SHAPES = tuple(jax.ShapeDtypeStruct(s, F32) for s in SHAPES[1:])


def short_call(which, scalars, tokens, upstream, mod, weights, prev):
    count, n, _ = tokens.shape
    in_specs = [SMEM] * 3 + [VMEM] * 7
    args = [*scalars, tokens, upstream, mod, *weights]
    aliases = {}
    if prev is not None:
        in_specs += [ANY, ANY]
        aliases = {len(args): 0, len(args) + 1: 1}
        args += list(prev)
    return pl.pallas_call(
        functools.partial(short_kernel, which),
        name="short" + str(which),
        out_shape=(
            jax.ShapeDtypeStruct(tokens.shape, BF16),
            jax.ShapeDtypeStruct(tokens.shape, F32),
            *GRAD_SHAPES,
            jax.ShapeDtypeStruct((8, D), F32),
        ),
        in_specs=in_specs,
        out_specs=(ANY, ANY) + (VMEM,) * 5,
        scratch_shapes=[
            pltpu.VMEM((n, 3 * D), BF16),
            pltpu.VMEM((HEADS, n, n), F32),
            pltpu.VMEM((n, D), F32),
            pltpu.VMEM((n, D), F32),
            pltpu.VMEM((n, D), F32),
            pltpu.VMEM((n, D), BF16),
            pltpu.VMEM((n, 3 * D), BF16),
            pltpu.VMEM((2, n, n), BF16),
            pltpu.VMEM((n, D), F32),
            pltpu.VMEM((n, D), BF16),
            pltpu.SemaphoreType.DMA((2,)),
        ],
        input_output_aliases=aliases,
        compiler_params=PARAMS,
        cost_estimate=pl.CostEstimate(
            flops=8 * 10**9, bytes_accessed=2 * 10**7, transcendentals=2 * 10**6
        ),
    )(*args)


def long_in_kernel(labels_l, lengths_l, x_ref, mod_ref, w_qkv, q_ref, kv_ref):
    label, _ = own_long(labels_l, lengths_l)
    _, _, _, qkv = project(x_ref[0].astype(F32), mods_of(label, mod_ref), w_qkv)
    q_ref[...] = qkv[:, :D]
    kv_ref[...] = qkv[:, D:]


def long_in(scalars, tokens, mod, w_qkv):
    n = tokens.shape[1]
    return pl.pallas_call(
        long_in_kernel,
        name="long_in",
        out_shape=(
            jax.ShapeDtypeStruct((n, D), BF16),
            jax.ShapeDtypeStruct((n, 2 * D), BF16),
        ),
        in_specs=[SMEM] * 2 + [VMEM] * 3,
        out_specs=(VMEM,) * 2,
        compiler_params=PARAMS,
        cost_estimate=pl.CostEstimate(flops=10**8, bytes_accessed=10**6, transcendentals=0),
    )(*scalars, tokens, mod, w_qkv)


def long_mid_kernel(
    direct, labels_l, labels_s, lengths_l, x_ref, up_ref, mod_ref, q_ref, kv,
    w_out, w_up, w_down,
    out_ref, dx1_ref, pack_ref, stat_ref, dw_out, dw_up, dw_down, dmod_ref,
    o_f, mo, dm,
):
    n = x_ref.shape[1]
    label, length = own_long(labels_l, lengths_l)
    mod = mods_of(label, mod_ref)
    bias = key_bias(direct, n, kv.shape[0], length)
    lane = lax.broadcasted_iota(jnp.int32, (1, 128), 1)
    stat_ref[...] = jnp.zeros_like(stat_ref)

    @pl.loop(0, PAIRS)
    def _(hp):
        q_cols = pl.ds(pl.multiple_of(hp * 128, 128), 128)
        k2 = kv[:, q_cols]
        v2 = kv[:, pl.ds(pl.multiple_of(D + hp * 128, 128), 128)]

        rows = slice(0, n)
        q2 = q_ref[rows, q_cols]
        o2 = None
        for j in range(2):
            s = dot_nt(q2, only_head(k2, j)) * score_scale + bias
            top = jnp.max(s, axis=-1, keepdims=True)
            e = jnp.exp(s - top)
            total = jnp.sum(e, axis=-1, keepdims=True)
            part = dot_nn(e.astype(BF16), only_head(v2, j)) * (1.0 / total)
            o2 = part if o2 is None else o2 + part
            lse = top + jnp.log(total)
            stat_ref[rows, :] += jnp.where(lane == hp * 2 + j, lse, 0.0)
        o_f[rows, q_cols] = o2

    row = lax.axis_index("seq") * n + lax.broadcasted_iota(jnp.int32, (n, 1), 0)
    g = cotangent(up_ref[0], share_of(label, labels_l, labels_s), row < length)
    o_low = o_f[...].astype(BF16)
    out, dx1, d_o, dm_parts = mlp_both(
        x_ref[0].astype(F32), o_low, g, mod, w_out, w_up, w_down,
        dw_out, dw_up, dw_down, mo, dm,
    )
    out_ref[0] = out
    dx1_ref[...] = dx1
    pack_ref[:, :D] = q_ref[...]
    pack_ref[:, D : 2 * D] = d_o
    stat = stat_ref[...]
    for hp in range(PAIRS):
        cols = slice(hp * 128, (hp + 1) * 128)
        prod = d_o[:, cols].astype(F32) * o_f[:, cols]
        for j in range(2):
            delta = jnp.sum(only_head(prod, j), axis=-1, keepdims=True)
            stat = stat + jnp.where(lane == 8 + hp * 2 + j, delta, 0.0)
    stat_ref[...] = stat
    for i in range(3):
        term = stat.astype(BF16)
        pack_ref[:, 2 * D + i * 128 : 2 * D + (i + 1) * 128] = term
        stat = stat - term.astype(F32)
    pad = jnp.zeros((4, D), F32)
    dmod_ref[...] = jnp.concatenate([*dm_parts, pad], axis=0)


def long_mid(direct, scalars, tokens, *args):
    n = tokens.shape[1]
    return pl.pallas_call(
        functools.partial(long_mid_kernel, direct),
        name="long_mid",
        out_shape=(
            jax.ShapeDtypeStruct(tokens.shape, BF16),
            jax.ShapeDtypeStruct((n, D), F32),
            jax.ShapeDtypeStruct((n, 3 * D), BF16),
            jax.ShapeDtypeStruct((n, 128), F32),
            *GRAD_SHAPES[1:],
            jax.ShapeDtypeStruct((8, D), F32),
        ),
        in_specs=[SMEM] * 3 + [VMEM] * 8,
        out_specs=(VMEM,) * 8,
        scratch_shapes=[pltpu.VMEM((n, D), F32)] * 3,
        compiler_params=PARAMS,
        cost_estimate=pl.CostEstimate(
            flops=4 * 10**9, bytes_accessed=2 * 10**7, transcendentals=2 * 10**6
        ),
    )(*scalars, tokens, *args)


def long_back_kernel(
    direct, labels_l, lengths_l, x_ref, mod_ref, kv_own, kv, own_ref, stat_ref, pack_all,
    dx1_ref, w_qkv, grad_ref, dw_qkv, dmod_ref, dqkv, dk_s, dv_s, rows_all,
):
    n = x_ref.shape[1]
    total = kv.shape[0]
    label, length = own_long(labels_l, lengths_l)
    mod = mods_of(label, mod_ref)
    bias = key_bias(direct, n, total, length)
    lane = lax.broadcasted_iota(jnp.int32, (1, 128), 1)

    @pl.loop(0, total // n)
    def _(i):
        at = pl.ds(pl.multiple_of(i * n, n), n)
        terms = [pack_all[at, 2 * D + j * 128 : 2 * D + (j + 1) * 128] for j in range(3)]
        stat = terms[0].astype(F32) + (terms[1].astype(F32) + terms[2].astype(F32))
        rows_all[i] = stat.T[:16, :]

    @pl.loop(0, PAIRS)
    def _(hp):
        q_cols = pl.ds(pl.multiple_of(hp * 128, 128), 128)
        k_cols = pl.ds(pl.multiple_of(D + hp * 128, 128), 128)
        v_cols = pl.ds(pl.multiple_of(2 * D + hp * 128, 128), 128)
        k2 = kv[:, q_cols]
        v2 = kv[:, k_cols]

        rows = slice(0, n)
        q2 = own_ref[rows, q_cols]
        do2 = own_ref[rows, k_cols]
        stat = stat_ref[rows, :]
        dq2 = None
        for j in range(2):
            kz = only_head(k2, j)
            h = hp * 2 + j
            lse = jnp.sum(jnp.where(lane == h, stat, 0.0), axis=-1, keepdims=True)
            delta = jnp.sum(jnp.where(lane == 8 + h, stat, 0.0), axis=-1, keepdims=True)
            p = jnp.exp(dot_nt(q2, kz) * score_scale + bias - lse)
            dp = dot_nt(do2, only_head(v2, j))
            ds = (p * (dp - delta)).astype(BF16)
            part = dot_nn(ds, kz)
            dq2 = part if dq2 is None else dq2 + part
        dqkv[rows, q_cols] = (dq2 * score_scale).astype(BF16)

        k_own = kv_own[:, q_cols]
        v_own = kv_own[:, k_cols]
        dk_s[...] = jnp.zeros_like(dk_s)
        dv_s[...] = jnp.zeros_like(dv_s)

        @pl.loop(0, total // n)
        def _(qc):
            rows = pl.ds(pl.multiple_of(qc * n, n), n)
            q2 = pack_all[rows, q_cols]
            do2 = pack_all[rows, k_cols]
            for j in range(2):
                h = hp * 2 + j
                lse = rows_all[qc, pl.ds(h, 1), :]
                delta = rows_all[qc, pl.ds(8 + h, 1), :]
                p = jnp.exp(dot_nt(only_head(k_own, j), q2) * score_scale - lse)
                dp = dot_nt(only_head(v_own, j), do2)
                ds = (p * (dp - delta)).astype(BF16)
                dv_s[j] += dot_nn(p.astype(BF16), do2)
                dk_s[j] += dot_nn(ds, q2)

        row = lax.axis_index("seq") * n + lax.broadcasted_iota(jnp.int32, (n, 1), 0)
        ok = row < length
        dk2 = jnp.where(head_mask(0), dk_s[0], dk_s[1])
        dv2 = jnp.where(head_mask(0), dv_s[0], dv_s[1])
        dqkv[:, k_cols] = jnp.where(ok, dk2 * score_scale, 0.0).astype(BF16)
        dqkv[:, v_cols] = jnp.where(ok, dv2, 0.0).astype(BF16)

    hat, scale = norm_parts(x_ref[0].astype(F32))
    a = (hat * (1.0 + mod[1]) + mod[0]).astype(BF16)
    grad, d_shift1, d_scale1 = project_back(
        dqkv[...], dx1_ref[...], hat, scale, a, mod, w_qkv, dw_qkv
    )
    grad_ref[0] = grad
    pad = jnp.zeros((6, D), F32)
    dmod_ref[...] = jnp.concatenate([d_shift1, d_scale1, pad], axis=0)


def long_back(direct, scalars, tokens, *args):
    n = tokens.shape[1]
    return pl.pallas_call(
        functools.partial(long_back_kernel, direct),
        name="long_back",
        out_shape=(
            jax.ShapeDtypeStruct(tokens.shape, F32),
            GRAD_SHAPES[0],
            jax.ShapeDtypeStruct((8, D), F32),
        ),
        in_specs=[SMEM] * 2 + [VMEM] * 9,
        out_specs=(VMEM,) * 3,
        scratch_shapes=[
            pltpu.VMEM((n, 3 * D), BF16),
            pltpu.VMEM((2, n, 128), F32),
            pltpu.VMEM((2, n, 128), F32),
            pltpu.VMEM((args[2].shape[0] // n, 16, n), F32),
        ],
        compiler_params=PARAMS,
        cost_estimate=pl.CostEstimate(
            flops=4 * 10**9, bytes_accessed=10**7, transcendentals=4 * 10**6
        ),
    )(*scalars, tokens, *args)


def pack_kernel(
    nq, slots, base, labels_l, labels_s, lengths_l, lengths_s, table,
    dmod_mid, dmod_back, dmod_s0, dmod_s1, *refs,
):
    grads = refs[:12]
    outs = refs[12:-1]
    cond_s = refs[-1]
    part = TILE // nq
    for out in outs:
        out[...] = jnp.zeros_like(out)
    labels = [own_long(labels_l, lengths_l)[0]]
    labels += [own_short(i, 2, labels_s, lengths_s)[0] for i in range(2)]
    d_long = jnp.concatenate([dmod_back[:2, :], dmod_mid[:4, :]], axis=0)
    per_seq = (d_long, dmod_s0[:6, :], dmod_s1[:6, :])
    by_label = []
    for v in range(3):
        acc = None
        for s in range(3):
            term = jnp.where(labels[s] == v, per_seq[s], 0.0)
            acc = term if acc is None else acc + term
        by_label.append(acc)
    v = table[...]
    cond = (v * jax.nn.sigmoid(v)).astype(BF16).astype(F32)
    cond_t = jnp.concatenate([cond, jnp.zeros((5, D), F32)], axis=0).T
    seq = lax.axis_index("seq")
    turns = [(outs[0], 0, 0)]
    if nq > 1:
        turns = [
            (outs[r % 2], (seq ^ r) * part, (r // 2) * 2 * slots) for r in range(nq)
        ]
    cond_s[...] = cond_t

    @pl.loop(0, D // TILE)
    def _(r):
        for out, row, offset in turns:
            here = pl.ds(pl.multiple_of(r * TILE + row, part), part)
            col = [cond_s[here, v : v + 1] for v in range(3)]
            for c in range(6 * D // TILE):
                i, off = divmod(c, D // TILE)
                lanes = slice(off * TILE, (off + 1) * TILE)
                tile = None
                for v in range(3):
                    term = col[v] * by_label[v][i : i + 1, lanes]
                    tile = term if tile is None else tile + term
                out[base[r * (6 * D // TILE) + c] + offset] = tile.astype(BF16)

    first = SHAPES[0][0] * SHAPES[0][1] // TILE**2
    for m, (rows, cols) in enumerate(SHAPES[1:]):
        nr, nc = rows // TILE, cols // TILE
        terms = grads[3 * m : 3 * m + 3]

        @pl.loop(0, nr)
        def _(r, first=first, nc=nc, terms=terms):
            for c in range(nc):
                at = base[first + r * nc + c]
                lanes = slice(c * TILE, (c + 1) * TILE)
                for out, row, offset in turns:
                    here = pl.ds(pl.multiple_of(r * TILE + row, part), part)
                    v = terms[0][here, lanes] + terms[1][here, lanes] + terms[2][here, lanes]
                    out[at + offset] = v.astype(BF16)

        first += nr * nc


def pack(nq, slots, size, base, scalars, table, dmods, grads):
    part = TILE // nq
    halves = 2 if nq > 1 else 1
    return pl.pallas_call(
        functools.partial(pack_kernel, nq, slots),
        name="pack",
        out_shape=(jax.ShapeDtypeStruct((size, part, TILE), BF16),) * halves,
        in_specs=[SMEM] * 5 + [VMEM] * 17,
        out_specs=(VMEM,) * halves,
        scratch_shapes=[pltpu.VMEM((D, 8), F32)],
        compiler_params=PARAMS,
        cost_estimate=pl.CostEstimate(flops=10**7, bytes_accessed=3 * 10**7, transcendentals=0),
    )(base, *scalars, table, *dmods, *grads)


def halves(v):
    high = v.astype(BF16)
    return high, (v - high.astype(F32)).astype(BF16)


def dot3(dot, a, b):
    return dot(a[0], b[0]) + (dot(a[0], b[1]) + dot(a[1], b[0]))


def soap_kernel(nq, g_ref, left, right, first, second, master, gs, fn, sn, wn):
    many = range(master.shape[0])
    place = [0]
    if nq > 1:
        turn = [lax.axis_index("seq") ^ q for q in range(nq)]
        place = [(r % 2) * 2 + r // 2 for r in turn]
    g = [jnp.concatenate([g_ref[place[q], i] for q in range(nq)], axis=0) for i in many]
    for i in many:
        gs[i] = g[i].astype(F32)
    lo = [halves(left[i]) for i in many]
    ro = [halves(right[i]) for i in many]
    rot = [halves(dot_tn(lo[i][0], g[i]) + dot_tn(lo[i][1], g[i])) for i in many]
    rot = [dot3(dot_nn, rot[i], ro[i]) for i in many]
    step = []
    for i in many:
        f = beta_first * first[i] + (1.0 - beta_first) * rot[i]
        s = beta_second * second[i] + (1.0 - beta_second) * rot[i] * rot[i]
        fn[i] = f
        sn[i] = s
        bias_f = 1.0 - beta_first**STEP
        bias_s = 1.0 - beta_second**STEP
        step.append(halves(f / bias_f / (jnp.sqrt(s / bias_s) + adam_eps)))
    back = [halves(dot3(dot_nn, lo[i], step[i])) for i in many]
    back = [dot3(dot_nt, back[i], ro[i]) for i in many]
    for i in many:
        w = master[i]
        mean = jnp.mean(jnp.mean(w * w, axis=1, keepdims=True), axis=0, keepdims=True)
        spread = jnp.sqrt(mean + 1e-06)
        wn[i] = w - base_rate * spread * (back[i] + decay_rate * w)


def soap(nq, g, left, right, first, second, master):
    slots = master.shape[0]
    block = max(k for k in range(1, 12) if slots % k == 0)
    part = TILE // nq
    spec = pl.BlockSpec((block, TILE, TILE), lambda i: (i, 0, 0))
    g_spec = pl.BlockSpec((nq, block, part, TILE), lambda i: (0, i, 0, 0))
    shape = jax.ShapeDtypeStruct(master.shape, F32)
    return pl.pallas_call(
        functools.partial(soap_kernel, nq),
        name="soap",
        grid=(slots // block,),
        out_shape=(shape,) * 4,
        in_specs=[g_spec] + [spec] * 5,
        out_specs=(spec,) * 4,
        compiler_params=PARAMS,
        cost_estimate=pl.CostEstimate(flops=10**9, bytes_accessed=10**7, transcendentals=10**6),
    )(g, left, right, first, second, master)


class Grid:
    def __init__(self, n_dp, n_seq):
        self.direct = n_dp == 8 and n_seq == 4
        self.n = {"z": n_dp // 2, "y": 2, "x": n_seq // 2, "c": 2}
        self.n_dp = n_dp
        self.n_seq = n_seq
        self.nq = n_seq if self.direct else 1

    def shift(self, v, names):
        pairs = []
        for dp in range(self.n_dp):
            for seq in range(self.n_seq):
                at = {"z": dp // 2, "y": dp % 2, "x": seq // 2, "c": seq % 2}
                to = {k: (v + (k in names)) % self.n[k] for k, v in at.items()}
                pairs.append(((dp, seq), (to["z"] * 2 + to["y"], to["x"] * 2 + to["c"])))
        if not set(names) & set("zy"):
            axis, flat = "seq", {(a[1], b[1]) for a, b in pairs}
        elif not set(names) & set("xc"):
            axis, flat = "dp", {(a[0], b[0]) for a, b in pairs}
        else:
            axis = ("dp", "seq")
            flat = {tuple(d * self.n_seq + q for d, q in pair) for pair in pairs}
        return lax.ppermute(v, axis, sorted(flat))

    def over_seq(self, v):
        if not self.direct:
            return lax.all_gather(v, "seq", axis=0, tiled=True)
        return jnp.concatenate([v] + [self.shift(v, n) for n in ("x", "c", "xc")], axis=0)

    def table(self, tile_slot, slots, sign):
        if not self.direct:
            return tile_slot
        dp = lax.axis_index("dp")
        owner = tile_slot // slots
        rz = (sign * (dp // 2 - owner // 2)) % self.n["z"]
        ry = (dp ^ owner) & 1
        return (rz * (8 if sign > 0 else 4) + ry) * slots + tile_slot % slots

    def gather_slots(self, low):
        if not self.direct:
            return [lax.all_gather(low, "dp", axis=0, tiled=True)]
        part = TILE // self.nq
        piece = lax.dynamic_slice_in_dim(low, lax.axis_index("seq") * part, part, 1)
        out = []
        last = self.n["z"] - 1
        k = piece.shape[0]
        for r in range(last + 1):
            if r:
                piece = self.shift(piece, "z")
            if r == last:
                near = [piece] + [self.shift(piece, n) for n in ("y", "x", "xy")]
            elif r % 2:
                by_x = self.shift(piece, "x")
                by_y = self.shift(jnp.concatenate([piece, by_x], axis=0), "y")
                near = [piece, by_y[:k], by_x, by_y[k:]]
            else:
                by_y = jnp.concatenate([piece, self.shift(piece, "y")], axis=0)
                near = [by_y, self.shift(by_y, "x")]
            near = jnp.concatenate(near, axis=0)
            out += [near, self.shift(near, "c")]
        return out

    def reduce_slots(self, parts):
        if not self.direct:
            total = lax.psum_scatter(
                parts[0].astype(F32), "dp", scatter_dimension=0, tiled=True
            )
            return lax.psum(total, "seq")[None]
        acc = None
        k = parts[0].shape[0] // (4 * self.n["z"])
        other = self.shift(parts[1], "c")
        for r in range(self.n["z"] - 1, -1, -1):
            at = 4 * k * r
            block = [
                parts[0][at + i * k : at + (i + 1) * k].astype(F32)
                + other[at + i * k : at + (i + 1) * k].astype(F32)
                for i in range(4)
            ]
            first, second, one, two = ("x", "y", 2, 1) if r % 2 else ("y", "x", 1, 2)
            away = jnp.concatenate([block[one], block[3]], axis=0).astype(BF16)
            away = self.shift(away, first).astype(F32)
            far = self.shift((block[two] + away[k:]).astype(BF16), second)
            total = block[0] + away[:k] + far.astype(F32)
            if acc is not None:
                total = total + self.shift(acc, "z").astype(F32)
            acc = total.astype(BF16)
        return self.over_seq(acc[None])


def local(
    tokens_long,
    tokens_short,
    upstream_long,
    upstream_short,
    interval_table,
    labels_long,
    labels_short,
    lengths_long,
    lengths_short,
    tile_slot,
    master_slots,
    basis_left,
    basis_right,
    first_moment,
    second_moment,
):
    grid = Grid(lax.axis_size("dp"), lax.axis_size("seq"))
    slots = master_slots.shape[0]
    nq, direct = grid.nq, grid.direct
    srcs = grid.gather_slots(master_slots.astype(BF16))
    base_in = grid.table(tile_slot, slots, 1)
    base_out = grid.table(tile_slot, slots, -1)
    base_in, base_out, srcs[0] = lax.optimization_barrier((base_in, base_out, srcs[0]))
    *weights, mod_table = unpack(nq, slots, srcs, base_in, interval_table)
    w_qkv, w_out, w_up, w_down = weights

    def short(i, prev):
        return short_call(
            i, (labels_long, labels_short, lengths_short), tokens_short, upstream_short,
            mod_table, weights, prev,
        )

    q, kv_own = long_in((labels_long, lengths_long), tokens_long, mod_table, w_qkv)
    kv = grid.over_seq(kv_own)
    res0 = short(0, None)
    kv, dmod_s0 = lax.optimization_barrier((kv, res0[6]))
    (
        out_long, dx1, packed, stat, dw_out_l, dw_up_l, dw_down_l, dmod_mid,
    ) = long_mid(
        direct, (labels_long, labels_short, lengths_long), tokens_long, upstream_long,
        mod_table, q, kv, w_out, w_up, w_down,
    )
    packed_all = grid.over_seq(packed)
    prev0, prev1, dmod_mid = lax.optimization_barrier((res0[0], res0[1], dmod_mid))
    res1 = short(1, (prev0, prev1))
    packed_all, dmod_s1 = lax.optimization_barrier((packed_all, res1[6]))
    grad_long, dw_qkv_l, dmod_back = long_back(
        direct, (labels_long, lengths_long), tokens_long, mod_table, kv_own, kv, packed,
        stat, packed_all, dx1, w_qkv,
    )
    out_short, grad_short = res1[:2]
    terms = []
    for i, extra in enumerate((dw_qkv_l, dw_out_l, dw_up_l, dw_down_l)):
        terms += [res0[2 + i], res1[2 + i], extra]
    size = grid.n_dp * slots * (2 if direct else 1)
    parts = pack(
        nq, slots, size, base_out, (labels_long, labels_short, lengths_long, lengths_short),
        interval_table, (dmod_mid, dmod_back, dmod_s0, dmod_s1), terms,
    )
    g = grid.reduce_slots(parts)
    grad_slots, first_new, second_new, weight_new = soap(
        nq, g, basis_left, basis_right, first_moment, second_moment, master_slots
    )
    return (
        out_long, out_short, grad_long, grad_short,
        grad_slots, first_new, second_new, weight_new,
    )


def solution(mesh):
    rows = P(("dp", "seq"), None, None)
    cols = P("dp", "seq", None)
    slots = P("dp", None, None)
    return jax.shard_map(
        local,
        mesh=mesh,
        in_specs=(cols, rows, cols, rows) + (P(),) * 6 + (slots,) * 5,
        out_specs=(cols, rows, cols, rows) + (slots,) * 4,
        check_vma=False,
    )
```

```python
import functools

import jax
import jax.numpy as jnp
from jax import lax
from jax.experimental import pallas as pl
from jax.experimental.pallas import tpu as pltpu
from jax.sharding import PartitionSpec as P

D = 384
HEADS = 6
HD = 64
FF = 1536
STEP = 10
TILE = 128
PAIRS = HEADS // 2
SHAPES = ((D, 6 * D), (D, 3 * D), (D, D), (D, FF), (FF, D))

F32 = jnp.float32
BF16 = jnp.bfloat16
beta_first = 0.9
beta_second = 0.95
adam_eps = 1e-08
base_rate = 0.3
decay_rate = 0.01
norm_eps = 1e-06
masked_score = -1e30
score_scale = HD ** (-0.5)
FF_BLOCK = 768


VMEM = pl.BlockSpec(memory_space=pltpu.VMEM)
SMEM = pl.BlockSpec(memory_space=pltpu.SMEM)
ANY = pl.BlockSpec(memory_space=pl.ANY)
PARAMS = pltpu.CompilerParams(vmem_limit_bytes=30 * 2**20)


def dot_nn(a, b):
    return lax.dot_general(a, b, (((1,), (0,)), ((), ())), preferred_element_type=F32)


def dot_nt(a, b):
    return lax.dot_general(a, b, (((1,), (1,)), ((), ())), preferred_element_type=F32)


def dot_tn(a, b):
    return lax.dot_general(a, b, (((0,), (0,)), ((), ())), preferred_element_type=F32)


def norm_parts(v):
    centered = v - jnp.mean(v, axis=-1, keepdims=True)
    scale = lax.rsqrt(jnp.mean(centered * centered, axis=-1, keepdims=True) + norm_eps)
    return centered * scale, scale


def norm_back(dy, hat, scale):
    return scale * (
        dy
        - jnp.mean(dy, axis=-1, keepdims=True)
        - hat * jnp.mean(dy * hat, axis=-1, keepdims=True)
    )


def col_sum(v):
    return jnp.sum(v, axis=0, keepdims=True)


def head_mask(j):
    lane = lax.broadcasted_iota(jnp.int32, (1, 2 * HD), 1)
    return (lane >= j * HD) & (lane < (j + 1) * HD)


def only_head(v, j):
    return jnp.where(head_mask(j), v, jnp.zeros_like(v))


def with_one(q2, j):
    lane = lax.broadcasted_iota(jnp.int32, (1, 2 * HD), 1)
    one = (lane == (1 - j) * HD).astype(q2.dtype)
    return jnp.where(head_mask(j), q2 * jnp.asarray(score_scale, q2.dtype), one)


def with_mask(k2, j, bias):
    lane = lax.broadcasted_iota(jnp.int32, (1, 2 * HD), 1)
    rest = jnp.where(lane == (1 - j) * HD, bias, 0.0).astype(k2.dtype)
    return jnp.where(head_mask(j), k2, rest)


def gelu_both(u):
    k0 = 0.7978845608028654
    sq = u * u
    t = jnp.tanh(u * (k0 + (k0 * 0.044715) * sq))
    half = 0.5 * (1.0 + t)
    slope = half + (0.5 * u) * (1.0 - t * t) * (k0 + (3.0 * k0 * 0.044715) * sq)
    return u * half, slope


def own_long(labels, lengths):
    at = lax.axis_index("dp")
    return labels[at], lengths[at]


def own_short(which, count, labels, lengths):
    at = (lax.axis_index("dp") * lax.axis_size("seq") + lax.axis_index("seq")) * count + which
    return labels[at], lengths[at]


def share_of(label, *tables):
    total = 0
    many = jnp.int32(0)
    for table in tables:
        size = table.shape[0]
        total += size

        def body(i, n, t=table):
            for j in range(8):
                n = n + (t[i * 8 + j] == label).astype(jnp.int32)
            return n

        many = lax.fori_loop(0, size // 8, body, many)
    return float(total) / (3.0 * many.astype(F32))


def key_bias(direct, rows, total, length):
    seq = lax.axis_index("seq")
    row = lax.broadcasted_iota(jnp.int32, (rows, 1), 0)
    out = []
    for i in range(total // rows):
        block = (seq ^ ((i % 2) * 2 + i // 2)) if direct else i
        out.append(jnp.where(block * rows + row < length, 0.0, masked_score))
    return jnp.concatenate(out, axis=0)


def unpack_kernel(nq, slots, sizes, base, labels_l, labels_s, table, *refs):
    srcs = refs[: len(sizes)]
    w_qkv, w_out, w_up, w_down, mod, share, buf, w_ada, sems = refs[len(sizes) :]
    part = TILE // nq
    copies = []
    start = 0
    for i, size in enumerate(sizes):
        cp = pltpu.make_async_copy(srcs[i], buf.at[pl.ds(start, size)], sems.at[i])
        cp.start()
        copies.append(cp)
        start += size
    seq = lax.axis_index("seq")
    offset = [0]
    if nq > 1:
        turn = [seq ^ q for q in range(nq)]
        offset = [((r % 2) * 4 + (r // 2) * 2) * slots for r in turn]
    at = (lax.axis_index("dp") * lax.axis_size("seq") + seq) * 2
    labels = (labels_l[lax.axis_index("dp")], labels_s[at], labels_s[at + 1])
    for i, label in enumerate(labels):
        share[i] = share_of(label, labels_l, labels_s)
    for cp in copies:
        cp.wait()
    first = 0
    for (rows, cols), dst in zip(SHAPES, (w_ada, w_qkv, w_out, w_up, w_down)):
        nr, nc = rows // TILE, cols // TILE

        @pl.loop(0, nr)
        def _(r, first=first, nc=nc, dst=dst):
            for c in range(nc):
                at = base[first + r * nc + c]
                for q in range(nq):
                    row = pl.multiple_of(r * TILE + q * part, part)
                    dst[pl.ds(row, part), c * TILE : (c + 1) * TILE] = buf[at + offset[q]]

        first += nr * nc
    v = table[...]
    cond = v * jax.nn.sigmoid(v)
    cond = jnp.concatenate([cond, jnp.zeros((5, D), F32)], axis=0).astype(BF16)
    mod[...] = dot_nn(cond, w_ada[...])


def unpack(nq, slots, srcs, base, labels, table):
    sizes = tuple(s.shape[0] for s in srcs)
    part = TILE // nq
    return pl.pallas_call(
        functools.partial(unpack_kernel, nq, slots, sizes),
        name="unpack",
        out_shape=tuple(jax.ShapeDtypeStruct(s, BF16) for s in SHAPES[1:])
        + (jax.ShapeDtypeStruct((8, 6 * D), F32), jax.ShapeDtypeStruct((4,), F32)),
        in_specs=[SMEM] * 3 + [VMEM] + [ANY] * len(srcs),
        out_specs=(VMEM,) * 5 + (SMEM,),
        scratch_shapes=[
            pltpu.VMEM((sum(sizes), part, TILE), BF16),
            pltpu.VMEM(SHAPES[0], BF16),
            pltpu.SemaphoreType.DMA((len(sizes),)),
        ],
        compiler_params=PARAMS,
        cost_estimate=pl.CostEstimate(flops=10**7, bytes_accessed=10**7, transcendentals=0),
    )(base, *labels, table, *srcs)


def mods_of(label, mod):
    row = mod[pl.ds(label, 1), :]
    return [row[:, i * D : (i + 1) * D] for i in range(6)]


def project(x, mod, w_qkv):
    hat, scale = norm_parts(x)
    a = (hat * (1.0 + mod[1]) + mod[0]).astype(BF16)
    return hat, scale, a, dot_nn(a, w_qkv[...]).astype(BF16)


def mlp_both(x, o_low, g, mod, w_out, w_up, w_down, dw_out, dw_up, dw_down, mo, dm):
    att = dot_nn(o_low, w_out[...])
    x1 = x + mod[2] * att
    hat, scale = norm_parts(x1)
    m = (hat * (1.0 + mod[4]) + mod[3]).astype(BF16)
    d_mo = (mod[5] * g).astype(BF16)
    mo[...] = jnp.zeros_like(mo)
    dm[...] = jnp.zeros_like(dm)

    @pl.loop(0, FF // FF_BLOCK)
    def _(b):
        cols = pl.ds(pl.multiple_of(b * FF_BLOCK, FF_BLOCK), FF_BLOCK)
        u = dot_nn(m, w_up[:, cols])
        d_r = dot_nt(d_mo, w_down[cols, :])
        act, slope = gelu_both(u)
        r = act.astype(BF16)
        du = (d_r * slope).astype(BF16)
        mo[...] += dot_nn(r, w_down[cols, :])
        dm[...] += dot_nt(du, w_up[:, cols])
        dw_up[:, cols] = dot_tn(m, du)
        dw_down[cols, :] = dot_tn(r, d_mo)

    mo_v = mo[...]
    out = (x1 + mod[5] * mo_v).astype(BF16)
    d_gate2 = col_sum(mo_v * g)
    dm_v = dm[...]
    d_shift2 = col_sum(dm_v)
    d_scale2 = col_sum(dm_v * hat)
    dx1 = g + norm_back(dm_v * (1.0 + mod[4]), hat, scale)
    d_att = (mod[2] * dx1).astype(BF16)
    d_gate1 = col_sum(att * dx1)
    dw_out[...] = dot_tn(o_low, d_att)
    d_o = dot_nt(d_att, w_out[...]).astype(BF16)
    return out, dx1, d_o, (d_gate1, d_shift2, d_scale2, d_gate2)


def project_back(dqkv, dx1, hat, scale, a, mod, w_qkv, dw_qkv):
    dw_qkv[...] = dot_tn(a, dqkv)
    d_a = dot_nt(dqkv, w_qkv[...])
    d_shift = col_sum(d_a)
    d_scale = col_sum(d_a * hat)
    return dx1 + norm_back(d_a * (1.0 + mod[1]), hat, scale), d_shift, d_scale


def cotangent(up, weight, rows_ok):
    return jnp.where(rows_ok, up.astype(F32) * weight, 0.0)


def short_kernel(
    which, share, labels_s, lengths_s, x_all, up_all, mod_ref,
    w_qkv, w_out, w_up, w_down, *refs,
):
    if which:
        refs = refs[2:]
    (
        out_all, grad_all, dw_qkv, dw_out, dw_up, dw_down, dmod_ref,
        qkv, probs, o_f, mo, dm, d_o, dqkv, probs_low, x1_s, out_s, sems,
    ) = refs
    count, n, _ = x_all.shape
    x_ref = x_all.at[which]
    up_ref = up_all.at[which]
    label, length = own_short(which, count, labels_s, lengths_s)
    weight = share[1 + which]
    mod = mods_of(label, mod_ref)
    x = x_ref[...].astype(F32)
    hat, scale, a, qkv_v = project(x, mod, w_qkv)
    qkv[...] = qkv_v
    key = lax.broadcasted_iota(jnp.int32, (n, 1), 0)
    bias = jnp.where(key < length, 0.0, masked_score)

    @pl.loop(0, PAIRS)
    def _(hp):
        q_cols = pl.ds(pl.multiple_of(hp * 128, 128), 128)
        k2 = qkv[:, pl.ds(pl.multiple_of(D + hp * 128, 128), 128)]
        v2 = qkv[:, pl.ds(pl.multiple_of(2 * D + hp * 128, 128), 128)]

        rows = slice(0, n)
        q2 = qkv[rows, q_cols]
        o2 = None
        for j in range(2):
            s = dot_nt(with_one(q2, j), with_mask(k2, j, bias))
            e = jnp.exp(s - jnp.max(s, axis=-1, keepdims=True))
            p = e * (1.0 / jnp.sum(e, axis=-1, keepdims=True))
            probs[hp * 2 + j] = p
            p_low = p.astype(BF16)
            probs_low[hp * 2 + j] = p_low
            part = dot_nn(p_low, only_head(v2, j))
            o2 = part if o2 is None else o2 + part
        o_f[rows, q_cols] = o2

    row = lax.broadcasted_iota(jnp.int32, (n, 1), 0)
    g = cotangent(up_ref[...], weight, row < length)
    o_low = o_f[...].astype(BF16)
    out, dx1, d_o_v, dm_parts = mlp_both(
        x, o_low, g, mod, w_out, w_up, w_down, dw_out, dw_up, dw_down, mo, dm
    )
    out_s[...] = out
    save_out = pltpu.make_async_copy(out_s, out_all.at[which], sems.at[0])
    save_out.start()
    x1_s[...] = dx1
    d_o[...] = d_o_v

    @pl.loop(0, PAIRS)
    def _(hp):
        q_cols = pl.ds(pl.multiple_of(hp * 128, 128), 128)
        k_cols = pl.ds(pl.multiple_of(D + hp * 128, 128), 128)
        v_cols = pl.ds(pl.multiple_of(2 * D + hp * 128, 128), 128)
        k2 = qkv[:, k_cols]
        v2 = qkv[:, v_cols]

        q2 = qkv[:, q_cols]
        do2 = d_o[:, q_cols]
        prod = do2.astype(F32) * o_f[:, q_cols]
        dq2, dk2, dv2 = None, [], []
        for j in range(2):
            dp = dot_nt(do2, only_head(v2, j))
            delta = jnp.sum(only_head(prod, j), axis=-1, keepdims=True)
            ds = (probs[hp * 2 + j] * (dp - delta)).astype(BF16)
            part = dot_nn(ds, only_head(k2, j))
            dq2 = part if dq2 is None else dq2 + part
            dk2.append(dot_tn(ds, q2))
            dv2.append(dot_tn(probs_low[hp * 2 + j], do2))
        dqkv[:, q_cols] = (dq2 * score_scale).astype(BF16)
        dk2 = jnp.where(head_mask(0), dk2[0], dk2[1])
        dqkv[:, k_cols] = (dk2 * score_scale).astype(BF16)
        dqkv[:, v_cols] = jnp.where(head_mask(0), dv2[0], dv2[1]).astype(BF16)

    x = x_ref[...].astype(F32)
    hat, scale = norm_parts(x)
    a = (hat * (1.0 + mod[1]) + mod[0]).astype(BF16)
    grad, d_shift1, d_scale1 = project_back(
        dqkv[...], x1_s[...], hat, scale, a, mod, w_qkv, dw_qkv
    )
    x1_s[...] = grad
    save_grad = pltpu.make_async_copy(x1_s, grad_all.at[which], sems.at[1])
    save_grad.start()
    pad = jnp.zeros((2, D), F32)
    dmod_ref[...] = jnp.concatenate([d_shift1, d_scale1, *dm_parts, pad], axis=0)
    save_out.wait()
    save_grad.wait()


GRAD_SHAPES = tuple(jax.ShapeDtypeStruct(s, F32) for s in SHAPES[1:])


def short_call(which, scalars, tokens, upstream, mod, weights, prev):
    count, n, _ = tokens.shape
    in_specs = [SMEM] * 3 + [VMEM] * 7
    args = [*scalars, tokens, upstream, mod, *weights]
    aliases = {}
    if prev is not None:
        in_specs += [ANY, ANY]
        aliases = {len(args): 0, len(args) + 1: 1}
        args += list(prev)
    return pl.pallas_call(
        functools.partial(short_kernel, which),
        name="short" + str(which),
        out_shape=(
            jax.ShapeDtypeStruct(tokens.shape, BF16),
            jax.ShapeDtypeStruct(tokens.shape, F32),
            *GRAD_SHAPES,
            jax.ShapeDtypeStruct((8, D), F32),
        ),
        in_specs=in_specs,
        out_specs=(ANY, ANY) + (VMEM,) * 5,
        scratch_shapes=[
            pltpu.VMEM((n, 3 * D), BF16),
            pltpu.VMEM((HEADS, n, n), F32),
            pltpu.VMEM((n, D), F32),
            pltpu.VMEM((n, D), F32),
            pltpu.VMEM((n, D), F32),
            pltpu.VMEM((n, D), BF16),
            pltpu.VMEM((n, 3 * D), BF16),
            pltpu.VMEM((HEADS, n, n), BF16),
            pltpu.VMEM((n, D), F32),
            pltpu.VMEM((n, D), BF16),
            pltpu.SemaphoreType.DMA((2,)),
        ],
        input_output_aliases=aliases,
        compiler_params=PARAMS,
        cost_estimate=pl.CostEstimate(
            flops=8 * 10**9, bytes_accessed=2 * 10**7, transcendentals=2 * 10**6
        ),
    )(*args)


def long_in_kernel(labels_l, lengths_l, x_ref, mod_ref, w_qkv, q_ref, kv_ref):
    label, _ = own_long(labels_l, lengths_l)
    _, _, _, qkv = project(x_ref[0].astype(F32), mods_of(label, mod_ref), w_qkv)
    q_ref[...] = qkv[:, :D]
    kv_ref[...] = qkv[:, D:]


def long_in(scalars, tokens, mod, w_qkv):
    n = tokens.shape[1]
    return pl.pallas_call(
        long_in_kernel,
        name="long_in",
        out_shape=(
            jax.ShapeDtypeStruct((n, D), BF16),
            jax.ShapeDtypeStruct((n, 2 * D), BF16),
        ),
        in_specs=[SMEM] * 2 + [VMEM] * 3,
        out_specs=(VMEM,) * 2,
        compiler_params=PARAMS,
        cost_estimate=pl.CostEstimate(flops=10**8, bytes_accessed=10**6, transcendentals=0),
    )(*scalars, tokens, mod, w_qkv)


def long_mid_kernel(
    direct, share, labels_l, lengths_l, x_ref, up_ref, mod_ref, q_ref, kv,
    w_out, w_up, w_down,
    out_ref, dx1_ref, pack_ref, stat_ref, dw_out, dw_up, dw_down, dmod_ref,
    o_f, mo, dm,
):
    n = x_ref.shape[1]
    label, length = own_long(labels_l, lengths_l)
    mod = mods_of(label, mod_ref)
    bias = key_bias(direct, n, kv.shape[0], length)
    lane = lax.broadcasted_iota(jnp.int32, (1, 128), 1)
    stat_ref[...] = jnp.zeros_like(stat_ref)

    @pl.loop(0, PAIRS)
    def _(hp):
        q_cols = pl.ds(pl.multiple_of(hp * 128, 128), 128)
        k2 = kv[:, q_cols]
        v2 = kv[:, pl.ds(pl.multiple_of(D + hp * 128, 128), 128)]

        rows = slice(0, n)
        q2 = q_ref[rows, q_cols]
        o2 = None
        for j in range(2):
            s = dot_nt(with_one(q2, j), with_mask(k2, j, bias))
            top = jnp.max(s, axis=-1, keepdims=True)
            e = jnp.exp(s - top)
            total = jnp.sum(e, axis=-1, keepdims=True)
            part = dot_nn(e.astype(BF16), only_head(v2, j)) * (1.0 / total)
            o2 = part if o2 is None else o2 + part
            lse = top + jnp.log(total)
            stat_ref[rows, :] += jnp.where(lane == hp * 2 + j, lse, 0.0)
        o_f[rows, q_cols] = o2

    row = lax.axis_index("seq") * n + lax.broadcasted_iota(jnp.int32, (n, 1), 0)
    g = cotangent(up_ref[0], share[0], row < length)
    o_low = o_f[...].astype(BF16)
    out, dx1, d_o, dm_parts = mlp_both(
        x_ref[0].astype(F32), o_low, g, mod, w_out, w_up, w_down,
        dw_out, dw_up, dw_down, mo, dm,
    )
    out_ref[0] = out
    dx1_ref[...] = dx1
    pack_ref[:, :D] = q_ref[...]
    pack_ref[:, D : 2 * D] = d_o
    stat = stat_ref[...]
    for hp in range(PAIRS):
        cols = slice(hp * 128, (hp + 1) * 128)
        prod = d_o[:, cols].astype(F32) * o_f[:, cols]
        for j in range(2):
            delta = jnp.sum(only_head(prod, j), axis=-1, keepdims=True)
            stat = stat + jnp.where(lane == 8 + hp * 2 + j, delta, 0.0)
    stat_ref[...] = stat
    for i in range(3):
        term = stat.astype(BF16)
        pack_ref[:, 2 * D + i * 128 : 2 * D + (i + 1) * 128] = term
        stat = stat - term.astype(F32)
    pad = jnp.zeros((4, D), F32)
    dmod_ref[...] = jnp.concatenate([*dm_parts, pad], axis=0)


def long_mid(direct, scalars, tokens, *args):
    n = tokens.shape[1]
    return pl.pallas_call(
        functools.partial(long_mid_kernel, direct),
        name="long_mid",
        out_shape=(
            jax.ShapeDtypeStruct(tokens.shape, BF16),
            jax.ShapeDtypeStruct((n, D), F32),
            jax.ShapeDtypeStruct((n, 3 * D), BF16),
            jax.ShapeDtypeStruct((n, 128), F32),
            *GRAD_SHAPES[1:],
            jax.ShapeDtypeStruct((8, D), F32),
        ),
        in_specs=[SMEM] * 3 + [VMEM] * 8,
        out_specs=(VMEM,) * 8,
        scratch_shapes=[pltpu.VMEM((n, D), F32)] * 3,
        compiler_params=PARAMS,
        cost_estimate=pl.CostEstimate(
            flops=4 * 10**9, bytes_accessed=2 * 10**7, transcendentals=2 * 10**6
        ),
    )(*scalars, tokens, *args)


def long_back_kernel(
    direct, labels_l, lengths_l, x_ref, mod_ref, kv_own, kv, own_ref, stat_ref, pack_all,
    dx1_ref, w_qkv, grad_ref, dw_qkv, dmod_ref, dqkv, dk_s, dv_s, rows_all,
):
    n = x_ref.shape[1]
    total = kv.shape[0]
    label, length = own_long(labels_l, lengths_l)
    mod = mods_of(label, mod_ref)
    bias = key_bias(direct, n, total, length)
    lane = lax.broadcasted_iota(jnp.int32, (1, 128), 1)

    @pl.loop(0, total // n)
    def _(i):
        at = pl.ds(pl.multiple_of(i * n, n), n)
        terms = [pack_all[at, 2 * D + j * 128 : 2 * D + (j + 1) * 128] for j in range(3)]
        stat = terms[0].astype(F32) + (terms[1].astype(F32) + terms[2].astype(F32))
        rows_all[i] = stat.T[:16, :]

    @pl.loop(0, PAIRS)
    def _(hp):
        q_cols = pl.ds(pl.multiple_of(hp * 128, 128), 128)
        k_cols = pl.ds(pl.multiple_of(D + hp * 128, 128), 128)
        v_cols = pl.ds(pl.multiple_of(2 * D + hp * 128, 128), 128)
        k2 = kv[:, q_cols]
        v2 = kv[:, k_cols]

        rows = slice(0, n)
        q2 = own_ref[rows, q_cols]
        do2 = own_ref[rows, k_cols]
        stat = stat_ref[rows, :]
        dq2 = None
        for j in range(2):
            h = hp * 2 + j
            lse = jnp.sum(jnp.where(lane == h, stat, 0.0), axis=-1, keepdims=True)
            delta = jnp.sum(jnp.where(lane == 8 + h, stat, 0.0), axis=-1, keepdims=True)
            p = jnp.exp(dot_nt(with_one(q2, j), with_mask(k2, j, bias)) - lse)
            dp = dot_nt(do2, only_head(v2, j))
            ds = (p * (dp - delta)).astype(BF16)
            part = dot_nn(ds, only_head(k2, j))
            dq2 = part if dq2 is None else dq2 + part
        dqkv[rows, q_cols] = (dq2 * score_scale).astype(BF16)

        k_low = kv_own[:, q_cols] * jnp.asarray(score_scale, BF16)
        v_own = kv_own[:, k_cols]
        dk_s[...] = jnp.zeros_like(dk_s)
        dv_s[...] = jnp.zeros_like(dv_s)

        @pl.loop(0, total // n)
        def _(qc):
            rows = pl.ds(pl.multiple_of(qc * n, n), n)
            q2 = pack_all[rows, q_cols]
            do2 = pack_all[rows, k_cols]
            for j in range(2):
                h = hp * 2 + j
                lse = rows_all[qc, pl.ds(h, 1), :]
                delta = rows_all[qc, pl.ds(8 + h, 1), :]
                p = jnp.exp(dot_nt(only_head(k_low, j), q2) - lse)
                dp = dot_nt(only_head(v_own, j), do2)
                ds = (p * (dp - delta)).astype(BF16)
                dv_s[j] += dot_nn(p.astype(BF16), do2)
                dk_s[j] += dot_nn(ds, q2)

        row = lax.axis_index("seq") * n + lax.broadcasted_iota(jnp.int32, (n, 1), 0)
        ok = row < length
        dk2 = jnp.where(head_mask(0), dk_s[0], dk_s[1])
        dv2 = jnp.where(head_mask(0), dv_s[0], dv_s[1])
        dqkv[:, k_cols] = jnp.where(ok, dk2 * score_scale, 0.0).astype(BF16)
        dqkv[:, v_cols] = jnp.where(ok, dv2, 0.0).astype(BF16)

    hat, scale = norm_parts(x_ref[0].astype(F32))
    a = (hat * (1.0 + mod[1]) + mod[0]).astype(BF16)
    grad, d_shift1, d_scale1 = project_back(
        dqkv[...], dx1_ref[...], hat, scale, a, mod, w_qkv, dw_qkv
    )
    grad_ref[0] = grad
    pad = jnp.zeros((6, D), F32)
    dmod_ref[...] = jnp.concatenate([d_shift1, d_scale1, pad], axis=0)


def long_back(direct, scalars, tokens, *args):
    n = tokens.shape[1]
    return pl.pallas_call(
        functools.partial(long_back_kernel, direct),
        name="long_back",
        out_shape=(
            jax.ShapeDtypeStruct(tokens.shape, F32),
            GRAD_SHAPES[0],
            jax.ShapeDtypeStruct((8, D), F32),
        ),
        in_specs=[SMEM] * 2 + [VMEM] * 9,
        out_specs=(VMEM,) * 3,
        scratch_shapes=[
            pltpu.VMEM((n, 3 * D), BF16),
            pltpu.VMEM((2, n, 128), F32),
            pltpu.VMEM((2, n, 128), F32),
            pltpu.VMEM((args[2].shape[0] // n, 16, n), F32),
        ],
        compiler_params=PARAMS,
        cost_estimate=pl.CostEstimate(
            flops=4 * 10**9, bytes_accessed=10**7, transcendentals=4 * 10**6
        ),
    )(*scalars, tokens, *args)


def pack_kernel(
    nq, slots, base, labels_l, labels_s, lengths_l, lengths_s, table,
    dmod_mid, dmod_back, dmod_s0, dmod_s1, *refs,
):
    grads = refs[:12]
    outs = refs[12:-1]
    cond_s = refs[-1]
    part = TILE // nq
    for out in outs:
        out[...] = jnp.zeros_like(out)
    labels = [own_long(labels_l, lengths_l)[0]]
    labels += [own_short(i, 2, labels_s, lengths_s)[0] for i in range(2)]
    d_long = jnp.concatenate([dmod_back[:2, :], dmod_mid[:4, :]], axis=0)
    per_seq = (d_long, dmod_s0[:6, :], dmod_s1[:6, :])
    by_label = []
    for v in range(3):
        acc = None
        for s in range(3):
            term = jnp.where(labels[s] == v, per_seq[s], 0.0)
            acc = term if acc is None else acc + term
        by_label.append(acc)
    v = table[...]
    cond = (v * jax.nn.sigmoid(v)).astype(BF16).astype(F32)
    cond_t = jnp.concatenate([cond, jnp.zeros((5, D), F32)], axis=0).T
    seq = lax.axis_index("seq")
    turns = [(outs[0], 0, 0)]
    if nq > 1:
        turns = [
            (outs[r % 2], (seq ^ r) * part, (r // 2) * 2 * slots) for r in range(nq)
        ]
    cond_s[...] = cond_t

    @pl.loop(0, D // TILE)
    def _(r):
        for out, row, offset in turns:
            here = pl.ds(pl.multiple_of(r * TILE + row, part), part)
            col = [cond_s[here, v : v + 1] for v in range(3)]
            for c in range(6 * D // TILE):
                i, off = divmod(c, D // TILE)
                lanes = slice(off * TILE, (off + 1) * TILE)
                tile = None
                for v in range(3):
                    term = col[v] * by_label[v][i : i + 1, lanes]
                    tile = term if tile is None else tile + term
                out[base[r * (6 * D // TILE) + c] + offset] = tile.astype(BF16)

    first = SHAPES[0][0] * SHAPES[0][1] // TILE**2
    for m, (rows, cols) in enumerate(SHAPES[1:]):
        nr, nc = rows // TILE, cols // TILE
        terms = grads[3 * m : 3 * m + 3]

        @pl.loop(0, nr)
        def _(r, first=first, nc=nc, terms=terms):
            for c in range(nc):
                at = base[first + r * nc + c]
                lanes = slice(c * TILE, (c + 1) * TILE)
                for out, row, offset in turns:
                    here = pl.ds(pl.multiple_of(r * TILE + row, part), part)
                    v = terms[0][here, lanes] + terms[1][here, lanes] + terms[2][here, lanes]
                    out[at + offset] = v.astype(BF16)

        first += nr * nc


def pack(nq, slots, size, base, scalars, table, dmods, grads):
    part = TILE // nq
    halves = 2 if nq > 1 else 1
    return pl.pallas_call(
        functools.partial(pack_kernel, nq, slots),
        name="pack",
        out_shape=(jax.ShapeDtypeStruct((size, part, TILE), BF16),) * halves,
        in_specs=[SMEM] * 5 + [VMEM] * 17,
        out_specs=(VMEM,) * halves,
        scratch_shapes=[pltpu.VMEM((D, 8), F32)],
        compiler_params=PARAMS,
        cost_estimate=pl.CostEstimate(flops=10**7, bytes_accessed=3 * 10**7, transcendentals=0),
    )(base, *scalars, table, *dmods, *grads)


def halves(v):
    high = v.astype(BF16)
    return high, (v - high.astype(F32)).astype(BF16)


def dot3(dot, a, b):
    return dot(a[0], b[0]) + (dot(a[0], b[1]) + dot(a[1], b[0]))


def soap_kernel(nq, g_ref, left, right, first, second, master, gs, fn, sn, wn):
    many = range(master.shape[0])
    place = [0]
    if nq > 1:
        turn = [lax.axis_index("seq") ^ q for q in range(nq)]
        place = [(r % 2) * 2 + r // 2 for r in turn]
    g = [jnp.concatenate([g_ref[place[q], i] for q in range(nq)], axis=0) for i in many]
    for i in many:
        gs[i] = g[i].astype(F32)
    lo = [halves(left[i]) for i in many]
    ro = [halves(right[i]) for i in many]
    rot = [halves(dot_tn(lo[i][0], g[i]) + dot_tn(lo[i][1], g[i])) for i in many]
    rot = [dot3(dot_nn, rot[i], ro[i]) for i in many]
    step = []
    for i in many:
        f = beta_first * first[i] + (1.0 - beta_first) * rot[i]
        s = beta_second * second[i] + (1.0 - beta_second) * rot[i] * rot[i]
        fn[i] = f
        sn[i] = s
        bias_f = 1.0 - beta_first**STEP
        bias_s = 1.0 - beta_second**STEP
        step.append(halves(f / bias_f / (jnp.sqrt(s / bias_s) + adam_eps)))
    back = [halves(dot3(dot_nn, lo[i], step[i])) for i in many]
    back = [dot3(dot_nt, back[i], ro[i]) for i in many]
    for i in many:
        w = master[i]
        mean = jnp.mean(jnp.mean(w * w, axis=1, keepdims=True), axis=0, keepdims=True)
        spread = jnp.sqrt(mean + 1e-06)
        wn[i] = w - base_rate * spread * (back[i] + decay_rate * w)


def soap(nq, g, left, right, first, second, master):
    slots = master.shape[0]
    block = max(k for k in range(1, 12) if slots % k == 0)
    part = TILE // nq
    spec = pl.BlockSpec((block, TILE, TILE), lambda i: (i, 0, 0))
    g_spec = pl.BlockSpec((nq, block, part, TILE), lambda i: (0, i, 0, 0))
    shape = jax.ShapeDtypeStruct(master.shape, F32)
    return pl.pallas_call(
        functools.partial(soap_kernel, nq),
        name="soap",
        grid=(slots // block,),
        out_shape=(shape,) * 4,
        in_specs=[g_spec] + [spec] * 5,
        out_specs=(spec,) * 4,
        compiler_params=PARAMS,
        cost_estimate=pl.CostEstimate(flops=10**9, bytes_accessed=10**7, transcendentals=10**6),
    )(g, left, right, first, second, master)


class Grid:
    def __init__(self, n_dp, n_seq):
        self.direct = n_dp == 8 and n_seq == 4
        self.n = {"z": n_dp // 2, "y": 2, "x": n_seq // 2, "c": 2}
        self.n_dp = n_dp
        self.n_seq = n_seq
        self.nq = n_seq if self.direct else 1

    def shift(self, v, names, step=1):
        pairs = []
        for dp in range(self.n_dp):
            for seq in range(self.n_seq):
                at = {"z": dp // 2, "y": dp % 2, "x": seq // 2, "c": seq % 2}
                to = {k: (a + (k in names) * step) % self.n[k] for k, a in at.items()}
                pairs.append(((dp, seq), (to["z"] * 2 + to["y"], to["x"] * 2 + to["c"])))
        if not set(names) & set("zy"):
            axis, flat = "seq", {(a[1], b[1]) for a, b in pairs}
        elif not set(names) & set("xc"):
            axis, flat = "dp", {(a[0], b[0]) for a, b in pairs}
        else:
            axis = ("dp", "seq")
            flat = {tuple(d * self.n_seq + q for d, q in pair) for pair in pairs}
        return lax.ppermute(v, axis, sorted(flat))

    def over_seq(self, v):
        if not self.direct:
            return lax.all_gather(v, "seq", axis=0, tiled=True)
        return jnp.concatenate([v] + [self.shift(v, n) for n in ("x", "c", "xc")], axis=0)

    def table(self, tile_slot, slots, sign):
        if not self.direct:
            return tile_slot
        dp = lax.axis_index("dp")
        owner = tile_slot // slots
        rz = (sign * (dp // 2 - owner // 2)) % self.n["z"]
        ry = (dp ^ owner) & 1
        return (rz * (8 if sign > 0 else 4) + ry) * slots + tile_slot % slots

    def gather_slots(self, low):
        if not self.direct:
            return [lax.all_gather(low, "dp", axis=0, tiled=True)]
        part = TILE // self.nq
        piece = lax.dynamic_slice_in_dim(low, lax.axis_index("seq") * part, part, 1)
        k = piece.shape[0]
        by_y = self.shift(piece, "y")
        pieces = [piece, self.shift(piece, "z", 1), None, self.shift(piece, "z", 3)]
        by_y, piece = lax.optimization_barrier((by_y, piece))
        pieces[2] = self.shift(piece, "z", 2)
        out = []
        for r, piece in enumerate(pieces):
            if r == 2:
                near = [piece] + [self.shift(piece, n) for n in ("y", "x", "xy")]
            elif r == 1:
                by_x = self.shift(piece, "x")
                by_y = self.shift(jnp.concatenate([piece, by_x], axis=0), "y")
                near = [piece, by_y[:k], by_x, by_y[k:]]
            else:
                by_y = by_y if r == 0 else self.shift(piece, "y")
                by_y = jnp.concatenate([piece, by_y], axis=0)
                near = [by_y, self.shift(by_y, "x")]
            near = jnp.concatenate(near, axis=0)
            out += [near, self.shift(near, "c")]
        return out

    def reduce_slots(self, parts):
        if not self.direct:
            total = lax.psum_scatter(
                parts[0].astype(F32), "dp", scatter_dimension=0, tiled=True
            )
            return lax.psum(total, "seq")[None]
        k = parts[0].shape[0] // (4 * self.n["z"])
        other = self.shift(parts[1], "c")

        def blocks(r):
            rows = [slice(k * i, k * (i + 1)) for i in range(4 * r, 4 * r + 4)]
            return [parts[0][at].astype(F32) + other[at].astype(F32) for at in rows]

        acc = None
        for r in range(self.n["z"] - 1, -1, -1):
            block = blocks(r)
            total = block[0]
            for v, names in zip(block[1:], ("y", "x", "xy")):
                total = total + self.shift(v.astype(BF16), names).astype(F32)
            if acc is not None:
                total = total + self.shift(acc, "z").astype(F32)
            acc = total.astype(BF16)
        return self.over_seq(acc[None])


def local(
    tokens_long,
    tokens_short,
    upstream_long,
    upstream_short,
    interval_table,
    labels_long,
    labels_short,
    lengths_long,
    lengths_short,
    tile_slot,
    master_slots,
    basis_left,
    basis_right,
    first_moment,
    second_moment,
):
    grid = Grid(lax.axis_size("dp"), lax.axis_size("seq"))
    slots = master_slots.shape[0]
    nq, direct = grid.nq, grid.direct
    srcs = grid.gather_slots(master_slots.astype(BF16))
    base_in = grid.table(tile_slot, slots, 1)
    base_out = grid.table(tile_slot, slots, -1)
    base_in, base_out, srcs[0] = lax.optimization_barrier((base_in, base_out, srcs[0]))
    *weights, mod_table, share = unpack(
        nq, slots, srcs, base_in, (labels_long, labels_short), interval_table
    )
    w_qkv, w_out, w_up, w_down = weights

    def short(i, prev):
        return short_call(
            i, (share, labels_short, lengths_short), tokens_short, upstream_short,
            mod_table, weights, prev,
        )

    q, kv_own = long_in((labels_long, lengths_long), tokens_long, mod_table, w_qkv)
    kv = grid.over_seq(kv_own)
    res0 = short(0, None)
    kv, dmod_s0 = lax.optimization_barrier((kv, res0[6]))
    (
        out_long, dx1, packed, stat, dw_out_l, dw_up_l, dw_down_l, dmod_mid,
    ) = long_mid(
        direct, (share, labels_long, lengths_long), tokens_long, upstream_long,
        mod_table, q, kv, w_out, w_up, w_down,
    )
    packed_all = grid.over_seq(packed)
    prev0, prev1, dmod_mid = lax.optimization_barrier((res0[0], res0[1], dmod_mid))
    res1 = short(1, (prev0, prev1))
    packed_all, dmod_s1 = lax.optimization_barrier((packed_all, res1[6]))
    grad_long, dw_qkv_l, dmod_back = long_back(
        direct, (labels_long, lengths_long), tokens_long, mod_table, kv_own, kv, packed,
        stat, packed_all, dx1, w_qkv,
    )
    out_short, grad_short = res1[:2]
    terms = []
    for i, extra in enumerate((dw_qkv_l, dw_out_l, dw_up_l, dw_down_l)):
        terms += [res0[2 + i], res1[2 + i], extra]
    size = grid.n_dp * slots * (2 if direct else 1)
    parts = pack(
        nq, slots, size, base_out, (labels_long, labels_short, lengths_long, lengths_short),
        interval_table, (dmod_mid, dmod_back, dmod_s0, dmod_s1), terms,
    )
    g = grid.reduce_slots(parts)
    grad_slots, first_new, second_new, weight_new = soap(
        nq, g, basis_left, basis_right, first_moment, second_moment, master_slots
    )
    return (
        out_long, out_short, grad_long, grad_short,
        grad_slots, first_new, second_new, weight_new,
    )


def solution(mesh):
    rows = P(("dp", "seq"), None, None)
    cols = P("dp", "seq", None)
    slots = P("dp", None, None)
    return jax.shard_map(
        local,
        mesh=mesh,
        in_specs=(cols, rows, cols, rows) + (P(),) * 6 + (slots,) * 5,
        out_specs=(cols, rows, cols, rows) + (slots,) * 4,
        check_vma=False,
    )
```

```python
import functools

import jax
import jax.numpy as jnp
from jax import lax
from jax.experimental import pallas as pl
from jax.experimental.pallas import tpu as pltpu
from jax.sharding import PartitionSpec as P

D = 384
HEADS = 6
HD = 64
FF = 1536
STEP = 10
TILE = 128
PAIRS = HEADS // 2
SHAPES = ((D, 6 * D), (D, 3 * D), (D, D), (D, FF), (FF, D))

F32 = jnp.float32
BF16 = jnp.bfloat16
beta_first = 0.9
beta_second = 0.95
adam_eps = 1e-08
base_rate = 0.3
decay_rate = 0.01
norm_eps = 1e-06
masked_score = -1e30
score_scale = HD ** (-0.5)
FF_SHORT = 768
FF_LONG = 384


VMEM = pl.BlockSpec(memory_space=pltpu.VMEM)
SMEM = pl.BlockSpec(memory_space=pltpu.SMEM)
ANY = pl.BlockSpec(memory_space=pl.ANY)
PARAMS = pltpu.CompilerParams(vmem_limit_bytes=30 * 2**20)


def dot_nn(a, b):
    return lax.dot_general(a, b, (((1,), (0,)), ((), ())), preferred_element_type=F32)


def dot_nt(a, b):
    return lax.dot_general(a, b, (((1,), (1,)), ((), ())), preferred_element_type=F32)


def dot_tn(a, b):
    return lax.dot_general(a, b, (((0,), (0,)), ((), ())), preferred_element_type=F32)


def norm_parts(v):
    centered = v - jnp.mean(v, axis=-1, keepdims=True)
    scale = lax.rsqrt(jnp.mean(centered * centered, axis=-1, keepdims=True) + norm_eps)
    return centered * scale, scale


def norm_back(dy, hat, scale):
    return scale * (
        dy
        - jnp.mean(dy, axis=-1, keepdims=True)
        - hat * jnp.mean(dy * hat, axis=-1, keepdims=True)
    )


def col_sum(v):
    return jnp.sum(v, axis=0, keepdims=True)


def head_mask(j):
    lane = lax.broadcasted_iota(jnp.int32, (1, 2 * HD), 1)
    return (lane >= j * HD) & (lane < (j + 1) * HD)


def only_head(v, j):
    return jnp.where(head_mask(j), v, jnp.zeros_like(v))


def with_one(q2, j):
    lane = lax.broadcasted_iota(jnp.int32, (1, 2 * HD), 1)
    one = (lane == (1 - j) * HD).astype(q2.dtype)
    return jnp.where(head_mask(j), q2 * jnp.asarray(score_scale, q2.dtype), one)


def with_mask(k2, j, bias):
    lane = lax.broadcasted_iota(jnp.int32, (1, 2 * HD), 1)
    rest = jnp.where(lane == (1 - j) * HD, bias, 0.0).astype(k2.dtype)
    return jnp.where(head_mask(j), k2, rest)


def gelu_both(u):
    k0 = 0.7978845608028654
    sq = u * u
    t = jnp.tanh(u * (k0 + (k0 * 0.044715) * sq))
    half = 0.5 * (1.0 + t)
    slope = half + (0.5 * u) * (1.0 - t * t) * (k0 + (3.0 * k0 * 0.044715) * sq)
    return u * half, slope


def own_long(labels, lengths):
    at = lax.axis_index("dp")
    return labels[at], lengths[at]


def own_short(which, count, labels, lengths):
    at = (lax.axis_index("dp") * lax.axis_size("seq") + lax.axis_index("seq")) * count + which
    return labels[at], lengths[at]


def share_of(label, *tables):
    total = 0
    many = jnp.int32(0)
    for table in tables:
        size = table.shape[0]
        total += size

        def body(i, n, t=table):
            for j in range(8):
                n = n + (t[i * 8 + j] == label).astype(jnp.int32)
            return n

        many = lax.fori_loop(0, size // 8, body, many)
    return float(total) / (3.0 * many.astype(F32))


def key_bias(direct, rows, total, length):
    seq = lax.axis_index("seq")
    row = lax.broadcasted_iota(jnp.int32, (rows, 1), 0)
    out = []
    for i in range(total // rows):
        block = (seq ^ ((i % 2) * 2 + i // 2)) if direct else i
        out.append(jnp.where(block * rows + row < length, 0.0, masked_score))
    return jnp.concatenate(out, axis=0)


def unpack_kernel(nq, slots, sizes, base, labels_l, labels_s, table, *refs):
    srcs = refs[: len(sizes)]
    w_qkv, w_out, w_up, w_down, mod, share, buf, w_ada, sems = refs[len(sizes) :]
    part = TILE // nq
    copies = []
    start = 0
    for i, size in enumerate(sizes):
        cp = pltpu.make_async_copy(srcs[i], buf.at[pl.ds(start, size)], sems.at[i])
        cp.start()
        copies.append(cp)
        start += size
    seq = lax.axis_index("seq")
    offset = [0]
    if nq > 1:
        turn = [seq ^ q for q in range(nq)]
        offset = [((r % 2) * 4 + (r // 2) * 2) * slots for r in turn]
    at = (lax.axis_index("dp") * lax.axis_size("seq") + seq) * 2
    labels = (labels_l[lax.axis_index("dp")], labels_s[at], labels_s[at + 1])
    for i, label in enumerate(labels):
        share[i] = share_of(label, labels_l, labels_s)
    for cp in copies:
        cp.wait()
    first = 0
    for (rows, cols), dst in zip(SHAPES, (w_ada, w_qkv, w_out, w_up, w_down)):
        nr, nc = rows // TILE, cols // TILE

        @pl.loop(0, nr)
        def _(r, first=first, nc=nc, dst=dst):
            for c in range(nc):
                at = base[first + r * nc + c]
                for q in range(nq):
                    row = pl.multiple_of(r * TILE + q * part, part)
                    dst[pl.ds(row, part), c * TILE : (c + 1) * TILE] = buf[at + offset[q]]

        first += nr * nc
    v = table[...]
    cond = v * jax.nn.sigmoid(v)
    cond = jnp.concatenate([cond, jnp.zeros((5, D), F32)], axis=0).astype(BF16)
    mod[...] = dot_nn(cond, w_ada[...])


def unpack(nq, slots, srcs, base, labels, table):
    sizes = tuple(s.shape[0] for s in srcs)
    part = TILE // nq
    return pl.pallas_call(
        functools.partial(unpack_kernel, nq, slots, sizes),
        name="unpack",
        out_shape=tuple(jax.ShapeDtypeStruct(s, BF16) for s in SHAPES[1:])
        + (jax.ShapeDtypeStruct((8, 6 * D), F32), jax.ShapeDtypeStruct((4,), F32)),
        in_specs=[SMEM] * 3 + [VMEM] + [ANY] * len(srcs),
        out_specs=(VMEM,) * 5 + (SMEM,),
        scratch_shapes=[
            pltpu.VMEM((sum(sizes), part, TILE), BF16),
            pltpu.VMEM(SHAPES[0], BF16),
            pltpu.SemaphoreType.DMA((len(sizes),)),
        ],
        compiler_params=PARAMS,
        cost_estimate=pl.CostEstimate(flops=10**7, bytes_accessed=10**7, transcendentals=0),
    )(base, *labels, table, *srcs)


def mods_of(label, mod):
    row = mod[pl.ds(label, 1), :]
    return [row[:, i * D : (i + 1) * D] for i in range(6)]


def project(x, mod, w_qkv):
    hat, scale = norm_parts(x)
    a = (hat * (1.0 + mod[1]) + mod[0]).astype(BF16)
    return hat, scale, a, dot_nn(a, w_qkv[...]).astype(BF16)


def mlp_both(block, x, o_low, g, mod, w_out, w_up, w_down, dw_out, dw_up, dw_down, mo, dm):
    att = dot_nn(o_low, w_out[...])
    x1 = x + mod[2] * att
    hat, scale = norm_parts(x1)
    m = (hat * (1.0 + mod[4]) + mod[3]).astype(BF16)
    d_mo = (mod[5] * g).astype(BF16)
    mo[...] = jnp.zeros_like(mo)
    dm[...] = jnp.zeros_like(dm)

    @pl.loop(0, FF // block)
    def _(b):
        cols = pl.ds(pl.multiple_of(b * block, block), block)
        u = dot_nn(m, w_up[:, cols])
        d_r = dot_nt(d_mo, w_down[cols, :])
        act, slope = gelu_both(u)
        r = act.astype(BF16)
        du = (d_r * slope).astype(BF16)
        mo[...] += dot_nn(r, w_down[cols, :])
        dm[...] += dot_nt(du, w_up[:, cols])
        dw_up[:, cols] = dot_tn(m, du)
        dw_down[cols, :] = dot_tn(r, d_mo)

    mo_v = mo[...]
    out = (x1 + mod[5] * mo_v).astype(BF16)
    d_gate2 = col_sum(mo_v * g)
    dm_v = dm[...]
    d_shift2 = col_sum(dm_v)
    d_scale2 = col_sum(dm_v * hat)
    dx1 = g + norm_back(dm_v * (1.0 + mod[4]), hat, scale)
    d_att = (mod[2] * dx1).astype(BF16)
    d_gate1 = col_sum(att * dx1)
    dw_out[...] = dot_tn(o_low, d_att)
    d_o = dot_nt(d_att, w_out[...]).astype(BF16)
    return out, dx1, d_o, (d_gate1, d_shift2, d_scale2, d_gate2)


def project_back(dqkv, dx1, hat, scale, a, mod, w_qkv, dw_qkv):
    dw_qkv[...] = dot_tn(a, dqkv)
    d_a = dot_nt(dqkv, w_qkv[...])
    d_shift = col_sum(d_a)
    d_scale = col_sum(d_a * hat)
    return dx1 + norm_back(d_a * (1.0 + mod[1]), hat, scale), d_shift, d_scale


def cotangent(up, weight, rows_ok):
    return jnp.where(rows_ok, up.astype(F32) * weight, 0.0)


def short_kernel(
    which, share, labels_s, lengths_s, x_all, up_all, mod_ref,
    w_qkv, w_out, w_up, w_down, *refs,
):
    if which:
        refs = refs[2:]
    (
        out_all, grad_all, dw_qkv, dw_out, dw_up, dw_down, dmod_ref,
        qkv, probs, o_f, mo, dm, d_o, dqkv, probs_low, x1_s, out_s, up_ref, sems,
    ) = refs
    count, n, _ = x_all.shape
    x_ref = x_all.at[which]
    load_up = pltpu.make_async_copy(up_all.at[which], up_ref, sems.at[2])
    load_up.start()
    label, length = own_short(which, count, labels_s, lengths_s)
    weight = share[1 + which]
    mod = mods_of(label, mod_ref)
    x = x_ref[...].astype(F32)
    hat, scale, a, qkv_v = project(x, mod, w_qkv)
    qkv[...] = qkv_v
    key = lax.broadcasted_iota(jnp.int32, (n, 1), 0)
    bias = jnp.where(key < length, 0.0, masked_score)

    @pl.loop(0, PAIRS)
    def _(hp):
        q_cols = pl.ds(pl.multiple_of(hp * 128, 128), 128)
        k2 = qkv[:, pl.ds(pl.multiple_of(D + hp * 128, 128), 128)]
        v2 = qkv[:, pl.ds(pl.multiple_of(2 * D + hp * 128, 128), 128)]

        rows = slice(0, n)
        q2 = qkv[rows, q_cols]
        o2 = None
        for j in range(2):
            s = dot_nt(with_one(q2, j), with_mask(k2, j, bias))
            e = jnp.exp(s - jnp.max(s, axis=-1, keepdims=True))
            p = e * (1.0 / jnp.sum(e, axis=-1, keepdims=True))
            probs[hp * 2 + j] = p
            p_low = p.astype(BF16)
            probs_low[hp * 2 + j] = p_low
            part = dot_nn(p_low, only_head(v2, j))
            o2 = part if o2 is None else o2 + part
        o_f[rows, q_cols] = o2

    row = lax.broadcasted_iota(jnp.int32, (n, 1), 0)
    load_up.wait()
    g = cotangent(up_ref[...], weight, row < length)
    o_low = o_f[...].astype(BF16)
    out, dx1, d_o_v, dm_parts = mlp_both(
        FF_SHORT, x, o_low, g, mod, w_out, w_up, w_down, dw_out, dw_up, dw_down, mo, dm
    )
    out_s[...] = out
    save_out = pltpu.make_async_copy(out_s, out_all.at[which], sems.at[0])
    save_out.start()
    x1_s[...] = dx1
    d_o[...] = d_o_v

    @pl.loop(0, PAIRS)
    def _(hp):
        q_cols = pl.ds(pl.multiple_of(hp * 128, 128), 128)
        k_cols = pl.ds(pl.multiple_of(D + hp * 128, 128), 128)
        v_cols = pl.ds(pl.multiple_of(2 * D + hp * 128, 128), 128)
        k2 = qkv[:, k_cols]
        v2 = qkv[:, v_cols]

        q2 = qkv[:, q_cols]
        do2 = d_o[:, q_cols]
        prod = do2.astype(F32) * o_f[:, q_cols]
        dq2, dk2, dv2 = None, [], []
        for j in range(2):
            dp = dot_nt(do2, only_head(v2, j))
            delta = jnp.sum(only_head(prod, j), axis=-1, keepdims=True)
            ds = (probs[hp * 2 + j] * (dp - delta)).astype(BF16)
            part = dot_nn(ds, only_head(k2, j))
            dq2 = part if dq2 is None else dq2 + part
            dk2.append(dot_tn(ds, q2))
            dv2.append(dot_tn(probs_low[hp * 2 + j], do2))
        dqkv[:, q_cols] = (dq2 * score_scale).astype(BF16)
        dk2 = jnp.where(head_mask(0), dk2[0], dk2[1])
        dqkv[:, k_cols] = (dk2 * score_scale).astype(BF16)
        dqkv[:, v_cols] = jnp.where(head_mask(0), dv2[0], dv2[1]).astype(BF16)

    x = x_ref[...].astype(F32)
    hat, scale = norm_parts(x)
    a = (hat * (1.0 + mod[1]) + mod[0]).astype(BF16)
    grad, d_shift1, d_scale1 = project_back(
        dqkv[...], x1_s[...], hat, scale, a, mod, w_qkv, dw_qkv
    )
    x1_s[...] = grad
    save_grad = pltpu.make_async_copy(x1_s, grad_all.at[which], sems.at[1])
    save_grad.start()
    pad = jnp.zeros((2, D), F32)
    dmod_ref[...] = jnp.concatenate([d_shift1, d_scale1, *dm_parts, pad], axis=0)
    save_out.wait()
    save_grad.wait()


GRAD_SHAPES = tuple(jax.ShapeDtypeStruct(s, F32) for s in SHAPES[1:])


def short_call(which, scalars, tokens, upstream, mod, weights, prev):
    count, n, _ = tokens.shape
    in_specs = [SMEM] * 3 + [VMEM, ANY] + [VMEM] * 5
    args = [*scalars, tokens, upstream, mod, *weights]
    aliases = {}
    if prev is not None:
        in_specs += [ANY, ANY]
        aliases = {len(args): 0, len(args) + 1: 1}
        args += list(prev)
    return pl.pallas_call(
        functools.partial(short_kernel, which),
        name="short" + str(which),
        out_shape=(
            jax.ShapeDtypeStruct(tokens.shape, BF16),
            jax.ShapeDtypeStruct(tokens.shape, F32),
            *GRAD_SHAPES,
            jax.ShapeDtypeStruct((8, D), F32),
        ),
        in_specs=in_specs,
        out_specs=(ANY, ANY) + (VMEM,) * 5,
        scratch_shapes=[
            pltpu.VMEM((n, 3 * D), BF16),
            pltpu.VMEM((HEADS, n, n), F32),
            pltpu.VMEM((n, D), F32),
            pltpu.VMEM((n, D), F32),
            pltpu.VMEM((n, D), F32),
            pltpu.VMEM((n, D), BF16),
            pltpu.VMEM((n, 3 * D), BF16),
            pltpu.VMEM((HEADS, n, n), BF16),
            pltpu.VMEM((n, D), F32),
            pltpu.VMEM((n, D), BF16),
            pltpu.VMEM((n, D), BF16),
            pltpu.SemaphoreType.DMA((3,)),
        ],
        input_output_aliases=aliases,
        compiler_params=PARAMS,
        cost_estimate=pl.CostEstimate(
            flops=8 * 10**9, bytes_accessed=2 * 10**7, transcendentals=2 * 10**6
        ),
    )(*args)


def long_in_kernel(labels_l, lengths_l, x_ref, mod_ref, w_qkv, q_ref, kv_ref):
    label, _ = own_long(labels_l, lengths_l)
    _, _, _, qkv = project(x_ref[0].astype(F32), mods_of(label, mod_ref), w_qkv)
    q_ref[...] = qkv[:, :D]
    kv_ref[...] = qkv[:, D:]


def long_in(scalars, tokens, mod, w_qkv):
    n = tokens.shape[1]
    return pl.pallas_call(
        long_in_kernel,
        name="long_in",
        out_shape=(
            jax.ShapeDtypeStruct((n, D), BF16),
            jax.ShapeDtypeStruct((n, 2 * D), BF16),
        ),
        in_specs=[SMEM] * 2 + [VMEM] * 3,
        out_specs=(VMEM,) * 2,
        compiler_params=PARAMS,
        cost_estimate=pl.CostEstimate(flops=10**8, bytes_accessed=10**6, transcendentals=0),
    )(*scalars, tokens, mod, w_qkv)


def long_mid_kernel(
    direct, share, labels_l, lengths_l, x_ref, up_all, mod_ref, q_ref, kv,
    w_out, w_up, w_down,
    out_ref, dx1_ref, pack_ref, stat_ref, dw_out, dw_up, dw_down, dmod_ref,
    o_f, mo, dm, up_ref, sem,
):
    n = x_ref.shape[1]
    load_up = pltpu.make_async_copy(up_all.at[0], up_ref, sem.at[0])
    load_up.start()
    label, length = own_long(labels_l, lengths_l)
    mod = mods_of(label, mod_ref)
    bias = key_bias(direct, n, kv.shape[0], length)
    lane = lax.broadcasted_iota(jnp.int32, (1, 128), 1)
    stat_ref[...] = jnp.zeros_like(stat_ref)

    @pl.loop(0, PAIRS)
    def _(hp):
        q_cols = pl.ds(pl.multiple_of(hp * 128, 128), 128)
        k2 = kv[:, q_cols]
        v2 = kv[:, pl.ds(pl.multiple_of(D + hp * 128, 128), 128)]

        rows = slice(0, n)
        q2 = q_ref[rows, q_cols]
        o2 = None
        for j in range(2):
            s = dot_nt(with_one(q2, j), with_mask(k2, j, bias))
            top = jnp.max(s, axis=-1, keepdims=True)
            e = jnp.exp(s - top)
            total = jnp.sum(e, axis=-1, keepdims=True)
            part = dot_nn(e.astype(BF16), only_head(v2, j)) * (1.0 / total)
            o2 = part if o2 is None else o2 + part
            lse = top + jnp.log(total)
            stat_ref[rows, :] += jnp.where(lane == hp * 2 + j, lse, 0.0)
        o_f[rows, q_cols] = o2

    row = lax.axis_index("seq") * n + lax.broadcasted_iota(jnp.int32, (n, 1), 0)
    load_up.wait()
    g = cotangent(up_ref[...], share[0], row < length)
    o_low = o_f[...].astype(BF16)
    out, dx1, d_o, dm_parts = mlp_both(
        FF_LONG, x_ref[0].astype(F32), o_low, g, mod, w_out, w_up, w_down,
        dw_out, dw_up, dw_down, mo, dm,
    )
    out_ref[0] = out
    dx1_ref[...] = dx1
    pack_ref[:, :D] = q_ref[...]
    pack_ref[:, D : 2 * D] = d_o
    stat = stat_ref[...]
    for hp in range(PAIRS):
        cols = slice(hp * 128, (hp + 1) * 128)
        prod = d_o[:, cols].astype(F32) * o_f[:, cols]
        for j in range(2):
            delta = jnp.sum(only_head(prod, j), axis=-1, keepdims=True)
            stat = stat + jnp.where(lane == 8 + hp * 2 + j, delta, 0.0)
    stat_ref[...] = stat
    together = None
    for i in range(3):
        term = stat.astype(BF16).astype(F32)
        stat = stat - term
        together = term if i == 0 else together + pltpu.roll(term, 16 * i, 1)
    pack_ref[:, 2 * D :] = together.astype(BF16)
    pad = jnp.zeros((4, D), F32)
    dmod_ref[...] = jnp.concatenate([*dm_parts, pad], axis=0)


def long_mid(direct, scalars, tokens, *args):
    n = tokens.shape[1]
    return pl.pallas_call(
        functools.partial(long_mid_kernel, direct),
        name="long_mid",
        out_shape=(
            jax.ShapeDtypeStruct(tokens.shape, BF16),
            jax.ShapeDtypeStruct((n, D), F32),
            jax.ShapeDtypeStruct((n, 2 * D + 128), BF16),
            jax.ShapeDtypeStruct((n, 128), F32),
            *GRAD_SHAPES[1:],
            jax.ShapeDtypeStruct((8, D), F32),
        ),
        in_specs=[SMEM] * 3 + [VMEM, ANY] + [VMEM] * 6,
        out_specs=(VMEM,) * 8,
        scratch_shapes=[pltpu.VMEM((n, D), F32)] * 3
        + [pltpu.VMEM((n, D), BF16), pltpu.SemaphoreType.DMA((1,))],
        compiler_params=PARAMS,
        cost_estimate=pl.CostEstimate(
            flops=4 * 10**9, bytes_accessed=2 * 10**7, transcendentals=2 * 10**6
        ),
    )(*scalars, tokens, *args)


def long_back_kernel(
    direct, labels_l, lengths_l, x_ref, mod_ref, kv_own, kv, own_ref, stat_ref, pack_all,
    dx1_ref, w_qkv, grad_ref, dw_qkv, dmod_ref, dqkv, dk_s, dv_s, rows_all,
):
    n = x_ref.shape[1]
    total = kv.shape[0]
    label, length = own_long(labels_l, lengths_l)
    mod = mods_of(label, mod_ref)
    bias = key_bias(direct, n, total, length)
    lane = lax.broadcasted_iota(jnp.int32, (1, 128), 1)

    @pl.loop(0, total // n)
    def _(i):
        at = pl.ds(pl.multiple_of(i * n, n), n)
        terms = pack_all[at, 2 * D :].astype(F32).T
        rows_all[i] = terms[:16, :] + (terms[16:32, :] + terms[32:48, :])

    @pl.loop(0, PAIRS)
    def _(hp):
        q_cols = pl.ds(pl.multiple_of(hp * 128, 128), 128)
        k_cols = pl.ds(pl.multiple_of(D + hp * 128, 128), 128)
        v_cols = pl.ds(pl.multiple_of(2 * D + hp * 128, 128), 128)
        k2 = kv[:, q_cols]
        v2 = kv[:, k_cols]

        rows = slice(0, n)
        q2 = own_ref[rows, q_cols]
        do2 = own_ref[rows, k_cols]
        stat = stat_ref[rows, :]
        dq2 = None
        for j in range(2):
            h = hp * 2 + j
            lse = jnp.sum(jnp.where(lane == h, stat, 0.0), axis=-1, keepdims=True)
            delta = jnp.sum(jnp.where(lane == 8 + h, stat, 0.0), axis=-1, keepdims=True)
            p = jnp.exp(dot_nt(with_one(q2, j), with_mask(k2, j, bias)) - lse)
            dp = dot_nt(do2, only_head(v2, j))
            ds = (p * (dp - delta)).astype(BF16)
            part = dot_nn(ds, only_head(k2, j))
            dq2 = part if dq2 is None else dq2 + part
        dqkv[rows, q_cols] = (dq2 * score_scale).astype(BF16)

        k_low = kv_own[:, q_cols] * jnp.asarray(score_scale, BF16)
        v_own = kv_own[:, k_cols]
        dk_s[...] = jnp.zeros_like(dk_s)
        dv_s[...] = jnp.zeros_like(dv_s)

        @pl.loop(0, total // (2 * n))
        def _(qc):
            rows = pl.ds(pl.multiple_of(qc * 2 * n, 2 * n), 2 * n)
            q2 = pack_all[rows, q_cols]
            do2 = pack_all[rows, k_cols]
            for j in range(2):
                h = hp * 2 + j
                stat = [
                    jnp.concatenate(
                        [rows_all[2 * qc + i, pl.ds(at, 1), :] for i in range(2)], axis=1
                    )
                    for at in (h, 8 + h)
                ]
                lse, delta = stat
                p = jnp.exp(dot_nt(only_head(k_low, j), q2) - lse)
                dp = dot_nt(only_head(v_own, j), do2)
                ds = (p * (dp - delta)).astype(BF16)
                dv_s[j] += dot_nn(p.astype(BF16), do2)
                dk_s[j] += dot_nn(ds, q2)

        row = lax.axis_index("seq") * n + lax.broadcasted_iota(jnp.int32, (n, 1), 0)
        ok = row < length
        dk2 = jnp.where(head_mask(0), dk_s[0], dk_s[1])
        dv2 = jnp.where(head_mask(0), dv_s[0], dv_s[1])
        dqkv[:, k_cols] = jnp.where(ok, dk2 * score_scale, 0.0).astype(BF16)
        dqkv[:, v_cols] = jnp.where(ok, dv2, 0.0).astype(BF16)

    hat, scale = norm_parts(x_ref[0].astype(F32))
    a = (hat * (1.0 + mod[1]) + mod[0]).astype(BF16)
    grad, d_shift1, d_scale1 = project_back(
        dqkv[...], dx1_ref[...], hat, scale, a, mod, w_qkv, dw_qkv
    )
    grad_ref[0] = grad
    pad = jnp.zeros((6, D), F32)
    dmod_ref[...] = jnp.concatenate([d_shift1, d_scale1, pad], axis=0)


def long_back(direct, scalars, tokens, *args):
    n = tokens.shape[1]
    return pl.pallas_call(
        functools.partial(long_back_kernel, direct),
        name="long_back",
        out_shape=(
            jax.ShapeDtypeStruct(tokens.shape, F32),
            GRAD_SHAPES[0],
            jax.ShapeDtypeStruct((8, D), F32),
        ),
        in_specs=[SMEM] * 2 + [VMEM] * 9,
        out_specs=(VMEM,) * 3,
        scratch_shapes=[
            pltpu.VMEM((n, 3 * D), BF16),
            pltpu.VMEM((2, n, 128), F32),
            pltpu.VMEM((2, n, 128), F32),
            pltpu.VMEM((args[2].shape[0] // n, 16, n), F32),
        ],
        compiler_params=PARAMS,
        cost_estimate=pl.CostEstimate(
            flops=4 * 10**9, bytes_accessed=10**7, transcendentals=4 * 10**6
        ),
    )(*scalars, tokens, *args)


def pack_kernel(
    nq, slots, base, labels_l, labels_s, lengths_l, lengths_s, table,
    dmod_mid, dmod_back, dmod_s0, dmod_s1, *refs,
):
    grads = refs[:12]
    outs = refs[12:-1]
    cond_s = refs[-1]
    part = TILE // nq
    for out in outs:
        out[...] = jnp.zeros_like(out)
    labels = [own_long(labels_l, lengths_l)[0]]
    labels += [own_short(i, 2, labels_s, lengths_s)[0] for i in range(2)]
    d_long = jnp.concatenate([dmod_back[:2, :], dmod_mid[:4, :]], axis=0)
    per_seq = (d_long, dmod_s0[:6, :], dmod_s1[:6, :])
    by_label = []
    for v in range(3):
        acc = None
        for s in range(3):
            term = jnp.where(labels[s] == v, per_seq[s], 0.0)
            acc = term if acc is None else acc + term
        by_label.append(acc)
    v = table[...]
    cond = (v * jax.nn.sigmoid(v)).astype(BF16).astype(F32)
    cond_t = jnp.concatenate([cond, jnp.zeros((5, D), F32)], axis=0).T
    seq = lax.axis_index("seq")
    turns = [(outs[0], 0, 0)]
    if nq > 1:
        turns = [
            (outs[0] if r % 2 == 0 else None, (seq ^ r) * part, (r // 2) * 2 * slots)
            for r in range(nq)
        ]

    def put(out, at, v):
        if out is not None:
            out[at] = v
            return
        edge = outs[1].shape[0] - 1
        outs[1][jnp.where(at < edge, at, edge)] = v
        outs[2][jnp.where(at < edge, edge, at - edge)] = v

    cond_s[...] = cond_t

    @pl.loop(0, D // TILE)
    def _(r):
        for out, row, offset in turns:
            here = pl.ds(pl.multiple_of(r * TILE + row, part), part)
            col = [cond_s[here, v : v + 1] for v in range(3)]
            for c in range(6 * D // TILE):
                i, off = divmod(c, D // TILE)
                lanes = slice(off * TILE, (off + 1) * TILE)
                tile = None
                for v in range(3):
                    term = col[v] * by_label[v][i : i + 1, lanes]
                    tile = term if tile is None else tile + term
                put(out, base[r * (6 * D // TILE) + c] + offset, tile.astype(BF16))

    first = SHAPES[0][0] * SHAPES[0][1] // TILE**2
    for m, (rows, cols) in enumerate(SHAPES[1:]):
        nr, nc = rows // TILE, cols // TILE
        terms = grads[3 * m : 3 * m + 3]

        @pl.loop(0, nr)
        def _(r, first=first, nc=nc, terms=terms):
            for c in range(nc):
                at = base[first + r * nc + c]
                lanes = slice(c * TILE, (c + 1) * TILE)
                for out, row, offset in turns:
                    here = pl.ds(pl.multiple_of(r * TILE + row, part), part)
                    v = terms[0][here, lanes] + terms[1][here, lanes] + terms[2][here, lanes]
                    put(out, at + offset, v.astype(BF16))

        first += nr * nc


def pack(nq, slots, size, base, scalars, table, dmods, grads):
    part = TILE // nq
    sizes = (size, size // 2 + 1, size // 2 + 1) if nq > 1 else (size,)
    return pl.pallas_call(
        functools.partial(pack_kernel, nq, slots),
        name="pack",
        out_shape=tuple(jax.ShapeDtypeStruct((n, part, TILE), BF16) for n in sizes),
        in_specs=[SMEM] * 5 + [VMEM] * 17,
        out_specs=(VMEM,) * len(sizes),
        scratch_shapes=[pltpu.VMEM((D, 8), F32)],
        compiler_params=PARAMS,
        cost_estimate=pl.CostEstimate(flops=10**7, bytes_accessed=3 * 10**7, transcendentals=0),
    )(base, *scalars, table, *dmods, *grads)


def halves(v):
    high = v.astype(BF16)
    return high, (v - high.astype(F32)).astype(BF16)


def dot3(dot, a, b):
    return dot(a[0], b[0]) + (dot(a[0], b[1]) + dot(a[1], b[0]))


def soap_kernel(nq, g_ref, left, right, first, second, master, gs, fn, sn, wn):
    many = range(master.shape[0])
    place = [0]
    if nq > 1:
        turn = [lax.axis_index("seq") ^ q for q in range(nq)]
        place = [(r % 2) * 2 + r // 2 for r in turn]
    g = [jnp.concatenate([g_ref[place[q], i] for q in range(nq)], axis=0) for i in many]
    for i in many:
        gs[i] = g[i].astype(F32)
    lo = [halves(left[i]) for i in many]
    ro = [halves(right[i]) for i in many]
    rot = [halves(dot_tn(lo[i][0], g[i]) + dot_tn(lo[i][1], g[i])) for i in many]
    rot = [dot3(dot_nn, rot[i], ro[i]) for i in many]
    step = []
    for i in many:
        f = beta_first * first[i] + (1.0 - beta_first) * rot[i]
        s = beta_second * second[i] + (1.0 - beta_second) * rot[i] * rot[i]
        fn[i] = f
        sn[i] = s
        bias_f = 1.0 - beta_first**STEP
        bias_s = 1.0 - beta_second**STEP
        step.append(halves(f / bias_f / (jnp.sqrt(s / bias_s) + adam_eps)))
    back = [halves(dot3(dot_nn, lo[i], step[i])) for i in many]
    back = [dot3(dot_nt, back[i], ro[i]) for i in many]
    for i in many:
        w = master[i]
        mean = jnp.mean(jnp.mean(w * w, axis=1, keepdims=True), axis=0, keepdims=True)
        spread = jnp.sqrt(mean + 1e-06)
        wn[i] = w - base_rate * spread * (back[i] + decay_rate * w)


def soap(nq, g, left, right, first, second, master):
    slots = master.shape[0]
    block = max(k for k in range(1, 12) if slots % k == 0)
    part = TILE // nq
    spec = pl.BlockSpec((block, TILE, TILE), lambda i: (i, 0, 0))
    g_spec = pl.BlockSpec((nq, block, part, TILE), lambda i: (0, i, 0, 0))
    shape = jax.ShapeDtypeStruct(master.shape, F32)
    return pl.pallas_call(
        functools.partial(soap_kernel, nq),
        name="soap",
        grid=(slots // block,),
        out_shape=(shape,) * 4,
        in_specs=[g_spec] + [spec] * 5,
        out_specs=(spec,) * 4,
        compiler_params=PARAMS,
        cost_estimate=pl.CostEstimate(flops=10**9, bytes_accessed=10**7, transcendentals=10**6),
    )(g, left, right, first, second, master)


class Grid:
    def __init__(self, n_dp, n_seq):
        self.direct = n_dp == 8 and n_seq == 4
        self.n = {"z": n_dp // 2, "y": 2, "x": n_seq // 2, "c": 2}
        self.n_dp = n_dp
        self.n_seq = n_seq
        self.nq = n_seq if self.direct else 1

    def shift(self, v, names, step=1):
        pairs = []
        for dp in range(self.n_dp):
            for seq in range(self.n_seq):
                at = {"z": dp // 2, "y": dp % 2, "x": seq // 2, "c": seq % 2}
                to = {k: (a + (k in names) * step) % self.n[k] for k, a in at.items()}
                pairs.append(((dp, seq), (to["z"] * 2 + to["y"], to["x"] * 2 + to["c"])))
        if not set(names) & set("zy"):
            axis, flat = "seq", {(a[1], b[1]) for a, b in pairs}
        elif not set(names) & set("xc"):
            axis, flat = "dp", {(a[0], b[0]) for a, b in pairs}
        else:
            axis = ("dp", "seq")
            flat = {tuple(d * self.n_seq + q for d, q in pair) for pair in pairs}
        return lax.ppermute(v, axis, sorted(flat))

    def over_seq(self, v):
        if not self.direct:
            return lax.all_gather(v, "seq", axis=0, tiled=True)
        return jnp.concatenate([v] + [self.shift(v, n) for n in ("x", "c", "xc")], axis=0)

    def table(self, tile_slot, slots, sign):
        if not self.direct:
            return tile_slot
        dp = lax.axis_index("dp")
        owner = tile_slot // slots
        rz = (sign * (dp // 2 - owner // 2)) % self.n["z"]
        ry = (dp ^ owner) & 1
        return (rz * (8 if sign > 0 else 4) + ry) * slots + tile_slot % slots

    def gather_slots(self, low):
        if not self.direct:
            return [lax.all_gather(low, "dp", axis=0, tiled=True)]
        part = TILE // self.nq
        piece = lax.dynamic_slice_in_dim(low, lax.axis_index("seq") * part, part, 1)
        k = piece.shape[0]
        by_y = self.shift(piece, "y")
        pieces = [piece, self.shift(piece, "z", 1), None, self.shift(piece, "z", 3)]
        by_y, piece = lax.optimization_barrier((by_y, piece))
        pieces[2] = self.shift(piece, "z", 2)
        out = []
        for r, piece in enumerate(pieces):
            if r == 2:
                near = [piece] + [self.shift(piece, n) for n in ("y", "x", "xy")]
            elif r == 1:
                by_x = self.shift(piece, "x")
                by_y = self.shift(jnp.concatenate([piece, by_x], axis=0), "y")
                near = [piece, by_y[:k], by_x, by_y[k:]]
            else:
                by_y = by_y if r == 0 else self.shift(piece, "y")
                by_y = jnp.concatenate([piece, by_y], axis=0)
                near = [by_y, self.shift(by_y, "x")]
            near = jnp.concatenate(near, axis=0)
            out += [near, self.shift(near, "c")]
        return out

    def reduce_slots(self, parts):
        if not self.direct:
            total = lax.psum_scatter(
                parts[0].astype(F32), "dp", scatter_dimension=0, tiled=True
            )
            return lax.psum(total, "seq")[None]
        k = parts[0].shape[0] // (4 * self.n["z"])
        other = [self.shift(parts[2], "c"), self.shift(parts[1], "c")]
        half = parts[0].shape[0] // 2

        def blocks(r):
            rows = [slice(k * i, k * (i + 1)) for i in range(4 * r, 4 * r + 4)]
            far = other[0 if r >= self.n["z"] // 2 else 1]
            down = half if r >= self.n["z"] // 2 else 0
            back = [far[at.start - down : at.stop - down] for at in rows]
            return [parts[0][at].astype(F32) + v.astype(F32) for at, v in zip(rows, back)]

        acc = None
        for r in range(self.n["z"] - 1, -1, -1):
            block = blocks(r)
            total = block[0]
            for v, names in zip(block[1:], ("y", "x", "xy")):
                total = total + self.shift(v.astype(BF16), names).astype(F32)
            if acc is not None:
                total = total + self.shift(acc, "z").astype(F32)
            acc = total.astype(BF16)
        return self.over_seq(acc[None])


def local(
    tokens_long,
    tokens_short,
    upstream_long,
    upstream_short,
    interval_table,
    labels_long,
    labels_short,
    lengths_long,
    lengths_short,
    tile_slot,
    master_slots,
    basis_left,
    basis_right,
    first_moment,
    second_moment,
):
    grid = Grid(lax.axis_size("dp"), lax.axis_size("seq"))
    slots = master_slots.shape[0]
    nq, direct = grid.nq, grid.direct
    srcs = grid.gather_slots(master_slots.astype(BF16))
    base_in = grid.table(tile_slot, slots, 1)
    base_out = grid.table(tile_slot, slots, -1)
    base_in, base_out, srcs[0] = lax.optimization_barrier((base_in, base_out, srcs[0]))
    *weights, mod_table, share = unpack(
        nq, slots, srcs, base_in, (labels_long, labels_short), interval_table
    )
    w_qkv, w_out, w_up, w_down = weights

    def short(i, prev):
        return short_call(
            i, (share, labels_short, lengths_short), tokens_short, upstream_short,
            mod_table, weights, prev,
        )

    q, kv_own = long_in((labels_long, lengths_long), tokens_long, mod_table, w_qkv)
    kv = grid.over_seq(kv_own)
    res0 = short(0, None)
    kv, dmod_s0 = lax.optimization_barrier((kv, res0[6]))
    (
        out_long, dx1, packed, stat, dw_out_l, dw_up_l, dw_down_l, dmod_mid,
    ) = long_mid(
        direct, (share, labels_long, lengths_long), tokens_long, upstream_long,
        mod_table, q, kv, w_out, w_up, w_down,
    )
    packed_all = grid.over_seq(packed)
    prev0, prev1, dmod_mid = lax.optimization_barrier((res0[0], res0[1], dmod_mid))
    res1 = short(1, (prev0, prev1))
    packed_all, dmod_s1 = lax.optimization_barrier((packed_all, res1[6]))
    grad_long, dw_qkv_l, dmod_back = long_back(
        direct, (labels_long, lengths_long), tokens_long, mod_table, kv_own, kv, packed,
        stat, packed_all, dx1, w_qkv,
    )
    out_short, grad_short = res1[:2]
    terms = []
    for i, extra in enumerate((dw_qkv_l, dw_out_l, dw_up_l, dw_down_l)):
        terms += [res0[2 + i], res1[2 + i], extra]
    size = grid.n_dp * slots * (2 if direct else 1)
    parts = pack(
        nq, slots, size, base_out, (labels_long, labels_short, lengths_long, lengths_short),
        interval_table, (dmod_mid, dmod_back, dmod_s0, dmod_s1), terms,
    )
    g = grid.reduce_slots(parts)
    grad_slots, first_new, second_new, weight_new = soap(
        nq, g, basis_left, basis_right, first_moment, second_moment, master_slots
    )
    return (
        out_long, out_short, grad_long, grad_short,
        grad_slots, first_new, second_new, weight_new,
    )


def solution(mesh):
    rows = P(("dp", "seq"), None, None)
    cols = P("dp", "seq", None)
    slots = P("dp", None, None)
    return jax.shard_map(
        local,
        mesh=mesh,
        in_specs=(cols, rows, cols, rows) + (P(),) * 6 + (slots,) * 5,
        out_specs=(cols, rows, cols, rows) + (slots,) * 4,
        check_vma=False,
    )
```

```python
import functools

import jax
import jax.numpy as jnp
from jax import lax
from jax.experimental import pallas as pl
from jax.experimental.pallas import tpu as pltpu
from jax.sharding import PartitionSpec as P

D = 384
HEADS = 6
HD = 64
FF = 1536
STEP = 10
TILE = 128
PAIRS = HEADS // 2
SHAPES = ((D, 6 * D), (D, 3 * D), (D, D), (D, FF), (FF, D))

F32 = jnp.float32
BF16 = jnp.bfloat16
beta_first = 0.9
beta_second = 0.95
adam_eps = 1e-08
base_rate = 0.3
decay_rate = 0.01
norm_eps = 1e-06
masked_score = -1e30
score_scale = HD ** (-0.5)
FF_SHORT = 768
FF_LONG = 384


VMEM = pl.BlockSpec(memory_space=pltpu.VMEM)
SMEM = pl.BlockSpec(memory_space=pltpu.SMEM)
ANY = pl.BlockSpec(memory_space=pl.ANY)
PARAMS = pltpu.CompilerParams(vmem_limit_bytes=30 * 2**20)


def dot_nn(a, b):
    return lax.dot_general(a, b, (((1,), (0,)), ((), ())), preferred_element_type=F32)


def dot_nt(a, b):
    return lax.dot_general(a, b, (((1,), (1,)), ((), ())), preferred_element_type=F32)


def dot_tn(a, b):
    return lax.dot_general(a, b, (((0,), (0,)), ((), ())), preferred_element_type=F32)


def norm_parts(v):
    centered = v - jnp.mean(v, axis=-1, keepdims=True)
    scale = lax.rsqrt(jnp.mean(centered * centered, axis=-1, keepdims=True) + norm_eps)
    return centered * scale, scale


def norm_back(dy, hat, scale):
    return scale * (
        dy
        - jnp.mean(dy, axis=-1, keepdims=True)
        - hat * jnp.mean(dy * hat, axis=-1, keepdims=True)
    )


def col_sum(v):
    return jnp.sum(v, axis=0, keepdims=True)


def head_mask(j):
    lane = lax.broadcasted_iota(jnp.int32, (1, 2 * HD), 1)
    return (lane >= j * HD) & (lane < (j + 1) * HD)


def only_head(v, j):
    return jnp.where(head_mask(j), v, jnp.zeros_like(v))


def with_one(q2, j):
    lane = lax.broadcasted_iota(jnp.int32, (1, 2 * HD), 1)
    one = (lane == (1 - j) * HD).astype(q2.dtype)
    return jnp.where(head_mask(j), q2 * jnp.asarray(score_scale, q2.dtype), one)


def with_mask(k2, j, bias):
    lane = lax.broadcasted_iota(jnp.int32, (1, 2 * HD), 1)
    rest = jnp.where(lane == (1 - j) * HD, bias, 0.0).astype(k2.dtype)
    return jnp.where(head_mask(j), k2, rest)


def gelu_both(u):
    k0 = 0.7978845608028654
    sq = u * u
    t = jnp.tanh(u * (k0 + (k0 * 0.044715) * sq))
    half = 0.5 * (1.0 + t)
    slope = half + (0.5 * u) * (1.0 - t * t) * (k0 + (3.0 * k0 * 0.044715) * sq)
    return u * half, slope


def own_long(labels, lengths):
    at = lax.axis_index("dp")
    return labels[at], lengths[at]


def own_short(which, count, labels, lengths):
    at = (lax.axis_index("dp") * lax.axis_size("seq") + lax.axis_index("seq")) * count + which
    return labels[at], lengths[at]


def share_of(label, *tables):
    total = 0
    many = jnp.int32(0)
    for table in tables:
        size = table.shape[0]
        total += size

        def body(i, n, t=table):
            for j in range(8):
                n = n + (t[i * 8 + j] == label).astype(jnp.int32)
            return n

        many = lax.fori_loop(0, size // 8, body, many)
    return float(total) / (3.0 * many.astype(F32))


def key_bias(direct, rows, total, length):
    seq = lax.axis_index("seq")
    row = lax.broadcasted_iota(jnp.int32, (rows, 1), 0)
    out = []
    for i in range(total // rows):
        block = (seq ^ ((i % 2) * 2 + i // 2)) if direct else i
        out.append(jnp.where(block * rows + row < length, 0.0, masked_score))
    return jnp.concatenate(out, axis=0)


def unpack_kernel(nq, slots, sizes, base, labels_l, labels_s, table, *refs):
    srcs = refs[: len(sizes)]
    w_qkv, w_out, w_up, w_down, mod, share, buf, w_ada, sems = refs[len(sizes) :]
    part = TILE // nq
    copies = []
    start = 0
    for i, size in enumerate(sizes):
        cp = pltpu.make_async_copy(srcs[i], buf.at[pl.ds(start, size)], sems.at[i])
        cp.start()
        copies.append(cp)
        start += size
    seq = lax.axis_index("seq")
    offset = [0]
    if nq > 1:
        turn = [seq ^ q for q in range(nq)]
        offset = [((r % 2) * 4 + (r // 2) * 2) * slots for r in turn]
    at = (lax.axis_index("dp") * lax.axis_size("seq") + seq) * 2
    labels = (labels_l[lax.axis_index("dp")], labels_s[at], labels_s[at + 1])
    for i, label in enumerate(labels):
        share[i] = share_of(label, labels_l, labels_s)
    for cp in copies:
        cp.wait()
    first = 0
    for (rows, cols), dst in zip(SHAPES, (w_ada, w_qkv, w_out, w_up, w_down)):
        nr, nc = rows // TILE, cols // TILE

        @pl.loop(0, nr)
        def _(r, first=first, nc=nc, dst=dst):
            for c in range(nc):
                at = base[first + r * nc + c]
                for q in range(nq):
                    row = pl.multiple_of(r * TILE + q * part, part)
                    dst[pl.ds(row, part), c * TILE : (c + 1) * TILE] = buf[at + offset[q]]

        first += nr * nc
    v = table[...]
    cond = v * jax.nn.sigmoid(v)
    cond = jnp.concatenate([cond, jnp.zeros((5, D), F32)], axis=0).astype(BF16)
    mod[...] = dot_nn(cond, w_ada[...])


def unpack(nq, slots, srcs, base, labels, table):
    sizes = tuple(s.shape[0] for s in srcs)
    part = TILE // nq
    return pl.pallas_call(
        functools.partial(unpack_kernel, nq, slots, sizes),
        name="unpack",
        out_shape=tuple(jax.ShapeDtypeStruct(s, BF16) for s in SHAPES[1:])
        + (jax.ShapeDtypeStruct((8, 6 * D), F32), jax.ShapeDtypeStruct((4,), F32)),
        in_specs=[SMEM] * 3 + [VMEM] + [ANY] * len(srcs),
        out_specs=(VMEM,) * 5 + (SMEM,),
        scratch_shapes=[
            pltpu.VMEM((sum(sizes), part, TILE), BF16),
            pltpu.VMEM(SHAPES[0], BF16),
            pltpu.SemaphoreType.DMA((len(sizes),)),
        ],
        compiler_params=PARAMS,
        cost_estimate=pl.CostEstimate(flops=10**7, bytes_accessed=10**7, transcendentals=0),
    )(base, *labels, table, *srcs)


def mods_of(label, mod):
    row = mod[pl.ds(label, 1), :]
    return [row[:, i * D : (i + 1) * D] for i in range(6)]


def project(x, mod, w_qkv):
    hat, scale = norm_parts(x)
    a = (hat * (1.0 + mod[1]) + mod[0]).astype(BF16)
    return hat, scale, a, dot_nn(a, w_qkv[...]).astype(BF16)


def mlp_both(block, x, o_low, g, mod, w_out, w_up, w_down, dw_out, dw_up, dw_down, mo, dm):
    att = dot_nn(o_low, w_out[...])
    x1 = x + mod[2] * att
    hat, scale = norm_parts(x1)
    m = (hat * (1.0 + mod[4]) + mod[3]).astype(BF16)
    d_mo = (mod[5] * g).astype(BF16)
    mo[...] = jnp.zeros_like(mo)
    dm[...] = jnp.zeros_like(dm)

    @pl.loop(0, FF // block)
    def _(b):
        cols = pl.ds(pl.multiple_of(b * block, block), block)
        u = dot_nn(m, w_up[:, cols])
        d_r = dot_nt(d_mo, w_down[cols, :])
        act, slope = gelu_both(u)
        r = act.astype(BF16)
        du = (d_r * slope).astype(BF16)
        mo[...] += dot_nn(r, w_down[cols, :])
        dm[...] += dot_nt(du, w_up[:, cols])
        dw_up[:, cols] = dot_tn(m, du)
        dw_down[cols, :] = dot_tn(r, d_mo)

    mo_v = mo[...]
    out = (x1 + mod[5] * mo_v).astype(BF16)
    d_gate2 = col_sum(mo_v * g)
    dm_v = dm[...]
    d_shift2 = col_sum(dm_v)
    d_scale2 = col_sum(dm_v * hat)
    dx1 = g + norm_back(dm_v * (1.0 + mod[4]), hat, scale)
    d_att = (mod[2] * dx1).astype(BF16)
    d_gate1 = col_sum(att * dx1)
    dw_out[...] = dot_tn(o_low, d_att)
    d_o = dot_nt(d_att, w_out[...]).astype(BF16)
    return out, dx1, d_o, (d_gate1, d_shift2, d_scale2, d_gate2)


def project_back(dqkv, dx1, hat, scale, a, mod, w_qkv, dw_qkv):
    dw_qkv[...] = dot_tn(a, dqkv)
    d_a = dot_nt(dqkv, w_qkv[...])
    d_shift = col_sum(d_a)
    d_scale = col_sum(d_a * hat)
    return dx1 + norm_back(d_a * (1.0 + mod[1]), hat, scale), d_shift, d_scale


def cotangent(up, weight, rows_ok):
    return jnp.where(rows_ok, up.astype(F32) * weight, 0.0)


def short_kernel(
    which, share, labels_s, lengths_s, x_all, up_all, mod_ref,
    w_qkv, w_out, w_up, w_down, *refs,
):
    if which:
        refs = refs[2:]
    (
        out_all, grad_all, dw_qkv, dw_out, dw_up, dw_down, dmod_ref,
        qkv, probs, o_f, mo, dm, d_o, dqkv, probs_low, x1_s, out_s, up_ref, sems,
    ) = refs
    count, n, _ = x_all.shape
    x_ref = x_all.at[which]
    load_up = pltpu.make_async_copy(up_all.at[which], up_ref, sems.at[2])
    load_up.start()
    label, length = own_short(which, count, labels_s, lengths_s)
    weight = share[1 + which]
    mod = mods_of(label, mod_ref)
    x = x_ref[...].astype(F32)
    hat, scale, a, qkv_v = project(x, mod, w_qkv)
    qkv[...] = qkv_v
    key = lax.broadcasted_iota(jnp.int32, (n, 1), 0)
    bias = jnp.where(key < length, 0.0, masked_score)

    @pl.loop(0, PAIRS)
    def _(hp):
        q_cols = pl.ds(pl.multiple_of(hp * 128, 128), 128)
        k2 = qkv[:, pl.ds(pl.multiple_of(D + hp * 128, 128), 128)]
        v2 = qkv[:, pl.ds(pl.multiple_of(2 * D + hp * 128, 128), 128)]

        rows = slice(0, n)
        q2 = qkv[rows, q_cols]
        o2 = None
        for j in range(2):
            s = dot_nt(with_one(q2, j), with_mask(k2, j, bias))
            e = jnp.exp(s - jnp.max(s, axis=-1, keepdims=True))
            p = e * (1.0 / jnp.sum(e, axis=-1, keepdims=True))
            probs[hp * 2 + j] = p
            p_low = p.astype(BF16)
            probs_low[hp * 2 + j] = p_low
            part = dot_nn(p_low, only_head(v2, j))
            o2 = part if o2 is None else o2 + part
        o_f[rows, q_cols] = o2

    row = lax.broadcasted_iota(jnp.int32, (n, 1), 0)
    load_up.wait()
    g = cotangent(up_ref[...], weight, row < length)
    o_low = o_f[...].astype(BF16)
    out, dx1, d_o_v, dm_parts = mlp_both(
        FF_SHORT, x, o_low, g, mod, w_out, w_up, w_down, dw_out, dw_up, dw_down, mo, dm
    )
    out_s[...] = out
    save_out = pltpu.make_async_copy(out_s, out_all.at[which], sems.at[0])
    save_out.start()
    x1_s[...] = dx1
    d_o[...] = d_o_v

    @pl.loop(0, PAIRS)
    def _(hp):
        q_cols = pl.ds(pl.multiple_of(hp * 128, 128), 128)
        k_cols = pl.ds(pl.multiple_of(D + hp * 128, 128), 128)
        v_cols = pl.ds(pl.multiple_of(2 * D + hp * 128, 128), 128)
        k2 = qkv[:, k_cols]
        v2 = qkv[:, v_cols]

        q2 = qkv[:, q_cols]
        do2 = d_o[:, q_cols]
        prod = do2.astype(F32) * o_f[:, q_cols]
        dq2, dk2, dv2 = None, [], []
        for j in range(2):
            dp = dot_nt(do2, only_head(v2, j))
            delta = jnp.sum(only_head(prod, j), axis=-1, keepdims=True)
            ds = (probs[hp * 2 + j] * (dp - delta)).astype(BF16)
            part = dot_nn(ds, only_head(k2, j))
            dq2 = part if dq2 is None else dq2 + part
            dk2.append(dot_tn(ds, q2))
            dv2.append(dot_tn(probs_low[hp * 2 + j], do2))
        dqkv[:, q_cols] = (dq2 * score_scale).astype(BF16)
        dk2 = jnp.where(head_mask(0), dk2[0], dk2[1])
        dqkv[:, k_cols] = (dk2 * score_scale).astype(BF16)
        dqkv[:, v_cols] = jnp.where(head_mask(0), dv2[0], dv2[1]).astype(BF16)

    x = x_ref[...].astype(F32)
    hat, scale = norm_parts(x)
    a = (hat * (1.0 + mod[1]) + mod[0]).astype(BF16)
    grad, d_shift1, d_scale1 = project_back(
        dqkv[...], x1_s[...], hat, scale, a, mod, w_qkv, dw_qkv
    )
    x1_s[...] = grad
    save_grad = pltpu.make_async_copy(x1_s, grad_all.at[which], sems.at[1])
    save_grad.start()
    pad = jnp.zeros((2, D), F32)
    dmod_ref[...] = jnp.concatenate([d_shift1, d_scale1, *dm_parts, pad], axis=0)
    save_out.wait()
    save_grad.wait()


GRAD_SHAPES = tuple(jax.ShapeDtypeStruct(s, F32) for s in SHAPES[1:])


def short_call(which, scalars, tokens, upstream, mod, weights, prev):
    count, n, _ = tokens.shape
    in_specs = [SMEM] * 3 + [VMEM, ANY] + [VMEM] * 5
    args = [*scalars, tokens, upstream, mod, *weights]
    aliases = {}
    if prev is not None:
        in_specs += [ANY, ANY]
        aliases = {len(args): 0, len(args) + 1: 1}
        args += list(prev)
    return pl.pallas_call(
        functools.partial(short_kernel, which),
        name="short" + str(which),
        out_shape=(
            jax.ShapeDtypeStruct(tokens.shape, BF16),
            jax.ShapeDtypeStruct(tokens.shape, F32),
            *GRAD_SHAPES,
            jax.ShapeDtypeStruct((8, D), F32),
        ),
        in_specs=in_specs,
        out_specs=(ANY, ANY) + (VMEM,) * 5,
        scratch_shapes=[
            pltpu.VMEM((n, 3 * D), BF16),
            pltpu.VMEM((HEADS, n, n), F32),
            pltpu.VMEM((n, D), F32),
            pltpu.VMEM((n, D), F32),
            pltpu.VMEM((n, D), F32),
            pltpu.VMEM((n, D), BF16),
            pltpu.VMEM((n, 3 * D), BF16),
            pltpu.VMEM((HEADS, n, n), BF16),
            pltpu.VMEM((n, D), F32),
            pltpu.VMEM((n, D), BF16),
            pltpu.VMEM((n, D), BF16),
            pltpu.SemaphoreType.DMA((3,)),
        ],
        input_output_aliases=aliases,
        compiler_params=PARAMS,
        cost_estimate=pl.CostEstimate(
            flops=8 * 10**9, bytes_accessed=2 * 10**7, transcendentals=2 * 10**6
        ),
    )(*args)


def long_in_kernel(labels_l, lengths_l, x_ref, mod_ref, w_qkv, q_ref, kv_ref):
    label, _ = own_long(labels_l, lengths_l)
    _, _, _, qkv = project(x_ref[0].astype(F32), mods_of(label, mod_ref), w_qkv)
    q_ref[...] = qkv[:, :D]
    kv_ref[...] = qkv[:, D:]


def long_in(scalars, tokens, mod, w_qkv):
    n = tokens.shape[1]
    return pl.pallas_call(
        long_in_kernel,
        name="long_in",
        out_shape=(
            jax.ShapeDtypeStruct((n, D), BF16),
            jax.ShapeDtypeStruct((n, 2 * D), BF16),
        ),
        in_specs=[SMEM] * 2 + [VMEM] * 3,
        out_specs=(VMEM,) * 2,
        compiler_params=PARAMS,
        cost_estimate=pl.CostEstimate(flops=10**8, bytes_accessed=10**6, transcendentals=0),
    )(*scalars, tokens, mod, w_qkv)


def long_mid_kernel(
    direct, share, labels_l, lengths_l, x_ref, up_all, mod_ref, q_ref, kv,
    w_out, w_up, w_down,
    out_ref, dx1_ref, pack_ref, stat_ref, dw_out, dw_up, dw_down, dmod_ref,
    o_f, mo, dm, up_ref, sem,
):
    n = x_ref.shape[1]
    load_up = pltpu.make_async_copy(up_all.at[0], up_ref, sem.at[0])
    load_up.start()
    label, length = own_long(labels_l, lengths_l)
    mod = mods_of(label, mod_ref)
    bias = key_bias(direct, n, kv.shape[0], length)
    lane = lax.broadcasted_iota(jnp.int32, (1, 128), 1)
    stat_ref[...] = jnp.zeros_like(stat_ref)

    @pl.loop(0, PAIRS)
    def _(hp):
        q_cols = pl.ds(pl.multiple_of(hp * 128, 128), 128)
        k2 = kv[:, q_cols]
        v2 = kv[:, pl.ds(pl.multiple_of(D + hp * 128, 128), 128)]

        rows = slice(0, n)
        q2 = q_ref[rows, q_cols]
        o2 = None
        for j in range(2):
            s = dot_nt(with_one(q2, j), with_mask(k2, j, bias))
            top = jnp.max(s, axis=-1, keepdims=True)
            e = jnp.exp(s - top)
            total = jnp.sum(e, axis=-1, keepdims=True)
            part = dot_nn(e.astype(BF16), only_head(v2, j)) * (1.0 / total)
            o2 = part if o2 is None else o2 + part
            lse = top + jnp.log(total)
            stat_ref[rows, :] += jnp.where(lane == hp * 2 + j, lse, 0.0)
        o_f[rows, q_cols] = o2

    row = lax.axis_index("seq") * n + lax.broadcasted_iota(jnp.int32, (n, 1), 0)
    load_up.wait()
    g = cotangent(up_ref[...], share[0], row < length)
    o_low = o_f[...].astype(BF16)
    out, dx1, d_o, dm_parts = mlp_both(
        FF_LONG, x_ref[0].astype(F32), o_low, g, mod, w_out, w_up, w_down,
        dw_out, dw_up, dw_down, mo, dm,
    )
    out_ref[0] = out
    dx1_ref[...] = dx1
    pack_ref[:, :D] = q_ref[...]
    pack_ref[:, D : 2 * D] = d_o
    stat = stat_ref[...]
    for hp in range(PAIRS):
        cols = slice(hp * 128, (hp + 1) * 128)
        prod = d_o[:, cols].astype(F32) * o_f[:, cols]
        for j in range(2):
            delta = jnp.sum(only_head(prod, j), axis=-1, keepdims=True)
            stat = stat + jnp.where(lane == 8 + hp * 2 + j, delta, 0.0)
    stat_ref[...] = stat
    together = None
    for i in range(3):
        term = stat.astype(BF16).astype(F32)
        stat = stat - term
        together = term if i == 0 else together + pltpu.roll(term, 16 * i, 1)
    pack_ref[:, 2 * D :] = together.astype(BF16)
    pad = jnp.zeros((4, D), F32)
    dmod_ref[...] = jnp.concatenate([*dm_parts, pad], axis=0)


def long_mid(direct, scalars, tokens, *args):
    n = tokens.shape[1]
    return pl.pallas_call(
        functools.partial(long_mid_kernel, direct),
        name="long_mid",
        out_shape=(
            jax.ShapeDtypeStruct(tokens.shape, BF16),
            jax.ShapeDtypeStruct((n, D), F32),
            jax.ShapeDtypeStruct((n, 2 * D + 128), BF16),
            jax.ShapeDtypeStruct((n, 128), F32),
            *GRAD_SHAPES[1:],
            jax.ShapeDtypeStruct((8, D), F32),
        ),
        in_specs=[SMEM] * 3 + [VMEM, ANY] + [VMEM] * 6,
        out_specs=(VMEM,) * 8,
        scratch_shapes=[pltpu.VMEM((n, D), F32)] * 3
        + [pltpu.VMEM((n, D), BF16), pltpu.SemaphoreType.DMA((1,))],
        compiler_params=PARAMS,
        cost_estimate=pl.CostEstimate(
            flops=4 * 10**9, bytes_accessed=2 * 10**7, transcendentals=2 * 10**6
        ),
    )(*scalars, tokens, *args)


def long_back_kernel(
    direct, labels_l, lengths_l, x_ref, mod_ref, kv_own, kv, own_ref, stat_ref, pack_all,
    dx1_ref, w_qkv, grad_ref, dw_qkv, dmod_ref, dqkv, dk_s, dv_s, rows_all,
):
    n = x_ref.shape[1]
    total = kv.shape[0]
    label, length = own_long(labels_l, lengths_l)
    mod = mods_of(label, mod_ref)
    bias = key_bias(direct, n, total, length)
    lane = lax.broadcasted_iota(jnp.int32, (1, 128), 1)

    @pl.loop(0, total // n)
    def _(i):
        at = pl.ds(pl.multiple_of(i * n, n), n)
        terms = pack_all[at, 2 * D :].astype(F32).T
        rows_all[i] = terms[:16, :] + (terms[16:32, :] + terms[32:48, :])

    @pl.loop(0, PAIRS)
    def _(hp):
        q_cols = pl.ds(pl.multiple_of(hp * 128, 128), 128)
        k_cols = pl.ds(pl.multiple_of(D + hp * 128, 128), 128)
        v_cols = pl.ds(pl.multiple_of(2 * D + hp * 128, 128), 128)
        k2 = kv[:, q_cols]
        v2 = kv[:, k_cols]

        rows = slice(0, n)
        q2 = own_ref[rows, q_cols]
        do2 = own_ref[rows, k_cols]
        stat = stat_ref[rows, :]
        dq2 = None
        for j in range(2):
            h = hp * 2 + j
            lse = jnp.sum(jnp.where(lane == h, stat, 0.0), axis=-1, keepdims=True)
            delta = jnp.sum(jnp.where(lane == 8 + h, stat, 0.0), axis=-1, keepdims=True)
            p = jnp.exp(dot_nt(with_one(q2, j), with_mask(k2, j, bias)) - lse)
            dp = dot_nt(do2, only_head(v2, j))
            ds = (p * (dp - delta)).astype(BF16)
            part = dot_nn(ds, only_head(k2, j))
            dq2 = part if dq2 is None else dq2 + part
        dqkv[rows, q_cols] = (dq2 * score_scale).astype(BF16)

        k_low = kv_own[:, q_cols] * jnp.asarray(score_scale, BF16)
        v_own = kv_own[:, k_cols]
        dk_s[...] = jnp.zeros_like(dk_s)
        dv_s[...] = jnp.zeros_like(dv_s)

        @pl.loop(0, total // (2 * n))
        def _(qc):
            rows = pl.ds(pl.multiple_of(qc * 2 * n, 2 * n), 2 * n)
            q2 = pack_all[rows, q_cols]
            do2 = pack_all[rows, k_cols]
            for j in range(2):
                h = hp * 2 + j
                stat = [
                    jnp.concatenate(
                        [rows_all[2 * qc + i, pl.ds(at, 1), :] for i in range(2)], axis=1
                    )
                    for at in (h, 8 + h)
                ]
                lse, delta = stat
                p = jnp.exp(dot_nt(only_head(k_low, j), q2) - lse)
                dp = dot_nt(only_head(v_own, j), do2)
                ds = (p * (dp - delta)).astype(BF16)
                dv_s[j] += dot_nn(p.astype(BF16), do2)
                dk_s[j] += dot_nn(ds, q2)

        row = lax.axis_index("seq") * n + lax.broadcasted_iota(jnp.int32, (n, 1), 0)
        ok = row < length
        dk2 = jnp.where(head_mask(0), dk_s[0], dk_s[1])
        dv2 = jnp.where(head_mask(0), dv_s[0], dv_s[1])
        dqkv[:, k_cols] = jnp.where(ok, dk2 * score_scale, 0.0).astype(BF16)
        dqkv[:, v_cols] = jnp.where(ok, dv2, 0.0).astype(BF16)

    hat, scale = norm_parts(x_ref[0].astype(F32))
    a = (hat * (1.0 + mod[1]) + mod[0]).astype(BF16)
    grad, d_shift1, d_scale1 = project_back(
        dqkv[...], dx1_ref[...], hat, scale, a, mod, w_qkv, dw_qkv
    )
    grad_ref[0] = grad
    pad = jnp.zeros((6, D), F32)
    dmod_ref[...] = jnp.concatenate([d_shift1, d_scale1, pad], axis=0)


def long_back(direct, scalars, tokens, *args):
    n = tokens.shape[1]
    return pl.pallas_call(
        functools.partial(long_back_kernel, direct),
        name="long_back",
        out_shape=(
            jax.ShapeDtypeStruct(tokens.shape, F32),
            GRAD_SHAPES[0],
            jax.ShapeDtypeStruct((8, D), F32),
        ),
        in_specs=[SMEM] * 2 + [VMEM] * 9,
        out_specs=(VMEM,) * 3,
        scratch_shapes=[
            pltpu.VMEM((n, 3 * D), BF16),
            pltpu.VMEM((2, n, 128), F32),
            pltpu.VMEM((2, n, 128), F32),
            pltpu.VMEM((args[2].shape[0] // n, 16, n), F32),
        ],
        compiler_params=PARAMS,
        cost_estimate=pl.CostEstimate(
            flops=4 * 10**9, bytes_accessed=10**7, transcendentals=4 * 10**6
        ),
    )(*scalars, tokens, *args)


def pack_kernel(
    nq, slots, base, labels_l, labels_s, lengths_l, lengths_s, table,
    dmod_mid, dmod_back, dmod_s0, dmod_s1, *refs,
):
    grads = refs[:12]
    outs = refs[12:-1]
    cond_s = refs[-1]
    part = TILE // nq
    for out in outs:
        out[...] = jnp.zeros_like(out)
    labels = [own_long(labels_l, lengths_l)[0]]
    labels += [own_short(i, 2, labels_s, lengths_s)[0] for i in range(2)]
    d_long = jnp.concatenate([dmod_back[:2, :], dmod_mid[:4, :]], axis=0)
    per_seq = (d_long, dmod_s0[:6, :], dmod_s1[:6, :])
    by_label = []
    for v in range(3):
        acc = None
        for s in range(3):
            term = jnp.where(labels[s] == v, per_seq[s], 0.0)
            acc = term if acc is None else acc + term
        by_label.append(acc)
    v = table[...]
    cond = (v * jax.nn.sigmoid(v)).astype(BF16).astype(F32)
    cond_t = jnp.concatenate([cond, jnp.zeros((5, D), F32)], axis=0).T
    seq = lax.axis_index("seq")
    turns = [(outs[0], 0, 0)]
    if nq > 1:
        turns = [
            (outs[0] if r % 2 == 0 else None, (seq ^ r) * part, (r // 2) * 2 * slots)
            for r in range(nq)
        ]

    def put(out, at, v):
        if out is not None:
            out[at] = v
            return
        edge = outs[1].shape[0] - 1
        outs[1][jnp.where(at < edge, at, edge)] = v
        outs[2][jnp.where(at < edge, edge, at - edge)] = v

    cond_s[...] = cond_t

    @pl.loop(0, D // TILE)
    def _(r):
        for out, row, offset in turns:
            here = pl.ds(pl.multiple_of(r * TILE + row, part), part)
            col = [cond_s[here, v : v + 1] for v in range(3)]
            for c in range(6 * D // TILE):
                i, off = divmod(c, D // TILE)
                lanes = slice(off * TILE, (off + 1) * TILE)
                tile = None
                for v in range(3):
                    term = col[v] * by_label[v][i : i + 1, lanes]
                    tile = term if tile is None else tile + term
                put(out, base[r * (6 * D // TILE) + c] + offset, tile.astype(BF16))

    first = SHAPES[0][0] * SHAPES[0][1] // TILE**2
    for m, (rows, cols) in enumerate(SHAPES[1:]):
        nr, nc = rows // TILE, cols // TILE
        terms = grads[3 * m : 3 * m + 3]

        @pl.loop(0, nr)
        def _(r, first=first, nc=nc, terms=terms):
            for c in range(nc):
                at = base[first + r * nc + c]
                lanes = slice(c * TILE, (c + 1) * TILE)
                for out, row, offset in turns:
                    here = pl.ds(pl.multiple_of(r * TILE + row, part), part)
                    v = terms[0][here, lanes] + terms[1][here, lanes] + terms[2][here, lanes]
                    put(out, at + offset, v.astype(BF16))

        first += nr * nc


def pack(nq, slots, size, base, scalars, table, dmods, grads):
    part = TILE // nq
    sizes = (size, size // 2 + 1, size // 2 + 1) if nq > 1 else (size,)
    return pl.pallas_call(
        functools.partial(pack_kernel, nq, slots),
        name="pack",
        out_shape=tuple(jax.ShapeDtypeStruct((n, part, TILE), BF16) for n in sizes),
        in_specs=[SMEM] * 5 + [VMEM] * 17,
        out_specs=(VMEM,) * len(sizes),
        scratch_shapes=[pltpu.VMEM((D, 8), F32)],
        compiler_params=PARAMS,
        cost_estimate=pl.CostEstimate(flops=10**7, bytes_accessed=3 * 10**7, transcendentals=0),
    )(base, *scalars, table, *dmods, *grads)


def halves(v):
    high = v.astype(BF16)
    return high, (v - high.astype(F32)).astype(BF16)


def dot3(dot, a, b):
    return dot(a[0], b[0]) + (dot(a[0], b[1]) + dot(a[1], b[0]))


def soap_kernel(nq, g_ref, left, right, first, second, master, gs, fn, sn, wn):
    many = range(master.shape[0])
    place = [0]
    if nq > 1:
        turn = [lax.axis_index("seq") ^ q for q in range(nq)]
        place = [(r % 2) * 2 + r // 2 for r in turn]
    g = [jnp.concatenate([g_ref[place[q], i] for q in range(nq)], axis=0) for i in many]
    for i in many:
        gs[i] = g[i].astype(F32)
    lo = [halves(left[i]) for i in many]
    ro = [halves(right[i]) for i in many]
    rot = [halves(dot_tn(lo[i][0], g[i]) + dot_tn(lo[i][1], g[i])) for i in many]
    rot = [dot3(dot_nn, rot[i], ro[i]) for i in many]
    step = []
    for i in many:
        f = beta_first * first[i] + (1.0 - beta_first) * rot[i]
        s = beta_second * second[i] + (1.0 - beta_second) * rot[i] * rot[i]
        fn[i] = f
        sn[i] = s
        bias_f = 1.0 - beta_first**STEP
        bias_s = 1.0 - beta_second**STEP
        step.append((f / bias_f / (jnp.sqrt(s / bias_s) + adam_eps)).astype(BF16))
    back = [dot_nn(lo[i][0], step[i]).astype(BF16) for i in many]
    back = [dot_nt(back[i], ro[i][0]) for i in many]
    for i in many:
        w = master[i]
        mean = jnp.mean(jnp.mean(w * w, axis=1, keepdims=True), axis=0, keepdims=True)
        spread = jnp.sqrt(mean + 1e-06)
        wn[i] = w - base_rate * spread * (back[i] + decay_rate * w)


def soap(nq, g, left, right, first, second, master):
    slots = master.shape[0]
    block = max(k for k in range(1, 12) if slots % k == 0)
    part = TILE // nq
    spec = pl.BlockSpec((block, TILE, TILE), lambda i: (i, 0, 0))
    g_spec = pl.BlockSpec((nq, block, part, TILE), lambda i: (0, i, 0, 0))
    shape = jax.ShapeDtypeStruct(master.shape, F32)
    return pl.pallas_call(
        functools.partial(soap_kernel, nq),
        name="soap",
        grid=(slots // block,),
        out_shape=(shape,) * 4,
        in_specs=[g_spec] + [spec] * 5,
        out_specs=(spec,) * 4,
        compiler_params=PARAMS,
        cost_estimate=pl.CostEstimate(flops=10**9, bytes_accessed=10**7, transcendentals=10**6),
    )(g, left, right, first, second, master)


class Grid:
    def __init__(self, n_dp, n_seq):
        self.direct = n_dp == 8 and n_seq == 4
        self.n = {"z": n_dp // 2, "y": 2, "x": n_seq // 2, "c": 2}
        self.n_dp = n_dp
        self.n_seq = n_seq
        self.nq = n_seq if self.direct else 1

    def shift(self, v, names, step=1):
        pairs = []
        for dp in range(self.n_dp):
            for seq in range(self.n_seq):
                at = {"z": dp // 2, "y": dp % 2, "x": seq // 2, "c": seq % 2}
                to = {k: (a + (k in names) * step) % self.n[k] for k, a in at.items()}
                pairs.append(((dp, seq), (to["z"] * 2 + to["y"], to["x"] * 2 + to["c"])))
        if not set(names) & set("zy"):
            axis, flat = "seq", {(a[1], b[1]) for a, b in pairs}
        elif not set(names) & set("xc"):
            axis, flat = "dp", {(a[0], b[0]) for a, b in pairs}
        else:
            axis = ("dp", "seq")
            flat = {tuple(d * self.n_seq + q for d, q in pair) for pair in pairs}
        return lax.ppermute(v, axis, sorted(flat))

    def over_seq(self, v):
        if not self.direct:
            return lax.all_gather(v, "seq", axis=0, tiled=True)
        return jnp.concatenate([v] + [self.shift(v, n) for n in ("x", "c", "xc")], axis=0)

    def table(self, tile_slot, slots, sign):
        if not self.direct:
            return tile_slot
        dp = lax.axis_index("dp")
        owner = tile_slot // slots
        rz = (sign * (dp // 2 - owner // 2)) % self.n["z"]
        ry = (dp ^ owner) & 1
        return (rz * (8 if sign > 0 else 4) + ry) * slots + tile_slot % slots

    def gather_slots(self, low):
        if not self.direct:
            return [lax.all_gather(low, "dp", axis=0, tiled=True)]
        part = TILE // self.nq
        piece = lax.dynamic_slice_in_dim(low, lax.axis_index("seq") * part, part, 1)
        own = piece
        out = []
        for r in range(self.n["z"]):
            piece = own if r == 0 else self.shift(own, "z", r)
            near = [piece] + [self.shift(piece, n) for n in ("y", "x", "xy")]
            near = jnp.concatenate(near, axis=0)
            out += [near, self.shift(near, "c")]
        return out

    def reduce_slots(self, parts):
        if not self.direct:
            total = lax.psum_scatter(
                parts[0].astype(F32), "dp", scatter_dimension=0, tiled=True
            )
            return lax.psum(total, "seq")[None]
        k = parts[0].shape[0] // (4 * self.n["z"])
        other = [self.shift(parts[2], "c"), self.shift(parts[1], "c")]
        half = parts[0].shape[0] // 2

        def blocks(r):
            rows = [slice(k * i, k * (i + 1)) for i in range(4 * r, 4 * r + 4)]
            far = other[0 if r >= self.n["z"] // 2 else 1]
            down = half if r >= self.n["z"] // 2 else 0
            back = [far[at.start - down : at.stop - down] for at in rows]
            return [parts[0][at].astype(F32) + v.astype(F32) for at, v in zip(rows, back)]

        acc = None
        for r in range(self.n["z"] - 1, -1, -1):
            block = blocks(r)
            total = block[0]
            for v, names in zip(block[1:], ("y", "x", "xy")):
                total = total + self.shift(v.astype(BF16), names).astype(F32)
            if acc is not None:
                total = total + self.shift(acc, "z").astype(F32)
            acc = total.astype(BF16)
        return self.over_seq(acc[None])


def local(
    tokens_long,
    tokens_short,
    upstream_long,
    upstream_short,
    interval_table,
    labels_long,
    labels_short,
    lengths_long,
    lengths_short,
    tile_slot,
    master_slots,
    basis_left,
    basis_right,
    first_moment,
    second_moment,
):
    grid = Grid(lax.axis_size("dp"), lax.axis_size("seq"))
    slots = master_slots.shape[0]
    nq, direct = grid.nq, grid.direct
    srcs = grid.gather_slots(master_slots.astype(BF16))
    base_in = grid.table(tile_slot, slots, 1)
    base_out = grid.table(tile_slot, slots, -1)
    base_in, base_out, srcs[0] = lax.optimization_barrier((base_in, base_out, srcs[0]))
    *weights, mod_table, share = unpack(
        nq, slots, srcs, base_in, (labels_long, labels_short), interval_table
    )
    w_qkv, w_out, w_up, w_down = weights

    def short(i, prev):
        return short_call(
            i, (share, labels_short, lengths_short), tokens_short, upstream_short,
            mod_table, weights, prev,
        )

    q, kv_own = long_in((labels_long, lengths_long), tokens_long, mod_table, w_qkv)
    kv = grid.over_seq(kv_own)
    res0 = short(0, None)
    kv, dmod_s0 = lax.optimization_barrier((kv, res0[6]))
    (
        out_long, dx1, packed, stat, dw_out_l, dw_up_l, dw_down_l, dmod_mid,
    ) = long_mid(
        direct, (share, labels_long, lengths_long), tokens_long, upstream_long,
        mod_table, q, kv, w_out, w_up, w_down,
    )
    packed_all = grid.over_seq(packed)
    prev0, prev1, dmod_mid = lax.optimization_barrier((res0[0], res0[1], dmod_mid))
    res1 = short(1, (prev0, prev1))
    packed_all, dmod_s1 = lax.optimization_barrier((packed_all, res1[6]))
    grad_long, dw_qkv_l, dmod_back = long_back(
        direct, (labels_long, lengths_long), tokens_long, mod_table, kv_own, kv, packed,
        stat, packed_all, dx1, w_qkv,
    )
    out_short, grad_short = res1[:2]
    terms = []
    for i, extra in enumerate((dw_qkv_l, dw_out_l, dw_up_l, dw_down_l)):
        terms += [res0[2 + i], res1[2 + i], extra]
    size = grid.n_dp * slots * (2 if direct else 1)
    parts = pack(
        nq, slots, size, base_out, (labels_long, labels_short, lengths_long, lengths_short),
        interval_table, (dmod_mid, dmod_back, dmod_s0, dmod_s1), terms,
    )
    g = grid.reduce_slots(parts)
    grad_slots, first_new, second_new, weight_new = soap(
        nq, g, basis_left, basis_right, first_moment, second_moment, master_slots
    )
    return (
        out_long, out_short, grad_long, grad_short,
        grad_slots, first_new, second_new, weight_new,
    )


def solution(mesh):
    rows = P(("dp", "seq"), None, None)
    cols = P("dp", "seq", None)
    slots = P("dp", None, None)
    return jax.shard_map(
        local,
        mesh=mesh,
        in_specs=(cols, rows, cols, rows) + (P(),) * 6 + (slots,) * 5,
        out_specs=(cols, rows, cols, rows) + (slots,) * 4,
        check_vma=False,
    )
```
